32 devices in a mesh: dp: 8 (over z, x), fsdp: 4 (over y, core).
Axes of the slice: x: 2, y: 2, z: 4, core: 2. Of those that a mesh axis runs over, the one named last changes fastest.
Arguments:
- tokens: bfloat16 [2, 16, 1024, 768], P(None, 'dp', 'fsdp'), may hold values from -6 to 6
- cotangent: bfloat16 [2, 16, 1024, 768], P(None, 'dp', 'fsdp'), may hold values from -6 to 6
- lengths: int32 [2, 16], P(None, 'dp'), may hold values from 256 to 1024, as said below
- inward_weight: float32 [768, 2304], P('fsdp'), may hold values from -0.21875 to 0.21875
- outward_weight: float32 [768, 768], P('fsdp'), may hold values from -6 to 6
- expand_weight: float32 [768, 2304], P('fsdp'), may hold values from -0.21875 to 0.21875
- shrink_weight: float32 [1152, 768], P('fsdp'), may hold values from -0.1875 to 0.1875
- gain_weight: float32 [2, 768], P(None, 'fsdp'), may hold values from 0.5 to 1.5
- inward_first: float32 [768, 2304], P('fsdp'), may hold values from -2048 to 2048
- outward_first: float32 [768, 768], P('fsdp'), may hold values from -64 to 64
- expand_first: float32 [768, 2304], P('fsdp'), may hold values from -512 to 512
- shrink_first: float32 [1152, 768], P('fsdp'), may hold values from -512 to 512
- gain_first: float32 [2, 768], P(None, 'fsdp'), may hold values from -2048 to 2048
- inward_second: float32 [768, 2304], P('fsdp'), may hold values from 104857.6 to 419430.4
- outward_second: float32 [768, 768], P('fsdp'), may hold values from 131.072 to 524.288
- expand_second: float32 [768, 2304], P('fsdp'), may hold values from 6553.6 to 26214.4
- shrink_second: float32 [1152, 768], P('fsdp'), may hold values from 9502.72 to 38010.88
- gain_second: float32 [2, 768], P(None, 'fsdp'), may hold values from 104857.6 to 419430.4
Outputs:
- block_out: bfloat16 [2, 16, 1024, 768], P(None, 'dp', 'fsdp')
- input_grad: float32 [2, 16, 1024, 768], P(None, 'dp', 'fsdp')
- inward_renewed: float32 [768, 2304], P('fsdp')
- inward_momentum: float32 [768, 2304], P('fsdp')
- inward_variance: float32 [768, 2304], P('fsdp')
- outward_renewed: float32 [768, 768], P('fsdp')
- outward_momentum: float32 [768, 768], P('fsdp')
- outward_variance: float32 [768, 768], P('fsdp')
- expand_renewed: float32 [768, 2304], P('fsdp')
- expand_momentum: float32 [768, 2304], P('fsdp')
- expand_variance: float32 [768, 2304], P('fsdp')
- shrink_renewed: float32 [1152, 768], P('fsdp')
- shrink_momentum: float32 [1152, 768], P('fsdp')
- shrink_variance: float32 [1152, 768], P('fsdp')
- gain_renewed: float32 [2, 768], P(None, 'fsdp')
- gain_momentum: float32 [2, 768], P(None, 'fsdp')
- gain_variance: float32 [2, 768], P(None, 'fsdp')
The draws below stay inside these ranges and needn't reach their ends.
Inputs may be any that keep to these rules, and one draw needn't show every extreme that they name: `lengths`: in each micro-batch, among the 2 sequences of each dp index, one has length 1024.
All inputs are finite; a program needn't handle non-finite values.
Results may differ from the reference program's by a relative error of at most 0.014.
Values may be sent and summed in bfloat16 or wider, within the bound.
No kernel may reach another device: no remote copies, remote signals or barrier semaphores. Data moves between devices by JAX's collectives and lax.ppermute only.
A program may use at most 256 MiB of HBM per device.

```python
import math
import jax
import jax.numpy as jnp
from jax import lax

D = 768
FF = 1152
HEADS = 12
HDIM = 64
SEQLEN = 1024
SEQ_GRP = 2
MICRO = 2
STEP = 10
GROUPSEQ = 16
TOKENS = 32768


def draw_lengths(key, part):
    base_key, pick_key = jax.random.split(key)
    group_count = GROUPSEQ // SEQ_GRP
    base_lengths = jax.random.randint(base_key, (MICRO, group_count, SEQ_GRP), SEQLEN // 4, SEQLEN + 1)
    chosen = jax.random.randint(pick_key, (MICRO, group_count, 1), 0, SEQ_GRP)
    slot_index = jnp.arange(SEQ_GRP, dtype=jnp.int32)[None, None, :]
    filled = jnp.where(slot_index == chosen, SEQLEN, base_lengths)
    return filled.astype(jnp.int32).reshape(MICRO, GROUPSEQ)


def levels(stream_key, dims, pieces, least, top_value):
    level, own = 1.0, jax.random.fold_in(stream_key, 6)
    for position, shards_of in pieces:
        heights = jnp.exp(jax.random.uniform(jax.random.fold_in(own, position), (shards_of,), jnp.float32, least / len(pieces), top_value / len(pieces)))
        level = level * jnp.repeat(heights, dims[position] // shards_of).reshape([-1 if axis == position else 1 for axis in range(len(dims))])
    return level


def centred(key, shape, deviation, bound, cuts=(), kind=jnp.bfloat16):
    drawn = deviation * jax.random.normal(key, shape, jnp.float32)
    if cuts:
        drawn = drawn * levels(key, shape, cuts, -0.22, 0.18)
    return jnp.clip(drawn, -bound, bound).astype(kind)


def setup_inputs(seed: int = 0) -> dict:
    seeds = jax.random.split(jax.random.key(seed), 19)
    tokens = centred(seeds[0], (MICRO, GROUPSEQ, SEQLEN, D), 1.0, 6.0, ((1, 8), (2, 4)))
    cotangent = centred(seeds[1], (MICRO, GROUPSEQ, SEQLEN, D), 1.0, 6.0, ((1, 8), (2, 4)))
    lengths = draw_lengths(jax.random.fold_in(seeds[18], 71), 0)
    inward_weight = centred(seeds[3], (D, 3 * D), D ** -0.5, 0.21875, ((0, 4),), jnp.float32)
    outward_weight = centred(seeds[4], (D, D), (max(1, D // (SEQLEN // 2))) ** -0.5, 6.0, ((0, 4),), jnp.float32)
    expand_weight = centred(seeds[5], (D, 2 * FF), D ** -0.5, 0.21875, ((0, 4),), jnp.float32)
    shrink_weight = centred(seeds[6], (FF, D), FF ** -0.5, 0.1875, ((0, 4),), jnp.float32)
    gain_weight = jnp.clip(1.0 + 0.1 * jax.random.normal(seeds[7], (2, D), jnp.float32), 0.5, 1.5)
    inward_first = centred(seeds[8], (D, 3 * D), (1.8 * TOKENS ** 0.5), 2048.0, ((0, 4),), jnp.float32)
    outward_first = centred(seeds[9], (D, D), (0.063 * TOKENS ** 0.5), 64.0, ((0, 4),), jnp.float32)
    expand_first = centred(seeds[10], (D, 2 * FF), (0.45 * TOKENS ** 0.5), 512.0, ((0, 4),), jnp.float32)
    shrink_first = centred(seeds[11], (FF, D), (0.54 * TOKENS ** 0.5), 512.0, ((0, 4),), jnp.float32)
    gain_first = centred(seeds[12], (2, D), (1.8 * TOKENS ** 0.5), 2048.0, ((1, 4),), jnp.float32)
    inward_second = jnp.clip(jnp.exp(math.log(419430.4) - 1.3862944 * jax.random.uniform(seeds[13], (D, 3 * D), jnp.float32) ** levels(seeds[13], (D, 3 * D), ((0, 4),), -0.2, 0.2)), 104857.6, 419430.4)
    outward_second = jnp.clip(jnp.exp(math.log(524.288) - 1.3862944 * jax.random.uniform(seeds[14], (D, D), jnp.float32) ** levels(seeds[14], (D, D), ((0, 4),), -0.2, 0.2)), 131.072, 524.288)
    expand_second = jnp.clip(jnp.exp(math.log(26214.4) - 1.3862944 * jax.random.uniform(seeds[15], (D, 2 * FF), jnp.float32) ** levels(seeds[15], (D, 2 * FF), ((0, 4),), -0.2, 0.2)), 6553.6, 26214.4)
    shrink_second = jnp.clip(jnp.exp(math.log(38010.88) - 1.3862944 * jax.random.uniform(seeds[16], (FF, D), jnp.float32) ** levels(seeds[16], (FF, D), ((0, 4),), -0.2, 0.2)), 9502.72, 38010.88)
    gain_second = jnp.clip(jnp.exp(math.log(419430.4) - 1.3862944 * jax.random.uniform(seeds[17], (2, D), jnp.float32) ** levels(seeds[17], (2, D), ((1, 4),), -0.2, 0.2)), 104857.6, 419430.4)
    return {"tokens": tokens, "cotangent": cotangent, "lengths": lengths, "inward_weight": inward_weight, "outward_weight": outward_weight, "expand_weight": expand_weight, "shrink_weight": shrink_weight, "gain_weight": gain_weight, "inward_first": inward_first, "outward_first": outward_first, "expand_first": expand_first, "shrink_first": shrink_first, "gain_first": gain_first, "inward_second": inward_second, "outward_second": outward_second, "expand_second": expand_second, "shrink_second": shrink_second, "gain_second": gain_second}


@jax.custom_vjp
def low(v):
    return lax.optimization_barrier(v.astype(jnp.bfloat16)).astype(jnp.float32)

@jax.custom_vjp
def reduced_backward(v):
    return v

def low_keep(v):
    return (low(v), None)

def low_pass(kept, grad):
    return (grad,)

def back_keep(v):
    return (v, None)

def back_low(kept, grad):
    return (low(grad),)
low.defvjp(low_keep, low_pass)
reduced_backward.defvjp(back_keep, back_low)
highest_precision = lax.Precision.HIGHEST
rope_base = 160000.0
norm_eps = 1e-05
adam_beta = 0.5
adam_eps = 1e-08
weight_decay = 0.01
rates = (0.07, 2.0, 0.07, 0.06, 0.2)
masked_score = -1e+30

def tables(positions):
    half_dim = HDIM // 2
    exponent = jnp.arange(half_dim, dtype=jnp.float32) * (2.0 / HDIM)
    inverse = jnp.power(jnp.float32(rope_base), -exponent)
    angles = positions.astype(jnp.float32)[:, None] * inverse[None, :]
    return (jnp.cos(angles), jnp.sin(angles))

def rotate(values, cosine, sine_table):
    half_dim = values.shape[-1] // 2
    former = values[..., :half_dim]
    latter = values[..., half_dim:]
    cos_wide = cosine[:, None, :]
    sin_wide = sine_table[:, None, :]
    return jnp.concatenate([former * cos_wide - latter * sin_wide, latter * cos_wide + former * sin_wide], axis=-1)

def normalize(values, gain_row):
    center = values - lax.optimization_barrier(jnp.mean(values, axis=-1, keepdims=True))
    spread = lax.optimization_barrier(jnp.mean(center * center, axis=-1, keepdims=True))
    return center * lax.rsqrt(spread + norm_eps) * gain_row

def geglu(joined_heads):
    gate_part = joined_heads[..., :FF]
    upward = joined_heads[..., FF:]
    return 0.5 * gate_part * (1.0 + lax.erf(gate_part * 0.7071067811865476)) * upward

def group_forward(input_tokens, limits, inward_matrix, outward_matrix, expand_matrix, shrink_matrix, gain_rows):
    group_size = input_tokens.shape[0]
    positions = jnp.arange(SEQLEN, dtype=jnp.int32)
    cosine, sine_table = tables(positions)
    live_keys = positions[None, :] < limits[:, None]
    hidden_first_norm = low(normalize(input_tokens, gain_rows[0]))
    joined_heads = reduced_backward(jnp.einsum('rnu,uo->rno', hidden_first_norm, inward_matrix, precision=highest_precision))
    joined_heads = joined_heads.reshape(group_size, SEQLEN, 3, HEADS, HDIM)
    queries = low(rotate(joined_heads[:, :, 0], cosine, sine_table))
    keys_rot = low(rotate(joined_heads[:, :, 1], cosine, sine_table))
    values = low(joined_heads[:, :, 2])
    score_scale = HDIM ** (-0.5)
    scores = reduced_backward(score_scale * jnp.einsum('sqhd,skhd->shqk', queries, keys_rot, precision=highest_precision))
    scores = jnp.where(live_keys[:, None, None, :], scores, masked_score)
    row_peak = lax.optimization_barrier(jnp.max(scores, axis=-1, keepdims=True))
    exp_terms = jnp.exp(scores - row_peak)
    attention = low(exp_terms / lax.optimization_barrier(jnp.sum(exp_terms, axis=-1, keepdims=True)))
    mixed_tokens = low(reduced_backward(jnp.einsum('shqk,skhd->sqhd', attention, values, precision=highest_precision)))
    mixed_tokens = mixed_tokens.reshape(group_size, SEQLEN, D)
    middle_state = input_tokens + reduced_backward(jnp.einsum('rnu,uo->rno', mixed_tokens, outward_matrix, precision=highest_precision))
    hidden_second_norm = low(normalize(middle_state, gain_rows[1]))
    expanded_rows = reduced_backward(jnp.einsum('rnu,uo->rno', hidden_second_norm, expand_matrix, precision=highest_precision))
    hidden_state = low(geglu(expanded_rows))
    layer_result = middle_state + reduced_backward(jnp.einsum('wmq,qn->wmn', hidden_state, shrink_matrix, precision=highest_precision))
    return layer_result * live_keys[:, :, None].astype(layer_result.dtype)

def adam_update(master, gradient, moment_one, moment_two, step_rate, decay_rate):
    first_new = adam_beta * moment_one + (1.0 - adam_beta) * gradient
    second_new = adam_beta * moment_two + (1.0 - adam_beta) * gradient * gradient
    correction = 1.0 - adam_beta ** STEP
    direction = first_new / correction / (jnp.sqrt(second_new / correction) + adam_eps)
    renewed = master - step_rate * (direction + decay_rate * master)
    return (renewed, first_new, second_new)

def reference(tokens, cotangent, lengths, inward_weight, outward_weight, expand_weight, shrink_weight, gain_weight, inward_first, outward_first, expand_first, shrink_first, gain_first, inward_second, outward_second, expand_second, shrink_second, gain_second):
    group_count = MICRO * GROUPSEQ // SEQ_GRP
    stacked = tokens.astype(jnp.float32).reshape(group_count, SEQ_GRP, SEQLEN, D)
    limits = lengths.reshape(group_count, SEQ_GRP)

    def forward(input_tokens, inward_matrix, outward_matrix, expand_matrix, shrink_matrix, gain_rows):
        inward_low = low(inward_matrix)
        outward_low = low(outward_matrix)
        expand_low = low(expand_matrix)
        shrink_low = low(shrink_matrix)
        gain_low = low(gain_rows)
        checked = jax.checkpoint(group_forward)

        def advance(carry, item):
            return (carry, checked(item[0], item[1], inward_low, outward_low, expand_low, shrink_low, gain_low))
        unused, outputs = lax.scan(advance, None, (input_tokens, limits))
        return outputs
    outputs, pullback = jax.vjp(forward, stacked, inward_weight, outward_weight, expand_weight, shrink_weight, gain_weight)
    grads = pullback(cotangent.astype(jnp.float32).reshape(outputs.shape))
    block_out = outputs.reshape(tokens.shape).astype(jnp.bfloat16)
    input_grad = grads[0].reshape(tokens.shape)
    inward_new = adam_update(inward_weight, grads[1], inward_first, inward_second, rates[0], weight_decay)
    outward_new = adam_update(outward_weight, grads[2], outward_first, outward_second, rates[1], weight_decay)
    expand_new = adam_update(expand_weight, grads[3], expand_first, expand_second, rates[2], weight_decay)
    shrink_new = adam_update(shrink_weight, grads[4], shrink_first, shrink_second, rates[3], weight_decay)
    gain_new = adam_update(gain_weight, grads[5], gain_first, gain_second, rates[4], 0.0)
    return (block_out, input_grad, inward_new[0], inward_new[1], inward_new[2], outward_new[0], outward_new[1], outward_new[2], expand_new[0], expand_new[1], expand_new[2], shrink_new[0], shrink_new[1], shrink_new[2], gain_new[0], gain_new[1], gain_new[2])
```

```python
import functools

import jax
import jax.numpy as jnp
from jax import lax
from jax.experimental import pallas as pl
from jax.experimental.pallas import tpu as pltpu
from jax.sharding import PartitionSpec as P

FF = 1152
HEADS = 12
HDIM = 64
STEP = 10

rope_base = 160000.0
norm_eps = 1e-05
adam_beta = 0.5
adam_eps = 1e-08
weight_decay = 0.01
rates = (0.07, 2.0, 0.07, 0.06, 0.2)
masked_score = -1e30

BF = jnp.bfloat16
F32 = jnp.float32
NN = (((1,), (0,)), ((), ()))
NT = (((1,), (1,)), ((), ()))
TN = (((0,), (0,)), ((), ()))
VMEM_BYTES = 58 << 20
LANES = 128
PAIRS = HEADS * HDIM // LANES


def dot(left, right, dims=NN):
    return lax.dot_general(left, right, dims, preferred_element_type=F32)


def swap_halves(values):
    lane = lax.broadcasted_iota(jnp.int32, (1, LANES), 1)
    former = lax.rem(lane, HDIM) < HDIM // 2
    ahead = pltpu.roll(values, LANES - HDIM // 2, 1)
    behind = pltpu.roll(values, HDIM // 2, 1)
    return jnp.where(former, ahead, behind)


def centre_scale(values):
    center = values - jnp.mean(values, axis=-1, keepdims=True)
    spread = jnp.mean(center * center, axis=-1, keepdims=True)
    inverse = lax.rsqrt(spread + norm_eps)
    return center * inverse, inverse


def norm_back(grad, normed, inverse, gain):
    scaled = grad * gain
    mean_one = jnp.mean(scaled, axis=-1, keepdims=True)
    mean_two = jnp.mean(scaled * normed, axis=-1, keepdims=True)
    return inverse * (scaled - mean_one - normed * mean_two)


def place(scratch, pieces, me, rows):
    for r, piece in enumerate(pieces):
        owner = me ^ r
        scratch[pl.ds(pl.multiple_of(owner * rows, 32), rows), :] = piece[...]


def qkv_kernel(info, x_ref, gain_ref, cos_ref, sin_ref, w0, w1, w2, w3, h_ref, ht_ref, qkv_ref, w_ref):
    @pl.when(pl.program_id(0) == 0)
    def _():
        place(w_ref, (w0, w1, w2, w3), info[0], w0.shape[0])

    normed, unused = centre_scale(x_ref[...].astype(F32))
    hidden = normed * gain_ref[0:1, :]
    low = hidden.astype(BF)
    h_ref[...] = low
    ht_ref[...] = low.astype(F32).T.astype(BF)
    cosine = cos_ref[...]
    sine = sin_ref[...]
    width = low.shape[1]
    for part in range(3):
        joined = dot(low, w_ref[:, part * width : (part + 1) * width])
        if part == 2:
            qkv_ref[:, part * width : (part + 1) * width] = joined.astype(BF)
            continue
        for pair in range(PAIRS):
            block = joined[:, pair * LANES : (pair + 1) * LANES]
            turned = block * cosine + swap_halves(block) * sine
            turned = turned.astype(BF)
            if part == 0:
                turned = turned * jnp.asarray(HDIM**-0.5, BF)
            start = part * width + pair * LANES
            qkv_ref[:, start : start + LANES] = turned


def qkv_call(info, x, gain, cosine, sine, pieces, tile=256):
    rows, width = x.shape
    wide = pieces[0].shape[1]
    total = 4 * pieces[0].shape[0]
    whole = lambda i, s: (0, 0)
    by_row = lambda i, s: (i, 0)
    return pl.pallas_call(
        qkv_kernel,
        grid_spec=pltpu.PrefetchScalarGridSpec(
            num_scalar_prefetch=1,
            grid=(rows // tile,),
            in_specs=[
                pl.BlockSpec((tile, width), by_row),
                pl.BlockSpec((2, width), whole),
                pl.BlockSpec((tile, LANES), by_row),
                pl.BlockSpec((tile, LANES), by_row),
            ]
            + [pl.BlockSpec(pieces[0].shape, whole)] * 4,
            out_specs=[
                pl.BlockSpec((tile, width), by_row),
                pl.BlockSpec((width, tile), lambda i, s: (0, i)),
                pl.BlockSpec((tile, wide), by_row),
                pl.BlockSpec((total, wide), whole),
            ],
        ),
        out_shape=[
            jax.ShapeDtypeStruct((rows, width), BF),
            jax.ShapeDtypeStruct((width, rows), BF),
            jax.ShapeDtypeStruct((rows, wide), BF),
            jax.ShapeDtypeStruct((total, wide), BF),
        ],
        compiler_params=pltpu.CompilerParams(vmem_limit_bytes=VMEM_BYTES),
        name="qkv",
    )(info, x, gain, cosine, sine, *pieces)


def attend_kernel(info, q_ref, k_ref, v_ref, o_ref, r_ref, p_ref, *, tile):
    rows = q_ref.shape[0]
    key_at = lax.broadcasted_iota(jnp.int32, (1, rows), 1)
    bias = jnp.where(key_at < info[1], 0.0, masked_score).astype(F32)
    keys = k_ref[...]
    values = v_ref[...]
    low = lax.broadcasted_iota(jnp.int32, (1, LANES), 1) < HDIM
    one = jnp.ones((), BF)
    zero = jnp.zeros((), BF)
    sides = (jnp.where(low, values, one), jnp.where(low, one, values))
    for step in range(rows // tile):
        at = pl.ds(step * tile, tile)
        queries = q_ref[at, :]
        heads = (jnp.where(low, queries, zero), jnp.where(low, zero, queries))
        outs = []
        for head in range(2):
            scores = dot(heads[head], keys, NT) + bias
            peak = jnp.max(scores, axis=-1, keepdims=True)
            terms = jnp.exp(scores - peak).astype(BF)
            p_ref[head, at, :] = terms
            outs.append(dot(terms, sides[head]))
        mixed = jnp.where(low, outs[0], outs[1])
        total = pltpu.roll(jnp.where(low, outs[1], outs[0]), HDIM, 1)
        inverse = 1.0 / total
        o_ref[at, :] = (mixed * inverse).astype(BF)
        r_ref[at, :] = inverse


def attend_call(info, qkv, tile=512):
    rows = qkv.shape[0]
    width = qkv.shape[1] // 3
    block = (rows, LANES)
    return pl.pallas_call(
        functools.partial(attend_kernel, tile=tile),
        grid_spec=pltpu.PrefetchScalarGridSpec(
            num_scalar_prefetch=1,
            grid=(PAIRS,),
            in_specs=[
                pl.BlockSpec(block, lambda p, s: (0, p)),
                pl.BlockSpec(block, lambda p, s: (0, PAIRS + p)),
                pl.BlockSpec(block, lambda p, s: (0, 2 * PAIRS + p)),
            ],
            out_specs=[
                pl.BlockSpec(block, lambda p, s: (0, p)),
                pl.BlockSpec(block, lambda p, s: (0, p)),
                pl.BlockSpec((2, rows, rows), lambda p, s: (p, 0, 0)),
            ],
        ),
        out_shape=[
            jax.ShapeDtypeStruct((rows, width), BF),
            jax.ShapeDtypeStruct((rows, width), F32),
            jax.ShapeDtypeStruct((HEADS, rows, rows), BF),
        ],
        compiler_params=pltpu.CompilerParams(vmem_limit_bytes=VMEM_BYTES),
        name="attend",
    )(info, qkv, qkv, qkv)


def split_rows(source, me, rows, keep, send):
    for r in range(4):
        owner = me ^ r
        value = source[pl.ds(pl.multiple_of(owner * rows, 32), rows), :].astype(BF)
        target = send if r % 2 else keep
        target[r // 2] = value


def feed_kernel(
    info, x_ref, o_ref, r_ref, cot_ref, gain_ref, a0, a1, a2, a3, d0, d1, d2, d3,
    out_ref, dmid_ref, do_ref, gg_ref, ga_keep, ga_send, gd_keep, gd_send,
    wa, wd, acc_o, acc_i, acc_d, *, tile,
):
    step = pl.program_id(0)
    me = info[0]
    width = x_ref.shape[1]

    @pl.when(step == 0)
    def _():
        place(wa, (a0, a1, a2, a3), me, a0.shape[0])
        place(wd, (d0, d1, d2, d3), me, d0.shape[0])
        acc_o[...] = jnp.zeros_like(acc_o)
        acc_i[...] = jnp.zeros_like(acc_i)
        acc_d[...] = jnp.zeros_like(acc_d)
        gg_ref[...] = jnp.zeros_like(gg_ref)

    gain = gain_ref[1:2, :]
    mixed = o_ref[...]
    middle = x_ref[...].astype(F32) + dot(mixed, wa[:, :width])
    normed, inverse = centre_scale(middle)
    hidden = (normed * gain).astype(BF)
    gate = dot(hidden, wa[:, width : width + FF])
    upward = dot(hidden, wa[:, width + FF :])
    cdf = 0.5 * (1.0 + lax.erf(gate * 0.7071067811865476))
    gelu = gate * cdf
    slope = cdf + gate * (jnp.exp(-0.5 * gate * gate) * 0.3989422804014327)
    state = (gelu * upward).astype(BF)
    row_at = step * tile + lax.broadcasted_iota(jnp.int32, (tile, 1), 0)
    live = row_at < info[1]
    out_ref[...] = jnp.where(live, middle + dot(state, wd[...]), 0.0).astype(BF)
    branch = jnp.where(live, cot_ref[...].astype(F32), 0.0)
    branch_low = branch.astype(BF)
    acc_d[...] += dot(state, branch_low, TN)
    state_grad = dot(branch_low, wd[...], NT)
    gate_grad = (state_grad * upward * slope).astype(BF)
    up_grad = (state_grad * gelu).astype(BF)
    acc_i[:, :FF] += dot(hidden, gate_grad, TN)
    acc_i[:, FF:] += dot(hidden, up_grad, TN)
    hidden_grad = dot(gate_grad, wa[:, width : width + FF], NT) + dot(up_grad, wa[:, width + FF :], NT)
    gg_ref[...] += jnp.sum(hidden_grad * normed, axis=0, keepdims=True)
    middle_grad = branch + norm_back(hidden_grad, normed, inverse, gain)
    dmid_ref[...] = middle_grad
    mixer = middle_grad.astype(BF)
    acc_o[...] += dot(mixed, mixer, TN)
    do_ref[...] = (dot(mixer, wa[:, :width], NT) * r_ref[...]).astype(BF)

    @pl.when(step == pl.num_programs(0) - 1)
    def _():
        rows = a0.shape[0]
        for r in range(4):
            at = pl.ds(pl.multiple_of((me ^ r) * rows, 32), rows)
            target = ga_send if r % 2 else ga_keep
            target[r // 2, :, :width] = acc_o[at, :].astype(BF)
            target[r // 2, :, width:] = acc_i[at, :].astype(BF)
        split_rows(acc_d, me, d0.shape[0], gd_keep, gd_send)


def feed_call(info, x, mixed, inverse, cot, gain, a_pieces, d_pieces, tile=256):
    rows, width = x.shape
    ra, ca = a_pieces[0].shape
    rd, cd = d_pieces[0].shape
    whole = lambda i, s: (0, 0)
    cube = lambda i, s: (0, 0, 0)
    by_row = lambda i, s: (i, 0)
    block = pl.BlockSpec((tile, width), by_row)
    return pl.pallas_call(
        functools.partial(feed_kernel, tile=tile),
        grid_spec=pltpu.PrefetchScalarGridSpec(
            num_scalar_prefetch=1,
            grid=(rows // tile,),
            in_specs=[block, block, block, block, pl.BlockSpec((2, width), whole)]
            + [pl.BlockSpec((ra, ca), whole)] * 4
            + [pl.BlockSpec((rd, cd), whole)] * 4,
            out_specs=[block, block, block, pl.BlockSpec((1, width), whole)]
            + [pl.BlockSpec((2, ra, ca), cube)] * 2
            + [pl.BlockSpec((2, rd, cd), cube)] * 2,
            scratch_shapes=[
                pltpu.VMEM((4 * ra, ca), BF),
                pltpu.VMEM((4 * rd, cd), BF),
                pltpu.VMEM((width, width), F32),
                pltpu.VMEM((width, 2 * FF), F32),
                pltpu.VMEM((FF, width), F32),
            ],
        ),
        out_shape=[
            jax.ShapeDtypeStruct((rows, width), BF),
            jax.ShapeDtypeStruct((rows, width), F32),
            jax.ShapeDtypeStruct((rows, width), BF),
            jax.ShapeDtypeStruct((1, width), F32),
        ]
        + [jax.ShapeDtypeStruct((2, ra, ca), BF)] * 2
        + [jax.ShapeDtypeStruct((2, rd, cd), BF)] * 2,
        compiler_params=pltpu.CompilerParams(vmem_limit_bytes=VMEM_BYTES),
        name="feed",
    )(info, x, mixed, inverse, cot, gain, *a_pieces, *d_pieces)


def back_kernel(
    info, q_ref, k_ref, v_ref, o_ref, do_ref, p_ref, cos_ref, sin_ref, ht_ref, wq_ref, wk_ref, wv_ref, *rest,
    tile, first, last,
):
    rest = list(rest)
    if not first:
        carry_ref = rest.pop(0)
    if last:
        x_ref, dmid_ref, gain_ref = rest[:3]
        rest = rest[3:]
    keep_ref, send_ref = rest[:2]
    rest = rest[2:]
    if last:
        dx_ref, gg_ref, acc = rest
    else:
        (acc,) = rest
    step = pl.program_id(0)

    @pl.when(step == 0)
    def _():
        if first:
            acc[...] = jnp.zeros_like(acc)
        else:
            acc[...] = carry_ref[...]

    rows = q_ref.shape[0]
    low = lax.broadcasted_iota(jnp.int32, (1, LANES), 1) < HDIM
    zero = jnp.zeros((), BF)
    keys = k_ref[...]
    values = v_ref[...]
    key_heads = (jnp.where(low, keys, zero), jnp.where(low, zero, keys))
    key_grads = [None, None]
    value_grads = [None, None]
    query_grads = []
    for part in range(rows // tile):
        at = pl.ds(part * tile, tile)
        queries = q_ref[at, :]
        grads = do_ref[at, :]
        wide = grads.astype(F32)
        inner = wide * o_ref[at, :].astype(F32)
        grad_heads = (jnp.where(low, grads, zero), jnp.where(low, zero, grads))
        queries_t = queries.astype(F32).T.astype(BF)
        grads_t = wide.T.astype(BF)
        query_grad = None
        for head in range(2):
            mine = low if head == 0 else jnp.logical_not(low)
            lanes = slice(head * HDIM, (head + 1) * HDIM)
            row_inner = jnp.sum(jnp.where(mine, inner, 0.0), axis=-1, keepdims=True)
            term_grad = dot(grad_heads[head], values, NT)
            terms = p_ref[head, at, :]
            score_grad = (terms.astype(F32) * (term_grad - row_inner)).astype(BF)
            partial = dot(score_grad, key_heads[head])
            query_grad = partial if query_grad is None else query_grad + partial
            for grad_list, left, right in (
                (key_grads, queries_t, score_grad),
                (value_grads, grads_t, terms),
            ):
                value = dot(left[lanes], right)
                grad_list[head] = value if grad_list[head] is None else grad_list[head] + value
        query_grads.append(query_grad)
    cosine = cos_ref[...]
    sine = sin_ref[...]
    query_grad = jnp.concatenate(query_grads, axis=0) * (HDIM**-0.5)
    key_grad = jnp.concatenate(key_grads, axis=0).T
    value_grad = jnp.concatenate(value_grads, axis=0).T
    joined = jnp.concatenate(
        [
            (query_grad * cosine - swap_halves(query_grad) * sine).astype(BF),
            (key_grad * cosine - swap_halves(key_grad) * sine).astype(BF),
            value_grad.astype(BF),
        ],
        axis=1,
    )
    weight = jnp.concatenate([wq_ref[...], wk_ref[...], wv_ref[...]], axis=1)
    acc[...] += dot(joined, weight, NT)
    weight_grad = dot(ht_ref[...], joined).astype(BF)
    share = keep_ref.shape[1]
    me = info[0]
    for owner in range(4):
        rel = me ^ owner
        value = weight_grad[owner * share : (owner + 1) * share, :]
        for target, odd in ((keep_ref, 0), (send_ref, 1)):

            @pl.when(rel % 2 == odd)
            def _():
                target[rel // 2] = value

    if last:

        @pl.when(step == pl.num_programs(0) - 1)
        def _():
            normed, inverse = centre_scale(x_ref[...].astype(F32))
            hidden_grad = acc[...]
            gg_ref[...] = jnp.sum(hidden_grad * normed, axis=0, keepdims=True)
            back = norm_back(hidden_grad, normed, inverse, gain_ref[0:1, :])
            dx_ref[...] = (dmid_ref[...] + back).astype(BF)


def back_call(info, qkv, mixed, grads, terms, cosine, sine, hidden_t, weight, start, count, carry, tail, tile=512):
    rows, width = mixed.shape
    last = tail is not None
    first = carry is None
    block = (rows, LANES)
    whole = lambda p, s: (0, 0)

    def column(offset):
        return lambda p, s: (0, offset + start + p)

    in_specs = [
        pl.BlockSpec(block, column(0)),
        pl.BlockSpec(block, column(PAIRS)),
        pl.BlockSpec(block, column(2 * PAIRS)),
        pl.BlockSpec(block, column(0)),
        pl.BlockSpec(block, column(0)),
        pl.BlockSpec((2, rows, rows), lambda p, s: (start + p, 0, 0)),
        pl.BlockSpec(block, whole),
        pl.BlockSpec(block, whole),
        pl.BlockSpec((width, rows), whole),
        pl.BlockSpec((width, LANES), column(0)),
        pl.BlockSpec((width, LANES), column(PAIRS)),
        pl.BlockSpec((width, LANES), column(2 * PAIRS)),
    ]
    operands = [qkv, qkv, qkv, mixed, grads, terms, cosine, sine, hidden_t, weight, weight, weight]
    if not first:
        in_specs.append(pl.BlockSpec((rows, width), whole))
        operands.append(carry)
    if last:
        in_specs += [
            pl.BlockSpec((rows, width), whole),
            pl.BlockSpec((rows, width), whole),
            pl.BlockSpec((2, width), whole),
        ]
        operands += list(tail)
    share = width // 4
    piece = (2, share, 3 * LANES)
    out_specs = [pl.BlockSpec(piece, lambda p, s: (0, 0, p))] * 2
    out_shape = [jax.ShapeDtypeStruct((2, share, 3 * LANES * count), BF)] * 2
    scratch = []
    if last:
        out_specs += [pl.BlockSpec((rows, width), whole), pl.BlockSpec((1, width), whole)]
        out_shape += [jax.ShapeDtypeStruct((rows, width), BF), jax.ShapeDtypeStruct((1, width), F32)]
        scratch = [pltpu.VMEM((rows, width), F32)]
    else:
        out_specs.append(pl.BlockSpec((rows, width), whole))
        out_shape.append(jax.ShapeDtypeStruct((rows, width), F32))
    return pl.pallas_call(
        functools.partial(back_kernel, tile=tile, first=first, last=last),
        grid_spec=pltpu.PrefetchScalarGridSpec(
            num_scalar_prefetch=1,
            grid=(count,),
            in_specs=in_specs,
            out_specs=out_specs,
            scratch_shapes=scratch,
        ),
        out_shape=out_shape,
        compiler_params=pltpu.CompilerParams(vmem_limit_bytes=VMEM_BYTES),
        name="back",
    )(info, *operands)


def adam_update(master, gradient, moment_one, moment_two, step_rate, decay_rate):
    first_new = adam_beta * moment_one + (1.0 - adam_beta) * gradient
    second_new = adam_beta * moment_two + (1.0 - adam_beta) * gradient * gradient
    correction = 1.0 - adam_beta**STEP
    direction = first_new / correction / (jnp.sqrt(second_new / correction) + adam_eps)
    renewed = master - step_rate * (direction + decay_rate * master)
    return (renewed, first_new, second_new)


def tables(seq_total):
    half_dim = HDIM // 2
    exponent = jnp.arange(half_dim, dtype=jnp.float32) * (2.0 / HDIM)
    inverse = jnp.power(jnp.float32(rope_base), -exponent)
    angles = jnp.arange(seq_total, dtype=jnp.float32)[:, None] * inverse[None, :]
    cosine = jnp.cos(angles)
    sine = jnp.sin(angles)
    return jnp.tile(cosine, (1, 4)), jnp.concatenate([-sine, sine, -sine, sine], axis=1)


CORE = [(0, 1), (1, 0), (2, 3), (3, 2)]
CROSS = [(0, 2), (1, 3), (2, 0), (3, 1)]


def gather_pieces(shard):
    near = lax.ppermute(shard, "fsdp", CORE)
    far = lax.ppermute(shard, "fsdp", CROSS)
    return shard, near, far, lax.ppermute(far, "fsdp", CORE)


def add_low(left, right):
    return (left.astype(F32) + right.astype(F32)).astype(BF)


def reduce_pieces(keep, send):
    total = add_low(keep, lax.ppermute(send, "fsdp", CORE))
    return add_low(total[0], lax.ppermute(total[1], "fsdp", CROSS))


def local(
    tokens, cotangent, lengths,
    inward_weight, outward_weight, expand_weight, shrink_weight, gain_weight,
    inward_first, outward_first, expand_first, shrink_first, gain_first,
    inward_second, outward_second, expand_second, shrink_second, gain_second,
):
    micro_count, group_size, local_len, width = tokens.shape
    fsdp = lax.axis_size("fsdp")
    assert fsdp == 4 and micro_count * group_size == fsdp
    seq_total = local_len * fsdp
    me = lax.axis_index("fsdp")
    info = jnp.stack([me.astype(jnp.int32), lengths.reshape(fsdp)[me]])

    def to_sequence(array):
        array = array.reshape(fsdp, local_len, width)
        return lax.all_to_all(array, "fsdp", 0, 0).reshape(seq_total, width)

    def to_positions(array):
        array = array.reshape(fsdp, local_len, width)
        return lax.all_to_all(array, "fsdp", 0, 0).reshape(micro_count, group_size, local_len, width)

    inward_pieces = gather_pieces(inward_weight.astype(BF))
    x = to_sequence(tokens)
    gain = lax.all_gather(gain_weight.astype(BF), "fsdp", axis=1, tiled=True).astype(F32)
    a_pieces = gather_pieces(jnp.concatenate([outward_weight.astype(BF), expand_weight.astype(BF)], axis=1))
    d_pieces = gather_pieces(shrink_weight.astype(BF))
    cot = to_sequence(cotangent)
    cosine, sine = tables(seq_total)

    hidden, hidden_t, qkv, weight = qkv_call(info, x, gain, cosine, sine, inward_pieces)
    mixed, inverse, terms = attend_call(info, qkv)
    out, middle_grad, grads, gain_two, ga_keep, ga_send, gd_keep, gd_send = feed_call(
        info, x, mixed, inverse, cot, gain, a_pieces, d_pieces
    )
    block_out = to_positions(out)
    grad_a = reduce_pieces(ga_keep, ga_send)
    grad_d = reduce_pieces(gd_keep, gd_send)
    grad_a, grad_d = lax.psum((grad_a, grad_d), "dp")

    carry = None
    chunks = []
    calls = 3
    for call in range(calls):
        tail = (x, middle_grad, gain) if call == calls - 1 else None
        count = PAIRS // calls
        outs = back_call(
            info, qkv, mixed, grads, terms, cosine, sine, hidden_t, weight, call * count, count, carry, tail
        )
        keep, send, carry = outs[:3]
        chunks.append(reduce_pieces(keep, send))
    input_low, gain_one = outs[2:]
    input_grad = to_positions(input_low).astype(F32)
    grad_w = lax.psum(tuple(chunks), "dp")
    share = inward_weight.shape[0]
    grad_w = jnp.concatenate(grad_w, axis=1).astype(F32)
    grad_w = grad_w.reshape(share, PAIRS, 3, LANES).transpose(0, 2, 1, 3).reshape(share, 3 * width)
    gain_grad = jnp.concatenate([gain_one, gain_two], axis=0)
    gain_grad = lax.psum(gain_grad, ("dp", "fsdp"))
    gain_grad = lax.dynamic_slice(gain_grad, (0, me * share), (2, share))
    grad_a = grad_a.astype(F32)
    grad_o = grad_a[:, :width]
    grad_i = grad_a[:, width:]
    grad_d = grad_d.astype(F32)

    results = [block_out, input_grad]
    results += adam_update(inward_weight, grad_w, inward_first, inward_second, rates[0], weight_decay)
    results += adam_update(outward_weight, grad_o, outward_first, outward_second, rates[1], weight_decay)
    results += adam_update(expand_weight, grad_i, expand_first, expand_second, rates[2], weight_decay)
    results += adam_update(shrink_weight, grad_d, shrink_first, shrink_second, rates[3], weight_decay)
    results += adam_update(gain_weight, gain_grad, gain_first, gain_second, rates[4], 0.0)
    return tuple(results)


def solution(mesh):
    split = P(None, "dp", "fsdp", None)
    rows = P("fsdp", None)
    columns = P(None, "fsdp")
    kinds = (rows, rows, rows, rows, columns)
    in_specs = (split, split, P(None, "dp")) + kinds * 3
    out_specs = (split, split) + (rows,) * 12 + (columns,) * 3
    return jax.shard_map(local, mesh=mesh, in_specs=in_specs, out_specs=out_specs, check_vma=False)
```

```python
import functools

import jax
import jax.numpy as jnp
from jax import lax
from jax.experimental import pallas as pl
from jax.experimental.pallas import tpu as pltpu
from jax.sharding import PartitionSpec as P

FF = 1152
HEADS = 12
HDIM = 64
STEP = 10

rope_base = 160000.0
norm_eps = 1e-05
adam_beta = 0.5
adam_eps = 1e-08
weight_decay = 0.01
rates = (0.07, 2.0, 0.07, 0.06, 0.2)
masked_score = -1e30

BF = jnp.bfloat16
F32 = jnp.float32
NN = (((1,), (0,)), ((), ()))
NT = (((1,), (1,)), ((), ()))
TN = (((0,), (0,)), ((), ()))
VMEM_BYTES = 58 << 20
LANES = 128
PAIRS = HEADS * HDIM // LANES


def cost(flops, size):
    return pl.CostEstimate(flops=int(flops), bytes_accessed=int(size), transcendentals=0)


def dot(left, right, dims=NN):
    return lax.dot_general(left, right, dims, preferred_element_type=F32)


def swap_halves(values):
    lane = lax.broadcasted_iota(jnp.int32, (1, LANES), 1)
    former = lax.rem(lane, HDIM) < HDIM // 2
    ahead = pltpu.roll(values, LANES - HDIM // 2, 1)
    behind = pltpu.roll(values, HDIM // 2, 1)
    return jnp.where(former, ahead, behind)


def centre_scale(values):
    center = values - jnp.mean(values, axis=-1, keepdims=True)
    spread = jnp.mean(center * center, axis=-1, keepdims=True)
    inverse = lax.rsqrt(spread + norm_eps)
    return center * inverse, inverse


def norm_back(grad, normed, inverse, gain):
    scaled = grad * gain
    mean_one = jnp.mean(scaled, axis=-1, keepdims=True)
    mean_two = jnp.mean(scaled * normed, axis=-1, keepdims=True)
    return inverse * (scaled - mean_one - normed * mean_two)


def place(scratch, pieces, info, rows):
    half = rows // 2
    for r, piece in enumerate(pieces):
        owner = info[0] ^ r
        for part, ref in enumerate(piece):
            side = part if r < 2 else info[2] ^ part
            at = pl.ds(pl.multiple_of(owner * rows + side * half, 32), half)
            for pair in range(PAIRS):
                for kind in range(3):
                    source = (kind * PAIRS + pair) * LANES
                    target = (pair * 3 + kind) * LANES
                    scratch[at, target : target + LANES] = ref[:half, source : source + LANES]


def pick(index, choices):
    value = choices[-1]
    for k in range(len(choices) - 2, -1, -1):
        value = jnp.where(index == k, choices[k], value)
    return value


def qkv_kernel(
    info, x_ref, cos_ref, sin_ref, w0, w1, w2a, w2b, w3a, w3b, ht_ref, qkv_ref, w_ref, gain_ref, *, share
):
    pieces = ((w0.at[0], w0.at[1]), (w1.at[0], w1.at[1]), (w2a, w2b), (w3a, w3b))

    @pl.when(pl.program_id(0) == 0)
    def _():
        place(w_ref, pieces, info, share)
        half = share // 2
        for row in range(2):
            found = []
            for r, piece in enumerate(pieces):
                one = piece[0][half : half + 1, :share].astype(F32)
                two = piece[1][half : half + 1, :share].astype(F32)
                swap = row if r < 2 else info[2] ^ row
                found.append(jnp.where(swap == 0, one, two))
            ordered = [pick(info[0] ^ owner, found) for owner in range(4)]
            gain_ref[row : row + 1, :] = jnp.concatenate(ordered, axis=1)

    normed, unused = centre_scale(x_ref[...].astype(F32))
    low = (normed * gain_ref[0:1, :]).astype(BF)
    ht_ref[...] = low.astype(F32).T.astype(BF)
    cosine = cos_ref[...]
    sine = sin_ref[...]
    for pair in range(PAIRS):
        start = pair * 3 * LANES
        joined = dot(low, w_ref[:, start : start + 3 * LANES])
        for kind in range(3):
            block = joined[:, kind * LANES : (kind + 1) * LANES]
            if kind < 2:
                block = block * cosine + swap_halves(block) * sine
            block = block.astype(BF)
            if kind == 0:
                block = block * jnp.asarray(HDIM**-0.5, BF)
            qkv_ref[:, start + kind * LANES : start + (kind + 1) * LANES] = block


def qkv_call(info, x, cosine, sine, pieces, tile=256):
    rows, width = x.shape
    wide = pieces[0].shape[2]
    whole = lambda i, s: (0, 0)
    by_row = lambda i, s: (i, 0)
    return pl.pallas_call(
        functools.partial(qkv_kernel, share=width // 4),
        grid_spec=pltpu.PrefetchScalarGridSpec(
            num_scalar_prefetch=1,
            grid=(rows // tile,),
            in_specs=[
                pl.BlockSpec((tile, width), by_row),
                pl.BlockSpec((tile, LANES), by_row),
                pl.BlockSpec((tile, LANES), by_row),
            ]
            + [pl.BlockSpec(piece.shape, lambda i, s, n=piece.ndim: (0,) * n) for piece in pieces],
            out_specs=[
                pl.BlockSpec((width, tile), lambda i, s: (0, i)),
                pl.BlockSpec((tile, wide), by_row),
                pl.BlockSpec((width, wide), whole),
                pl.BlockSpec((2, width), whole),
            ],
        ),
        out_shape=[
            jax.ShapeDtypeStruct((width, rows), BF),
            jax.ShapeDtypeStruct((rows, wide), BF),
            jax.ShapeDtypeStruct((width, wide), BF),
            jax.ShapeDtypeStruct((2, width), F32),
        ],
        compiler_params=pltpu.CompilerParams(vmem_limit_bytes=VMEM_BYTES),
        cost_estimate=cost(2 * rows * width * wide, 36e6),
        name="qkv",
    )(info, x, cosine, sine, *pieces)


def attend_kernel(info, qkv_ref, *rest, tile):
    o_ref, r_ref, p_ref = rest[-3:]
    rows = qkv_ref.shape[0]
    key_at = lax.broadcasted_iota(jnp.int32, (1, rows), 1)
    bias = jnp.where(key_at < info[1], 0.0, masked_score).astype(F32)
    keys = qkv_ref[:, LANES : 2 * LANES]
    values = qkv_ref[:, 2 * LANES :]
    low = lax.broadcasted_iota(jnp.int32, (1, LANES), 1) < HDIM
    one = jnp.ones((), BF)
    zero = jnp.zeros((), BF)
    sides = (jnp.where(low, values, one), jnp.where(low, one, values))
    for step in range(rows // tile):
        at = pl.ds(step * tile, tile)
        queries = qkv_ref[at, :LANES]
        heads = (jnp.where(low, queries, zero), jnp.where(low, zero, queries))
        outs = []
        for head in range(2):
            scores = dot(heads[head], keys, NT) + bias
            peak = jnp.max(scores, axis=-1, keepdims=True)
            terms = jnp.exp(scores - peak).astype(BF)
            p_ref[head, at, :] = terms
            outs.append(dot(terms, sides[head]))
        mixed = jnp.where(low, outs[0], outs[1])
        total = pltpu.roll(jnp.where(low, outs[1], outs[0]), HDIM, 1)
        inverse = 1.0 / total
        o_ref[at, :] = (mixed * inverse).astype(BF)
        r_ref[at, :] = inverse


def attend_call(info, qkv, start, count, buffers, tile=512):
    rows = qkv.shape[0]
    width = qkv.shape[1] // 3
    block = pl.BlockSpec((rows, LANES), lambda p, s: (0, start + p))
    buffers = tuple(buffers)
    return pl.pallas_call(
        functools.partial(attend_kernel, tile=tile),
        grid_spec=pltpu.PrefetchScalarGridSpec(
            num_scalar_prefetch=1,
            grid=(count,),
            in_specs=[pl.BlockSpec((rows, 3 * LANES), lambda p, s: (0, start + p))]
            + [pl.BlockSpec(memory_space=pl.ANY)] * len(buffers),
            out_specs=[
                block,
                block,
                pl.BlockSpec((2, rows, rows), lambda p, s: (start + p, 0, 0)),
            ],
        ),
        out_shape=[
            jax.ShapeDtypeStruct((rows, width), BF),
            jax.ShapeDtypeStruct((rows, width), F32),
            jax.ShapeDtypeStruct((HEADS, rows, rows), BF),
        ],
        input_output_aliases={2 + k: k for k in range(len(buffers))},
        compiler_params=pltpu.CompilerParams(vmem_limit_bytes=VMEM_BYTES),
        cost_estimate=cost(16 * rows * rows * LANES * count, 17e6 * count),
        name="attend",
    )(info, qkv, *buffers)


def feed_kernel(
    info, x_ref, o_ref, r_ref, cot_ref, gain_ref, m0, m1, m2a, m2b, m3a, m3b,
    out0, out1, out2, out3, dmid_ref, do_ref, gg_ref, keep_ref, send_ref,
    wo, wi, wd, acc_o, acc_i, acc_d, *, tile, share,
):
    step = pl.program_id(0)
    me = info[0]
    width = x_ref.shape[1]
    inner = wi.shape[1]
    base = width + inner
    half = share // 2

    @pl.when(step == 0)
    def _():
        pieces = ((m0.at[0], m0.at[1]), (m1.at[0], m1.at[1]), (m2a, m2b), (m3a, m3b))
        for r, piece in enumerate(pieces):
            owner = me ^ r
            for part, ref in enumerate(piece):
                side = part if r < 2 else info[2] ^ part
                at = pl.ds(pl.multiple_of(owner * share + side * half, 32), half)
                wo[at, :] = ref[:, :width]
                wi[at, :] = ref[:, width:base]
                down = owner * (3 * half)
                at = pl.ds(pl.multiple_of(down + side * half, 32), half)
                wd[at, :] = ref[:, base : base + width]
                at = pl.ds(pl.multiple_of(down + 2 * half, 32), half)

                @pl.when(side == 0)
                def _():
                    wd[at, : width // 2] = ref[:, base + width :]

                @pl.when(side == 1)
                def _():
                    wd[at, width // 2 :] = ref[:, base + width :]

        acc_o[...] = jnp.zeros_like(acc_o)
        acc_i[...] = jnp.zeros_like(acc_i)
        acc_d[...] = jnp.zeros_like(acc_d)
        gg_ref[...] = jnp.zeros_like(gg_ref)

    gain = gain_ref[1:2, :]
    mixed = o_ref[...]
    middle = x_ref[...].astype(F32) + dot(mixed, wo[...])
    normed, inverse = centre_scale(middle)
    hidden = (normed * gain).astype(BF)
    gate = dot(hidden, wi[:, :FF])
    upward = dot(hidden, wi[:, FF:])
    cdf = 0.5 * (1.0 + lax.erf(gate * 0.7071067811865476))
    gelu = gate * cdf
    slope = cdf + gate * (jnp.exp(-0.5 * gate * gate) * 0.3989422804014327)
    state = (gelu * upward).astype(BF)
    row_at = step * tile + lax.broadcasted_iota(jnp.int32, (tile, 1), 0)
    live = row_at < info[1]
    result = jnp.where(live, middle + dot(state, wd[...]), 0.0).astype(BF)
    for r, out_ref in enumerate((out0, out1, out2, out3)):

        @pl.when(me ^ step == r)
        def _():
            out_ref[...] = result

    branch = jnp.where(live, cot_ref[...].astype(F32), 0.0)
    branch_low = branch.astype(BF)
    acc_d[...] += dot(state, branch_low, TN)
    state_grad = dot(branch_low, wd[...], NT)
    gate_grad = (state_grad * upward * slope).astype(BF)
    up_grad = (state_grad * gelu).astype(BF)
    acc_i[:, :FF] += dot(hidden, gate_grad, TN)
    acc_i[:, FF:] += dot(hidden, up_grad, TN)
    hidden_grad = dot(gate_grad, wi[:, :FF], NT) + dot(up_grad, wi[:, FF:], NT)
    gg_ref[...] += jnp.sum(hidden_grad * normed, axis=0, keepdims=True)
    middle_grad = branch + norm_back(hidden_grad, normed, inverse, gain)
    dmid_ref[...] = middle_grad
    mixer = middle_grad.astype(BF)
    acc_o[...] += dot(mixed, mixer, TN)
    do_ref[...] = (dot(mixer, wo[...], NT) * r_ref[...]).astype(BF)

    @pl.when(step == pl.num_programs(0) - 1)
    def _():
        for r in range(4):
            owner = me ^ r
            at = pl.ds(pl.multiple_of(owner * share, 32), share)
            target = send_ref if r % 2 else keep_ref
            slot = r // 2
            target[slot, :, :width] = acc_o[at, :].astype(BF)
            target[slot, :, width:base] = acc_i[at, :].astype(BF)
            down = owner * (3 * half)
            target[slot, :, base : base + width] = acc_d[pl.ds(pl.multiple_of(down, 32), share), :].astype(BF)
            rest = acc_d[pl.ds(pl.multiple_of(down + share, 32), half), :].astype(BF)
            target[slot, :half, base + width :] = rest[:, : width // 2]
            target[slot, half:, base + width :] = rest[:, width // 2 :]


def feed_call(info, x, mixed, inverse, cot, gain, pieces):
    rows, width = x.shape
    tile = rows // 4
    share = width // 4
    packed = pieces[0].shape[2]
    whole = lambda i, s: (0, 0)
    cube = lambda i, s: (0, 0, 0)
    by_row = lambda i, s: (i, 0)
    block = pl.BlockSpec((tile, width), by_row)
    return pl.pallas_call(
        functools.partial(feed_kernel, tile=tile, share=share),
        grid_spec=pltpu.PrefetchScalarGridSpec(
            num_scalar_prefetch=1,
            grid=(rows // tile,),
            in_specs=[block, block, block, block, pl.BlockSpec((2, width), whole)]
            + [pl.BlockSpec(piece.shape, lambda i, s, n=piece.ndim: (0,) * n) for piece in pieces],
            out_specs=[pl.BlockSpec((tile, width), whole)] * 4
            + [block, block, pl.BlockSpec((1, width), whole)]
            + [pl.BlockSpec((2, share, packed), cube)] * 2,
            scratch_shapes=[
                pltpu.VMEM((width, width), BF),
                pltpu.VMEM((width, 2 * FF), BF),
                pltpu.VMEM((FF, width), BF),
                pltpu.VMEM((width, width), F32),
                pltpu.VMEM((width, 2 * FF), F32),
                pltpu.VMEM((FF, width), F32),
            ],
        ),
        out_shape=[jax.ShapeDtypeStruct((tile, width), BF)] * 4
        + [
            jax.ShapeDtypeStruct((rows, width), F32),
            jax.ShapeDtypeStruct((rows, width), BF),
            jax.ShapeDtypeStruct((1, width), F32),
        ]
        + [jax.ShapeDtypeStruct((2, share, packed), BF)] * 2,
        compiler_params=pltpu.CompilerParams(vmem_limit_bytes=VMEM_BYTES),
        cost_estimate=cost(6 * rows * width * (width + 3 * FF), 130e6),
        name="feed",
    )(info, x, mixed, inverse, cot, gain, *pieces)


def back_kernel(info, qkv_ref, o_ref, do_ref, p_ref, cos_ref, sin_ref, ht_ref, *rest, tile):
    keep_ref, send_ref, joined_ref = rest[-3:]
    rows = qkv_ref.shape[0]
    low = lax.broadcasted_iota(jnp.int32, (1, LANES), 1) < HDIM
    zero = jnp.zeros((), BF)
    keys = qkv_ref[:, LANES : 2 * LANES]
    values = qkv_ref[:, 2 * LANES :]
    key_heads = (jnp.where(low, keys, zero), jnp.where(low, zero, keys))
    key_grads = [None, None]
    value_grads = [None, None]
    query_grads = []
    for part in range(rows // tile):
        at = pl.ds(part * tile, tile)
        queries = qkv_ref[at, :LANES]
        grads = do_ref[at, :]
        wide = grads.astype(F32)
        inner = wide * o_ref[at, :].astype(F32)
        grad_heads = (jnp.where(low, grads, zero), jnp.where(low, zero, grads))
        queries_t = queries.astype(F32).T.astype(BF)
        grads_t = wide.T.astype(BF)
        query_grad = None
        for head in range(2):
            mine = low if head == 0 else jnp.logical_not(low)
            lanes = slice(head * HDIM, (head + 1) * HDIM)
            row_inner = jnp.sum(jnp.where(mine, inner, 0.0), axis=-1, keepdims=True)
            term_grad = dot(grad_heads[head], values, NT)
            terms = p_ref[head, at, :]
            score_grad = (terms.astype(F32) * (term_grad - row_inner)).astype(BF)
            partial = dot(score_grad, key_heads[head])
            query_grad = partial if query_grad is None else query_grad + partial
            for grad_list, left, right in (
                (key_grads, queries_t, score_grad),
                (value_grads, grads_t, terms),
            ):
                value = dot(left[lanes], right)
                grad_list[head] = value if grad_list[head] is None else grad_list[head] + value
        query_grads.append(query_grad)
    cosine = cos_ref[...]
    sine = sin_ref[...]
    query_grad = jnp.concatenate(query_grads, axis=0) * (HDIM**-0.5)
    key_grad = jnp.concatenate(key_grads, axis=0).T
    value_grad = jnp.concatenate(value_grads, axis=0).T
    joined = jnp.concatenate(
        [
            (query_grad * cosine - swap_halves(query_grad) * sine).astype(BF),
            (key_grad * cosine - swap_halves(key_grad) * sine).astype(BF),
            value_grad.astype(BF),
        ],
        axis=1,
    )
    joined_ref[...] = joined
    weight_grad = dot(ht_ref[...], joined).astype(BF)
    share = weight_grad.shape[0] // 4
    me = info[0]
    for owner in range(4):
        rel = me ^ owner
        value = weight_grad[owner * share : (owner + 1) * share, :]
        for target, odd in ((keep_ref, 0), (send_ref, 1)):

            @pl.when(rel % 2 == odd)
            def _():
                target[rel // 2] = value


def back_call(info, qkv, mixed, grads, terms, cosine, sine, hidden_t, start, count, slot, slots, buffers, tile=512):
    rows, width = mixed.shape
    whole = lambda p, s: (0, 0)
    block = pl.BlockSpec((rows, LANES), lambda p, s: (0, start + p))
    wide = pl.BlockSpec((rows, 3 * LANES), lambda p, s: (0, start + p))
    table = pl.BlockSpec((rows, LANES), whole)
    operands = [qkv, mixed, grads, terms, cosine, sine, hidden_t]
    share = width // 4
    piece = pl.BlockSpec((2, share, 3 * LANES), lambda p, s: (0, 0, slot + p))
    chunk = jax.ShapeDtypeStruct((2, share, 3 * LANES * slots), BF)
    aliases = {}
    for k, buffer in enumerate(buffers):
        aliases[1 + len(operands)] = 3 - len(buffers) + k
        operands.append(buffer)
    return pl.pallas_call(
        functools.partial(back_kernel, tile=tile),
        grid_spec=pltpu.PrefetchScalarGridSpec(
            num_scalar_prefetch=1,
            grid=(count,),
            in_specs=[
                wide,
                block,
                block,
                pl.BlockSpec((2, rows, rows), lambda p, s: (start + p, 0, 0)),
                table,
                table,
                pl.BlockSpec((width, rows), whole),
            ]
            + [pl.BlockSpec(memory_space=pl.ANY)] * len(buffers),
            out_specs=[piece, piece, wide],
        ),
        out_shape=[chunk, chunk, jax.ShapeDtypeStruct((rows, 3 * width), BF)],
        input_output_aliases=aliases,
        compiler_params=pltpu.CompilerParams(vmem_limit_bytes=VMEM_BYTES),
        cost_estimate=cost(20 * rows * rows * LANES * count, 36e6 * count),
        name="back",
    )(info, *operands)


def finish_kernel(
    info, joined_ref, w_ref, x_ref, dmid_ref, gain_ref, gg_ref, dx0, dx1, dx2, dx3, keep_ref, send_ref, total
):
    step = pl.program_id(0)
    me = info[0]

    @pl.when(step == 0)
    def _():
        total[...] = jnp.zeros_like(total)

    normed, inverse = centre_scale(x_ref[...].astype(F32))
    hidden_grad = dot(joined_ref[...], w_ref[...], NT)
    total[...] += jnp.sum(hidden_grad * normed, axis=0, keepdims=True)
    back = norm_back(hidden_grad, normed, inverse, gain_ref[0:1, :])
    result = (dmid_ref[...] + back).astype(BF)
    for r, dx_ref in enumerate((dx0, dx1, dx2, dx3)):

        @pl.when(me ^ step == r)
        def _():
            dx_ref[...] = result

    @pl.when(step == pl.num_programs(0) - 1)
    def _():
        one = total[...]
        two = gg_ref[...]
        share = one.shape[1] // 4
        for r, target in enumerate((keep_ref, send_ref, keep_ref, send_ref)):
            parts = [slice(owner * share, (owner + 1) * share) for owner in range(4)]
            gains = [pick(me ^ r, [value[:, part] for part in parts]) for value in (one, two)]
            gains = jnp.concatenate(gains, axis=1)
            target[r // 2] = jnp.broadcast_to(gains, target.shape[1:]).astype(BF)


def finish_call(info, joined, weight, x, dmid, gain, gain_two):
    rows, width = x.shape
    tile = rows // 4
    wide = joined.shape[1]
    by_row = lambda i, s: (i, 0)
    whole = lambda i, s: (0, 0)
    cube = lambda i, s: (0, 0, 0)
    gains = (2, 8, width // 2)
    return pl.pallas_call(
        finish_kernel,
        grid_spec=pltpu.PrefetchScalarGridSpec(
            num_scalar_prefetch=1,
            grid=(4,),
            in_specs=[
                pl.BlockSpec((tile, wide), by_row),
                pl.BlockSpec((width, wide), whole),
                pl.BlockSpec((tile, width), by_row),
                pl.BlockSpec((tile, width), by_row),
                pl.BlockSpec((2, width), whole),
                pl.BlockSpec((1, width), whole),
            ],
            out_specs=[pl.BlockSpec((tile, width), whole)] * 4 + [pl.BlockSpec(gains, cube)] * 2,
            scratch_shapes=[pltpu.VMEM((1, width), F32)],
        ),
        out_shape=[jax.ShapeDtypeStruct((tile, width), BF)] * 4 + [jax.ShapeDtypeStruct(gains, BF)] * 2,
        compiler_params=pltpu.CompilerParams(vmem_limit_bytes=VMEM_BYTES),
        cost_estimate=cost(2 * rows * width * wide, 24e6),
        name="finish",
    )(info, joined, weight, x, dmid, gain, gain_two)


def restore_kernel(info, p0, p1, p2, p3, out_ref):
    for r, piece in enumerate((p0, p1, p2, p3)):
        out_ref[info[0] ^ r] = piece[...].astype(out_ref.dtype)


def restore_call(info, pieces, kind):
    rows, width = pieces[0].shape
    return pl.pallas_call(
        restore_kernel,
        grid_spec=pltpu.PrefetchScalarGridSpec(
            num_scalar_prefetch=1,
            grid=(1,),
            in_specs=[pl.BlockSpec((rows, width), lambda i, s: (0, 0))] * 4,
            out_specs=pl.BlockSpec((4, rows, width), lambda i, s: (0, 0, 0)),
        ),
        out_shape=jax.ShapeDtypeStruct((4, rows, width), kind),
        compiler_params=pltpu.CompilerParams(vmem_limit_bytes=VMEM_BYTES),
        cost_estimate=cost(0, 12e6),
        name="restore",
    )(info, *pieces)


def adam_update(master, gradient, moment_one, moment_two, step_rate, decay_rate):
    first_new = adam_beta * moment_one + (1.0 - adam_beta) * gradient
    second_new = adam_beta * moment_two + (1.0 - adam_beta) * gradient * gradient
    correction = 1.0 - adam_beta**STEP
    direction = first_new / correction / (jnp.sqrt(second_new / correction) + adam_eps)
    renewed = master - step_rate * (direction + decay_rate * master)
    return (renewed, first_new, second_new)


def tables(seq_total):
    lane = jnp.arange(LANES, dtype=jnp.int32)
    exponent = (lane % (HDIM // 2)).astype(F32) * (2.0 / HDIM)
    inverse = jnp.power(jnp.float32(rope_base), -exponent)
    angles = jnp.arange(seq_total, dtype=F32)[:, None] * inverse[None, :]
    sign = jnp.where(lane % HDIM < HDIM // 2, -1.0, 1.0).astype(F32)
    return jnp.cos(angles), jnp.sin(angles) * sign[None, :]


CORE = [(0, 1), (1, 0), (2, 3), (3, 2)]
CROSS = [(0, 2), (1, 3), (2, 0), (3, 1)]
tie = lax.optimization_barrier


def over_core(array):
    return lax.ppermute(array, "fsdp", CORE)


def over_cross(array):
    return lax.ppermute(array, "fsdp", CROSS)


def over_side(array):
    return lax.ppermute(array, "dp", [(k, k ^ 1) for k in range(lax.axis_size("dp"))])


def along_line(array, groups=None):
    return lax.all_to_all(array, "dp", 0, 0, axis_index_groups=groups)


def add_low(left, right):
    return (left.astype(F32) + right.astype(F32)).astype(BF)


def sum_low(array):
    return jnp.sum(array.astype(F32), axis=0).astype(BF)


def pick_half(array, index, axis=0):
    return lax.dynamic_index_in_dim(array, index, axis, keepdims=False)


def local(
    tokens, cotangent, lengths,
    inward_weight, outward_weight, expand_weight, shrink_weight, gain_weight,
    inward_first, outward_first, expand_first, shrink_first, gain_first,
    inward_second, outward_second, expand_second, shrink_second, gain_second,
):
    micro_count, group_size, local_len, width = tokens.shape
    fsdp = lax.axis_size("fsdp")
    lines = lax.axis_size("dp")
    assert fsdp == 4 and micro_count * group_size == fsdp and lines % 2 == 0
    seq_total = local_len * fsdp
    share, wide = inward_weight.shape
    half = share // 2
    me = lax.axis_index("fsdp").astype(jnp.int32)
    side = (lax.axis_index("dp") % 2).astype(jnp.int32)
    info = jnp.stack([me, pick_half(lengths.reshape(fsdp), me), side])
    columns = [[k for k in range(lines) if k % 2 == odd] for odd in range(2)]

    def to_sequence(array):
        array = array.reshape(fsdp, local_len, width)
        return lax.all_to_all(array, "fsdp", 0, 0).reshape(seq_total, width)

    def with_gains(weight, gains):
        gains = jnp.pad(gains.astype(BF)[:, None, :], ((0, 0), (0, 7), (0, wide - share)))
        return jnp.concatenate([weight.astype(BF), gains], axis=1)

    inward_halves = inward_weight.reshape(2, half, wide)
    leaving = with_gains(pick_half(inward_halves, side)[None], pick_half(gain_weight, side)[None])[0]
    far_one = over_cross(leaving)

    (inward_halves, outward, leaving) = tie((inward_halves, outward_weight, leaving))
    own = with_gains(inward_halves, gain_weight)
    near = over_core(own)
    tokens, own = tie((tokens, own))
    x = to_sequence(tokens)
    shrink_low = shrink_weight.astype(BF)
    folded = jnp.concatenate([shrink_low[share:, : width // 2], shrink_low[share:, width // 2 :]], axis=0)
    packed = jnp.concatenate(
        [outward.astype(BF), expand_weight.astype(BF), shrink_low[:share], folded], axis=1
    ).reshape(2, half, -1)
    cosine, sine = tables(seq_total)
    leaving = pick_half(packed, side)
    far_one, cosine, sine, info, packed, leaving = tie((far_one, cosine, sine, info, packed, leaving))
    far_two = over_side(far_one)
    inward_pieces = (own, near, far_one, far_two, over_core(far_one), over_core(far_two))

    leaving, x = tie((leaving, x))
    other_far_one = over_cross(leaving)
    other_near = over_core(packed)

    hidden_t, qkv, weight, gain = qkv_call(info, x, cosine, sine, inward_pieces)
    cotangent, qkv = tie((cotangent, qkv))
    cot = to_sequence(cotangent)
    buffers = attend_call(info, qkv, 0, 2, ())
    other_far_one, buffers = tie((other_far_one, buffers))
    other_far_two = over_side(other_far_one)
    mixed, inverse, terms = attend_call(info, qkv, 2, 4, buffers)
    mixed, other_far_two = tie((mixed, other_far_two))
    other_pieces = (
        packed, other_near, other_far_one, other_far_two, over_core(other_far_one), over_core(other_far_two)
    )
    *out, middle_grad, grads, gain_two, keep, send = feed_call(info, x, mixed, inverse, cot, gain, other_pieces)

    def back(start, count, slot, slots, buffers):
        return back_call(
            info, qkv, mixed, grads, terms, cosine, sine, hidden_t, start, count, slot, slots, buffers
        )

    arrived = over_core(send)
    keep_x, send_x, joined = back(0, 1, 0, 3, ())
    total, joined = tie((add_low(keep, arrived), joined))
    first_y = over_cross(total[1, :half])
    second = total[:, half:].reshape(2, 2, half // 2, -1)
    second_x = over_side(pick_half(second, 1 - side, 1))
    keep_x, send_x, joined = back(1, 2, 1, 3, (keep_x, send_x, joined))
    arrived_x = over_core(send_x)
    first = add_low(total[0, :half], first_y).reshape(2, half // 2, -1)
    second = add_low(pick_half(second, side, 1), second_x)
    first, second, out, joined = tie((first, second, out, joined))
    first_x = over_side(pick_half(first, 1 - side))
    second_y = over_cross(second[1])
    keep_z, send_z, joined = back(3, 1, 0, 3, (joined,))
    first = add_low(pick_half(first, side), first_x)
    second = add_low(second[0], second_y)
    total_x = add_low(keep_x, arrived_x)
    both = jnp.concatenate([first, second], axis=0)
    both, total_x, out, joined = tie((both, total_x, out, joined))
    level = lines // 2
    both = both.reshape(level, half // level, -1)
    place = lax.axis_index("dp") // 2

    def halve(array, gap):
        count = array.shape[0] // 2
        array = array.reshape((count, 2) + array.shape[1:])
        bit = (place // gap) % 2
        going = pick_half(array, 1 - bit, 1)
        came = lax.ppermute(going, "dp", [(k, k ^ (2 * gap)) for k in range(lines)])
        return pick_half(array, bit, 1), came

    gap = 1
    far_x = over_cross(total_x[1])
    stay, came = halve(both, gap)
    keep_z, send_z, joined = back(4, 1, 1, 3, (keep_z, send_z, joined))
    while gap * 2 < level:
        both = add_low(stay, came)
        gap = gap * 2
        stay, came = halve(both, gap)
    chunk_x = add_low(total_x[0], far_x)
    stay, chunk_x, joined = tie((stay, chunk_x, joined))
    chunk_x = along_line(chunk_x.reshape(lines, share // lines, -1))
    near_out = over_core(out[1])
    far_out = over_cross(out[2])
    diagonal_out = over_cross(out[3])
    keep_z, send_z, joined = back(5, 1, 2, 3, (keep_z, send_z, joined))
    both = add_low(stay, came)[0]
    arrived_z = over_core(send_z)
    both, joined = tie((both, joined))
    both = lax.all_gather(both, "dp", axis=0)
    chunk_x = sum_low(chunk_x)
    chunk_x, joined = tie((chunk_x, joined))
    chunk_x = along_line(jnp.broadcast_to(chunk_x[None], (lines,) + chunk_x.shape)).reshape(share, -1)
    *input_low, gain_keep, gain_send = finish_call(info, joined, weight, x, middle_grad, gain, gain_two)
    total_z = add_low(keep_z, arrived_z)
    far_z = over_cross(total_z[1])
    gain_total = add_low(gain_keep, over_core(gain_send))
    gain_row = add_low(gain_total[0], over_cross(gain_total[1]))

    chunk_z = add_low(total_z[0], far_z).reshape(lines, share // lines, -1)
    gain_row = jnp.pad(gain_row[:1], ((0, 0), (0, chunk_z.shape[2] - 2 * share)))
    chunk_z = jnp.concatenate([chunk_z, jnp.broadcast_to(gain_row[None], (lines, 1, chunk_z.shape[2]))], axis=1)
    chunk_x, chunk_z = tie((chunk_x, chunk_z))
    chunk_z = sum_low(along_line(chunk_z))
    chunk_z = along_line(jnp.broadcast_to(chunk_z[None], (lines,) + chunk_z.shape))
    gain_grad = chunk_z[0, share // lines, : 2 * share].reshape(2, share).astype(F32)
    chunk_z = chunk_z[:, : share // lines].reshape(share, -1)

    block_out = restore_call(info, (out[0], near_out, far_out, over_core(diagonal_out)), BF).reshape(tokens.shape)
    far_low, diagonal_low, far_z = tie((input_low[2], input_low[3], far_z))
    pieces = (input_low[0], over_core(input_low[1]), over_cross(far_low), over_core(over_cross(diagonal_low)))
    input_grad = restore_call(info, pieces, F32).reshape(tokens.shape)

    both = both.reshape(level, 2, half // level, -1).transpose(1, 0, 2, 3).reshape(2, 2, half // 2, -1)
    grad_m = both.transpose(1, 0, 2, 3).reshape(share, -1).astype(F32)
    grad_o = grad_m[:, :width]
    grad_i = grad_m[:, width : width + 2 * FF]
    rest = grad_m[:, width + 2 * FF :]
    grad_d = jnp.concatenate(
        [rest[:, :width], jnp.concatenate([rest[:half, width:], rest[half:, width:]], axis=1)], axis=0
    )
    grad_w = jnp.concatenate([chunk_x, chunk_z], axis=1).astype(F32)
    grad_w = grad_w.reshape(share, PAIRS, 3, LANES).transpose(0, 2, 1, 3).reshape(share, wide)

    results = [block_out, input_grad]
    results += adam_update(inward_weight, grad_w, inward_first, inward_second, rates[0], weight_decay)
    results += adam_update(outward_weight, grad_o, outward_first, outward_second, rates[1], weight_decay)
    results += adam_update(expand_weight, grad_i, expand_first, expand_second, rates[2], weight_decay)
    results += adam_update(shrink_weight, grad_d, shrink_first, shrink_second, rates[3], weight_decay)
    results += adam_update(gain_weight, gain_grad, gain_first, gain_second, rates[4], 0.0)
    return tuple(results)


def solution(mesh):
    split = P(None, "dp", "fsdp", None)
    rows = P("fsdp", None)
    columns = P(None, "fsdp")
    kinds = (rows, rows, rows, rows, columns)
    in_specs = (split, split, P(None, "dp")) + kinds * 3
    out_specs = (split, split) + (rows,) * 12 + (columns,) * 3
    return jax.shard_map(local, mesh=mesh, in_specs=in_specs, out_specs=out_specs, check_vma=False)
```

```python
import functools

import jax
import jax.numpy as jnp
from jax import lax
from jax.experimental import pallas as pl
from jax.experimental.pallas import tpu as pltpu
from jax.sharding import PartitionSpec as P

FF = 1152
HEADS = 12
HDIM = 64
STEP = 10

rope_base = 160000.0
norm_eps = 1e-05
adam_beta = 0.5
adam_eps = 1e-08
weight_decay = 0.01
rates = (0.07, 2.0, 0.07, 0.06, 0.2)
masked_score = -1e30

BF = jnp.bfloat16
F32 = jnp.float32
NN = (((1,), (0,)), ((), ()))
NT = (((1,), (1,)), ((), ()))
TN = (((0,), (0,)), ((), ()))
VMEM_BYTES = 58 << 20
LANES = 128
PAIRS = HEADS * HDIM // LANES


def cost(flops, size):
    return pl.CostEstimate(flops=int(flops), bytes_accessed=int(size), transcendentals=0)


def dot(left, right, dims=NN):
    return lax.dot_general(left, right, dims, preferred_element_type=F32)


def swap_halves(values):
    lane = lax.broadcasted_iota(jnp.int32, (1, LANES), 1)
    former = lax.rem(lane, HDIM) < HDIM // 2
    ahead = pltpu.roll(values, LANES - HDIM // 2, 1)
    behind = pltpu.roll(values, HDIM // 2, 1)
    return jnp.where(former, ahead, behind)


def centre_scale(values):
    center = values - jnp.mean(values, axis=-1, keepdims=True)
    spread = jnp.mean(center * center, axis=-1, keepdims=True)
    inverse = lax.rsqrt(spread + norm_eps)
    return center * inverse, inverse


def norm_back(grad, normed, inverse, gain):
    scaled = grad * gain
    mean_one = jnp.mean(scaled, axis=-1, keepdims=True)
    mean_two = jnp.mean(scaled * normed, axis=-1, keepdims=True)
    return inverse * (scaled - mean_one - normed * mean_two)


def place(scratch, pieces, info, rows):
    half = rows // 2
    for r, piece in enumerate(pieces):
        owner = info[0] ^ r
        for part, ref in enumerate(piece):
            side = part if r < 2 else info[2] ^ part
            at = pl.ds(pl.multiple_of(owner * rows + side * half, 32), half)
            for pair in range(PAIRS):
                for kind in range(3):
                    source = (kind * PAIRS + pair) * LANES
                    target = (pair * 3 + kind) * LANES
                    scratch[at, target : target + LANES] = ref[:half, source : source + LANES]


def pick(index, choices):
    value = choices[-1]
    for k in range(len(choices) - 2, -1, -1):
        value = jnp.where(index == k, choices[k], value)
    return value


def qkv_kernel(
    info, x_ref, cos_ref, sin_ref, w0, w1, w2a, w2b, w3a, w3b, ht_ref, qkv_ref, w_ref, gain_ref, *, share
):
    pieces = ((w0.at[0], w0.at[1]), (w1.at[0], w1.at[1]), (w2a, w2b), (w3a, w3b))

    @pl.when(pl.program_id(0) == 0)
    def _():
        place(w_ref, pieces, info, share)
        half = share // 2
        for row in range(2):
            found = []
            for r, piece in enumerate(pieces):
                one = piece[0][half : half + 1, :share].astype(F32)
                two = piece[1][half : half + 1, :share].astype(F32)
                swap = row if r < 2 else info[2] ^ row
                found.append(jnp.where(swap == 0, one, two))
            ordered = [pick(info[0] ^ owner, found) for owner in range(4)]
            gain_ref[row : row + 1, :] = jnp.concatenate(ordered, axis=1)

    normed, unused = centre_scale(x_ref[...].astype(F32))
    low = (normed * gain_ref[0:1, :]).astype(BF)
    ht_ref[...] = low.astype(F32).T.astype(BF)
    cosine = cos_ref[...]
    sine = sin_ref[...]
    for pair in range(PAIRS):
        start = pair * 3 * LANES
        joined = dot(low, w_ref[:, start : start + 3 * LANES])
        for kind in range(3):
            block = joined[:, kind * LANES : (kind + 1) * LANES]
            if kind < 2:
                block = block * cosine + swap_halves(block) * sine
            block = block.astype(BF)
            if kind == 0:
                block = block * jnp.asarray(HDIM**-0.5, BF)
            qkv_ref[:, start + kind * LANES : start + (kind + 1) * LANES] = block


def qkv_call(info, x, cosine, sine, pieces, tile=256):
    rows, width = x.shape
    wide = pieces[0].shape[2]
    whole = lambda i, s: (0, 0)
    by_row = lambda i, s: (i, 0)
    return pl.pallas_call(
        functools.partial(qkv_kernel, share=width // 4),
        grid_spec=pltpu.PrefetchScalarGridSpec(
            num_scalar_prefetch=1,
            grid=(rows // tile,),
            in_specs=[
                pl.BlockSpec((tile, width), by_row),
                pl.BlockSpec((tile, LANES), by_row),
                pl.BlockSpec((tile, LANES), by_row),
            ]
            + [pl.BlockSpec(piece.shape, lambda i, s, n=piece.ndim: (0,) * n) for piece in pieces],
            out_specs=[
                pl.BlockSpec((width, tile), lambda i, s: (0, i)),
                pl.BlockSpec((tile, wide), by_row),
                pl.BlockSpec((width, wide), whole),
                pl.BlockSpec((2, width), whole),
            ],
        ),
        out_shape=[
            jax.ShapeDtypeStruct((width, rows), BF),
            jax.ShapeDtypeStruct((rows, wide), BF),
            jax.ShapeDtypeStruct((width, wide), BF),
            jax.ShapeDtypeStruct((2, width), F32),
        ],
        compiler_params=pltpu.CompilerParams(vmem_limit_bytes=VMEM_BYTES),
        cost_estimate=cost(2 * rows * width * wide, 36e6),
        name="qkv",
    )(info, x, cosine, sine, *pieces)


def attend_kernel(info, qkv_ref, *rest, tile):
    o_ref, r_ref, p_ref = rest[-3:]
    rows = qkv_ref.shape[0]
    key_at = lax.broadcasted_iota(jnp.int32, (1, rows), 1)
    bias = jnp.where(key_at < info[1], 0.0, masked_score).astype(F32)
    keys = qkv_ref[:, LANES : 2 * LANES]
    values = qkv_ref[:, 2 * LANES :]
    low = lax.broadcasted_iota(jnp.int32, (1, LANES), 1) < HDIM
    one = jnp.ones((), BF)
    zero = jnp.zeros((), BF)
    sides = (jnp.where(low, values, one), jnp.where(low, one, values))
    for step in range(rows // tile):
        at = pl.ds(step * tile, tile)
        queries = qkv_ref[at, :LANES]
        heads = (jnp.where(low, queries, zero), jnp.where(low, zero, queries))
        outs = []
        for head in range(2):
            scores = dot(heads[head], keys, NT) + bias
            peak = jnp.max(scores, axis=-1, keepdims=True)
            terms = jnp.exp(scores - peak).astype(BF)
            p_ref[head, at, :] = terms
            outs.append(dot(terms, sides[head]))
        mixed = jnp.where(low, outs[0], outs[1])
        total = pltpu.roll(jnp.where(low, outs[1], outs[0]), HDIM, 1)
        inverse = 1.0 / total
        o_ref[at, :] = (mixed * inverse).astype(BF)
        r_ref[at, :] = inverse


def attend_call(info, qkv, start, count, buffers, tile=512):
    rows = qkv.shape[0]
    width = qkv.shape[1] // 3
    block = pl.BlockSpec((rows, LANES), lambda p, s: (0, start + p))
    buffers = tuple(buffers)
    return pl.pallas_call(
        functools.partial(attend_kernel, tile=tile),
        grid_spec=pltpu.PrefetchScalarGridSpec(
            num_scalar_prefetch=1,
            grid=(count,),
            in_specs=[pl.BlockSpec((rows, 3 * LANES), lambda p, s: (0, start + p))]
            + [pl.BlockSpec(memory_space=pl.ANY)] * len(buffers),
            out_specs=[
                block,
                block,
                pl.BlockSpec((2, rows, rows), lambda p, s: (start + p, 0, 0)),
            ],
        ),
        out_shape=[
            jax.ShapeDtypeStruct((rows, width), BF),
            jax.ShapeDtypeStruct((rows, width), F32),
            jax.ShapeDtypeStruct((HEADS, rows, rows), BF),
        ],
        input_output_aliases={2 + k: k for k in range(len(buffers))},
        compiler_params=pltpu.CompilerParams(vmem_limit_bytes=VMEM_BYTES),
        cost_estimate=cost(16 * rows * rows * LANES * count, 17e6 * count),
        name="attend",
    )(info, qkv, *buffers)


def feed_kernel(
    info, x_ref, o_ref, r_ref, cot_ref, gain_ref, m0, m1, m2a, m2b, m3a, m3b,
    out0, out1, out2, out3, dmid_ref, do_ref, keep_ref, send_ref,
    wo, wi, wd, acc_o, acc_i, acc_d, *, tile, share,
):
    step = pl.program_id(0)
    me = info[0]
    width = x_ref.shape[1]
    inner = wi.shape[1]
    base = width + inner
    half = share // 2

    @pl.when(step == 0)
    def _():
        pieces = ((m0.at[0], m0.at[1]), (m1.at[0], m1.at[1]), (m2a, m2b), (m3a, m3b))
        for r, piece in enumerate(pieces):
            owner = me ^ r
            for part, ref in enumerate(piece):
                side = part if r < 2 else info[2] ^ part
                at = pl.ds(pl.multiple_of(owner * share + side * half, 32), half)
                wo[at, :] = ref[:, :width]
                wi[at, :] = ref[:, width:base]
                down = owner * (3 * half)
                at = pl.ds(pl.multiple_of(down + side * half, 32), half)
                wd[at, :] = ref[:, base : base + width]
                at = pl.ds(pl.multiple_of(down + 2 * half, 32), half)

                @pl.when(side == 0)
                def _():
                    wd[at, : width // 2] = ref[:, base + width :]

                @pl.when(side == 1)
                def _():
                    wd[at, width // 2 :] = ref[:, base + width :]

        acc_o[...] = jnp.zeros_like(acc_o)
        acc_i[...] = jnp.zeros_like(acc_i)
        acc_d[...] = jnp.zeros_like(acc_d)

    gain = gain_ref[1:2, :]
    mixed = o_ref[...]
    middle = x_ref[...].astype(F32) + dot(mixed, wo[...])
    normed, inverse = centre_scale(middle)
    hidden = (normed * gain).astype(BF)
    gate = dot(hidden, wi[:, :FF])
    upward = dot(hidden, wi[:, FF:])
    cdf = 0.5 * (1.0 + lax.erf(gate * 0.7071067811865476))
    gelu = gate * cdf
    slope = cdf + gate * (jnp.exp(-0.5 * gate * gate) * 0.3989422804014327)
    state = (gelu * upward).astype(BF)
    row_at = step * tile + lax.broadcasted_iota(jnp.int32, (tile, 1), 0)
    live = row_at < info[1]
    result = jnp.where(live, middle + dot(state, wd[...]), 0.0).astype(BF)
    for r, out_ref in enumerate((out0, out1, out2, out3)):

        @pl.when(me ^ step == r)
        def _():
            out_ref[...] = result

    branch = jnp.where(live, cot_ref[...].astype(F32), 0.0)
    branch_low = branch.astype(BF)
    acc_d[...] += dot(state, branch_low, TN)
    state_grad = dot(branch_low, wd[...], NT)
    gate_grad = (state_grad * upward * slope).astype(BF)
    up_grad = (state_grad * gelu).astype(BF)
    acc_i[:, :FF] += dot(hidden, gate_grad, TN)
    acc_i[:, FF:] += dot(hidden, up_grad, TN)
    hidden_grad = dot(gate_grad, wi[:, :FF], NT) + dot(up_grad, wi[:, FF:], NT)
    middle_grad = branch + norm_back(hidden_grad, normed, inverse, gain)
    dmid_ref[...] = middle_grad
    mixer = middle_grad.astype(BF)
    acc_o[...] += dot(mixed, mixer, TN)
    do_ref[...] = (dot(mixer, wo[...], NT) * r_ref[...]).astype(BF)

    @pl.when(step == pl.num_programs(0) - 1)
    def _():
        quarter = share // 4
        for r in range(4):
            owner = me ^ r
            target = send_ref if r % 2 else keep_ref
            mate = r // 2
            for part in range(2):
                for other in range(2):
                    side = info[2] ^ other
                    group, spot = ((2 * (1 - mate), other), (3 - 2 * other, mate))[part]
                    to = slice(spot * quarter, (spot + 1) * quarter)
                    shift = part * half + side * quarter
                    at = pl.ds(pl.multiple_of(owner * share + shift, 16), quarter)
                    target[group, to, :width] = acc_o[at, :].astype(BF)
                    target[group, to, width:base] = acc_i[at, :].astype(BF)
                    at = pl.ds(pl.multiple_of(owner * (3 * half) + shift, 16), quarter)
                    target[group, to, base : base + width] = acc_d[at, :].astype(BF)
                    at = pl.ds(pl.multiple_of(owner * (3 * half) + share + side * quarter, 16), quarter)
                    fold = slice(part * width // 2, (part + 1) * width // 2)
                    target[group, to, base + width :] = acc_d[at, fold].astype(BF)


def feed_call(info, x, mixed, inverse, cot, gain, pieces):
    rows, width = x.shape
    tile = rows // 4
    share = width // 4
    packed = pieces[0].shape[2]
    whole = lambda i, s: (0, 0)
    cube = lambda i, s: (0, 0, 0)
    by_row = lambda i, s: (i, 0)
    block = pl.BlockSpec((tile, width), by_row)
    return pl.pallas_call(
        functools.partial(feed_kernel, tile=tile, share=share),
        grid_spec=pltpu.PrefetchScalarGridSpec(
            num_scalar_prefetch=1,
            grid=(rows // tile,),
            in_specs=[block, block, block, block, pl.BlockSpec((2, width), whole)]
            + [pl.BlockSpec(piece.shape, lambda i, s, n=piece.ndim: (0,) * n) for piece in pieces],
            out_specs=[pl.BlockSpec((tile, width), whole)] * 4
            + [block, block]
            + [pl.BlockSpec((4, share // 2, packed), cube)] * 2,
            scratch_shapes=[
                pltpu.VMEM((width, width), BF),
                pltpu.VMEM((width, 2 * FF), BF),
                pltpu.VMEM((FF, width), BF),
                pltpu.VMEM((width, width), F32),
                pltpu.VMEM((width, 2 * FF), F32),
                pltpu.VMEM((FF, width), F32),
            ],
        ),
        out_shape=[jax.ShapeDtypeStruct((tile, width), BF)] * 4
        + [
            jax.ShapeDtypeStruct((rows, width), F32),
            jax.ShapeDtypeStruct((rows, width), BF),
        ]
        + [jax.ShapeDtypeStruct((4, share // 2, packed), BF)] * 2,
        compiler_params=pltpu.CompilerParams(vmem_limit_bytes=VMEM_BYTES),
        cost_estimate=cost(6 * rows * width * (width + 3 * FF), 130e6),
        name="feed",
    )(info, x, mixed, inverse, cot, gain, *pieces)


def back_kernel(info, qkv_ref, o_ref, do_ref, p_ref, cos_ref, sin_ref, ht_ref, *rest, tile):
    keep_ref, send_ref, joined_ref = rest[-3:]
    rows = qkv_ref.shape[0]
    low = lax.broadcasted_iota(jnp.int32, (1, LANES), 1) < HDIM
    zero = jnp.zeros((), BF)
    keys = qkv_ref[:, LANES : 2 * LANES]
    values = qkv_ref[:, 2 * LANES :]
    key_heads = (jnp.where(low, keys, zero), jnp.where(low, zero, keys))
    key_grads = [None, None]
    value_grads = [None, None]
    query_grads = []
    for part in range(rows // tile):
        at = pl.ds(part * tile, tile)
        queries = qkv_ref[at, :LANES]
        grads = do_ref[at, :]
        wide = grads.astype(F32)
        inner = wide * o_ref[at, :].astype(F32)
        grad_heads = (jnp.where(low, grads, zero), jnp.where(low, zero, grads))
        queries_t = queries.astype(F32).T.astype(BF)
        grads_t = wide.T.astype(BF)
        query_grad = None
        for head in range(2):
            mine = low if head == 0 else jnp.logical_not(low)
            lanes = slice(head * HDIM, (head + 1) * HDIM)
            row_inner = jnp.sum(jnp.where(mine, inner, 0.0), axis=-1, keepdims=True)
            term_grad = dot(grad_heads[head], values, NT)
            terms = p_ref[head, at, :]
            score_grad = (terms.astype(F32) * (term_grad - row_inner)).astype(BF)
            partial = dot(score_grad, key_heads[head])
            query_grad = partial if query_grad is None else query_grad + partial
            for grad_list, left, right in (
                (key_grads, queries_t, score_grad),
                (value_grads, grads_t, terms),
            ):
                value = dot(left[lanes], right)
                grad_list[head] = value if grad_list[head] is None else grad_list[head] + value
        query_grads.append(query_grad)
    cosine = cos_ref[...]
    sine = sin_ref[...]
    query_grad = jnp.concatenate(query_grads, axis=0) * (HDIM**-0.5)
    key_grad = jnp.concatenate(key_grads, axis=0).T
    value_grad = jnp.concatenate(value_grads, axis=0).T
    joined = jnp.concatenate(
        [
            (query_grad * cosine - swap_halves(query_grad) * sine).astype(BF),
            (key_grad * cosine - swap_halves(key_grad) * sine).astype(BF),
            value_grad.astype(BF),
        ],
        axis=1,
    )
    joined_ref[...] = joined
    weight_grad = dot(ht_ref[...], joined).astype(BF)
    share = weight_grad.shape[0] // 4
    me = info[0]
    for owner in range(4):
        rel = me ^ owner
        value = weight_grad[owner * share : (owner + 1) * share, :]
        for target, odd in ((keep_ref, 0), (send_ref, 1)):

            @pl.when(rel % 2 == odd)
            def _():
                for kind in range(3):
                    target[rel // 2, kind] = value[:, kind * LANES : (kind + 1) * LANES]


def back_call(info, qkv, mixed, grads, terms, cosine, sine, hidden_t, start, count, slot, slots, buffers, tile=512):
    rows, width = mixed.shape
    whole = lambda p, s: (0, 0)
    block = pl.BlockSpec((rows, LANES), lambda p, s: (0, start + p))
    wide = pl.BlockSpec((rows, 3 * LANES), lambda p, s: (0, start + p))
    table = pl.BlockSpec((rows, LANES), whole)
    operands = [qkv, mixed, grads, terms, cosine, sine, hidden_t]
    share = width // 4
    piece = pl.BlockSpec((2, 3, share, LANES), lambda p, s: (0, 0, 0, slot + p))
    chunk = jax.ShapeDtypeStruct((2, 3, share, LANES * slots), BF)
    aliases = {}
    for k, buffer in enumerate(buffers):
        aliases[1 + len(operands)] = 3 - len(buffers) + k
        operands.append(buffer)
    return pl.pallas_call(
        functools.partial(back_kernel, tile=tile),
        grid_spec=pltpu.PrefetchScalarGridSpec(
            num_scalar_prefetch=1,
            grid=(count,),
            in_specs=[
                wide,
                block,
                block,
                pl.BlockSpec((2, rows, rows), lambda p, s: (start + p, 0, 0)),
                table,
                table,
                pl.BlockSpec((width, rows), whole),
            ]
            + [pl.BlockSpec(memory_space=pl.ANY)] * len(buffers),
            out_specs=[piece, piece, wide],
        ),
        out_shape=[chunk, chunk, jax.ShapeDtypeStruct((rows, 3 * width), BF)],
        input_output_aliases=aliases,
        compiler_params=pltpu.CompilerParams(vmem_limit_bytes=VMEM_BYTES),
        cost_estimate=cost(20 * rows * rows * LANES * count, 36e6 * count),
        name="back",
    )(info, *operands)


def finish_kernel(info, joined_ref, w_ref, x_ref, dmid_ref, gain_ref, dx0, dx1, dx2, dx3):
    normed, inverse = centre_scale(x_ref[...].astype(F32))
    hidden_grad = dot(joined_ref[...], w_ref[...], NT)
    back = norm_back(hidden_grad, normed, inverse, gain_ref[0:1, :])
    result = (dmid_ref[...] + back).astype(BF)
    for r, dx_ref in enumerate((dx0, dx1, dx2, dx3)):

        @pl.when(info[0] ^ pl.program_id(0) == r)
        def _():
            dx_ref[...] = result


def finish_call(info, joined, weight, x, dmid, gain):
    rows, width = x.shape
    tile = rows // 4
    wide = joined.shape[1]
    by_row = lambda i, s: (i, 0)
    whole = lambda i, s: (0, 0)
    return pl.pallas_call(
        finish_kernel,
        grid_spec=pltpu.PrefetchScalarGridSpec(
            num_scalar_prefetch=1,
            grid=(4,),
            in_specs=[
                pl.BlockSpec((tile, wide), by_row),
                pl.BlockSpec((width, wide), whole),
                pl.BlockSpec((tile, width), by_row),
                pl.BlockSpec((tile, width), by_row),
                pl.BlockSpec((2, width), whole),
            ],
            out_specs=[pl.BlockSpec((tile, width), whole)] * 4,
        ),
        out_shape=[jax.ShapeDtypeStruct((tile, width), BF)] * 4,
        compiler_params=pltpu.CompilerParams(vmem_limit_bytes=VMEM_BYTES),
        cost_estimate=cost(2 * rows * width * wide, 24e6),
        name="finish",
    )(info, joined, weight, x, dmid, gain)


def restore_kernel(info, p0, p1, p2, p3, out_ref):
    for r, piece in enumerate((p0, p1, p2, p3)):
        out_ref[info[0] ^ r] = piece[...].astype(out_ref.dtype)


def restore_call(info, pieces, kind):
    rows, width = pieces[0].shape
    return pl.pallas_call(
        restore_kernel,
        grid_spec=pltpu.PrefetchScalarGridSpec(
            num_scalar_prefetch=1,
            grid=(1,),
            in_specs=[pl.BlockSpec((rows, width), lambda i, s: (0, 0))] * 4,
            out_specs=pl.BlockSpec((4, rows, width), lambda i, s: (0, 0, 0)),
        ),
        out_shape=jax.ShapeDtypeStruct((4, rows, width), kind),
        compiler_params=pltpu.CompilerParams(vmem_limit_bytes=VMEM_BYTES),
        cost_estimate=cost(0, 12e6),
        name="restore",
    )(info, *pieces)


def adam_update(master, gradient, moment_one, moment_two, step_rate, decay_rate):
    first_new = adam_beta * moment_one + (1.0 - adam_beta) * gradient
    second_new = adam_beta * moment_two + (1.0 - adam_beta) * gradient * gradient
    correction = 1.0 - adam_beta**STEP
    direction = first_new / correction / (jnp.sqrt(second_new / correction) + adam_eps)
    renewed = master - step_rate * (direction + decay_rate * master)
    return (renewed, first_new, second_new)


def inward_kernel(grad_ref, master_ref, one_ref, two_ref, *rest):
    renewed_ref, first_ref, second_ref, product_ref = rest[-4:]
    grad = grad_ref[0].astype(F32)
    master = master_ref[...]
    renewed_ref[...], first_ref[...], second_ref[...] = adam_update(
        master, grad, one_ref[...], two_ref[...], rates[0], weight_decay
    )
    product = grad * master.astype(BF).astype(F32)

    @pl.when(pl.program_id(0) == 0)
    def _():
        product_ref[...] = jnp.zeros_like(product_ref)

    for start in range(0, product.shape[1], LANES):
        product_ref[...] += product[:, start : start + LANES]


def inward_call(grad, master, one, two):
    rows, wide = master.shape
    columns = grad.shape[2]
    block = pl.BlockSpec((rows, columns), lambda k: (0, k))
    array = jax.ShapeDtypeStruct((rows, wide), F32)
    return pl.pallas_call(
        inward_kernel,
        grid=(3,),
        in_specs=[pl.BlockSpec((1, rows, columns), lambda k: (k, 0, 0)), block, block, block],
        out_specs=[block, block, block, pl.BlockSpec((rows, LANES), lambda k: (0, 0))],
        out_shape=[array, array, array, jax.ShapeDtypeStruct((rows, LANES), F32)],
        compiler_params=pltpu.CompilerParams(vmem_limit_bytes=VMEM_BYTES),
        cost_estimate=cost(0, 18e6),
        name="inward",
    )(grad, master, one, two)


def tables(seq_total):
    lane = jnp.arange(LANES, dtype=jnp.int32)
    exponent = (lane % (HDIM // 2)).astype(F32) * (2.0 / HDIM)
    inverse = jnp.power(jnp.float32(rope_base), -exponent)
    angles = jnp.arange(seq_total, dtype=F32)[:, None] * inverse[None, :]
    sign = jnp.where(lane % HDIM < HDIM // 2, -1.0, 1.0).astype(F32)
    return jnp.cos(angles), jnp.sin(angles) * sign[None, :]


CORE = [(0, 1), (1, 0), (2, 3), (3, 2)]
CROSS = [(0, 2), (1, 3), (2, 0), (3, 1)]
tie = lax.optimization_barrier


def over_core(array):
    return lax.ppermute(array, "fsdp", CORE)


def over_cross(array):
    return lax.ppermute(array, "fsdp", CROSS)


def over_side(array):
    return lax.ppermute(array, "dp", [(k, k ^ 1) for k in range(lax.axis_size("dp"))])


def along_line(array, groups=None):
    return lax.all_to_all(array, "dp", 0, 0, axis_index_groups=groups)


def add_low(left, right):
    return (left.astype(F32) + right.astype(F32)).astype(BF)


def sum_low(array):
    return jnp.sum(array.astype(F32), axis=0).astype(BF)


def pick_half(array, index, axis=0):
    return lax.dynamic_index_in_dim(array, index, axis, keepdims=False)


def local(
    tokens, cotangent, lengths,
    inward_weight, outward_weight, expand_weight, shrink_weight, gain_weight,
    inward_first, outward_first, expand_first, shrink_first, gain_first,
    inward_second, outward_second, expand_second, shrink_second, gain_second,
):
    micro_count, group_size, local_len, width = tokens.shape
    fsdp = lax.axis_size("fsdp")
    lines = lax.axis_size("dp")
    assert fsdp == 4 and micro_count * group_size == fsdp and lines % 2 == 0
    seq_total = local_len * fsdp
    share, wide = inward_weight.shape
    half = share // 2
    me = lax.axis_index("fsdp").astype(jnp.int32)
    side = (lax.axis_index("dp") % 2).astype(jnp.int32)
    info = jnp.stack([me, pick_half(lengths.reshape(fsdp), me), side])
    columns = [[k for k in range(lines) if k % 2 == odd] for odd in range(2)]

    def to_sequence(array):
        array = array.reshape(fsdp, local_len, width)
        return lax.all_to_all(array, "fsdp", 0, 0).reshape(seq_total, width)

    def with_gains(weight, gains):
        gains = jnp.pad(gains.astype(BF)[:, None, :], ((0, 0), (0, 7), (0, wide - share)))
        return jnp.concatenate([weight.astype(BF), gains], axis=1)

    inward_halves = inward_weight.reshape(2, half, wide)
    leaving = with_gains(pick_half(inward_halves, side)[None], pick_half(gain_weight, side)[None])[0]
    far_one = over_cross(leaving)

    (inward_halves, outward, leaving) = tie((inward_halves, outward_weight, leaving))
    own = with_gains(inward_halves, gain_weight)
    near = over_core(own)
    tokens, own = tie((tokens, own))
    x = to_sequence(tokens)
    shrink_low = shrink_weight.astype(BF)
    folded = jnp.concatenate([shrink_low[share:, : width // 2], shrink_low[share:, width // 2 :]], axis=0)
    packed = jnp.concatenate(
        [outward.astype(BF), expand_weight.astype(BF), shrink_low[:share], folded], axis=1
    ).reshape(2, half, -1)
    cosine, sine = tables(seq_total)
    leaving = pick_half(packed, side)
    far_one, cosine, sine, info, packed, leaving = tie((far_one, cosine, sine, info, packed, leaving))
    far_two = over_side(far_one)
    inward_pieces = (own, near, far_one, far_two, over_core(far_one), over_core(far_two))

    leaving, x = tie((leaving, x))
    other_far_one = over_cross(leaving)
    other_near = over_core(packed)

    hidden_t, qkv, weight, gain = qkv_call(info, x, cosine, sine, inward_pieces)
    cotangent, qkv = tie((cotangent, qkv))
    cot = to_sequence(cotangent)
    buffers = attend_call(info, qkv, 0, 2, ())
    other_far_one, buffers = tie((other_far_one, buffers))
    other_far_two = over_side(other_far_one)
    mixed, inverse, terms = attend_call(info, qkv, 2, 4, buffers)
    mixed, other_far_two = tie((mixed, other_far_two))
    other_pieces = (
        packed, other_near, other_far_one, other_far_two, over_core(other_far_one), over_core(other_far_two)
    )
    *out, middle_grad, grads, keep, send = feed_call(info, x, mixed, inverse, cot, gain, other_pieces)

    def back(start, count, slot, slots, buffers):
        return back_call(
            info, qkv, mixed, grads, terms, cosine, sine, hidden_t, start, count, slot, slots, buffers
        )

    quarter = half // 2
    level = lines // 2
    line_at = lax.axis_index("dp") // 2

    def over_line(array, gap):
        return lax.ppermute(array, "dp", [(k, k ^ (2 * gap)) for k in range(lines)])

    def halve(array, gap):
        array = array.reshape((array.shape[0] // 2, 2) + array.shape[1:])
        bit = (line_at // gap) % 2
        came = over_line(pick_half(array, 1 - bit, 1), gap)
        return pick_half(array, bit, 1), came

    def in_order(mine, other, gap):
        bit = (line_at // gap) % 2
        pair = jnp.stack([jnp.where(bit == 0, mine, other), jnp.where(bit == 0, other, mine)], axis=1)
        return pair.reshape((-1,) + mine.shape[1:])

    def add(*parts):
        total = parts[0].astype(F32)
        for part in parts[1:]:
            total = total + part.astype(F32)
        return total.astype(BF)

    came = over_core(send)
    keep_x, send_x, joined = back(0, 1, 0, 3, ())
    leave_y = add(keep[0], came[0])
    leave_x = add(keep[1], came[1])
    leave_y, leave_x, joined = tie((leave_y, leave_x, joined))
    first_y = over_cross(leave_y)
    second_x = over_side(leave_x)
    keep_x, send_x, joined = back(1, 2, 1, 3, (keep_x, send_x, joined))
    came_x = over_core(send_x)
    leave_x = add(keep[2, quarter:], came[2, quarter:], first_y[quarter:])
    leave_y = add(keep[3, quarter:], came[3, quarter:], second_x[quarter:])
    leave_x, leave_y, joined = tie((leave_x, leave_y, joined))
    first_x = over_side(leave_x)
    second_y = over_cross(leave_y)
    keep_z, send_z, joined = back(3, 1, 0, 3, (joined,))
    first = add(keep[2, :quarter], came[2, :quarter], first_y[:quarter], first_x)
    second = add(keep[3, :quarter], came[3, :quarter], second_x[:quarter], second_y)
    both = jnp.concatenate([first, second], axis=0).reshape(level, half // level, -1)
    leave_y = add(keep_x[1], came_x[1])
    both, leave_y, joined = tie((both, leave_y, joined))
    gap = 1
    far_x = over_cross(leave_y)
    stay, moved = halve(both, gap)
    keep_z, send_z, joined = back(4, 1, 1, 3, (keep_z, send_z, joined))
    while gap * 2 < level:
        both = add(stay, moved)
        gap = gap * 2
        stay, moved = halve(both, gap)
    out, stay, joined = tie((out, stay, joined))
    near_out = over_core(out[1])
    turned_out = over_core(out[3])
    far_out = over_cross(out[2])
    keep_z, send_z, joined = back(5, 1, 2, 3, (keep_z, send_z, joined))

    came_z = over_core(send_z)
    both = add(stay, moved)
    both, keep_z, near_out, turned_out, far_out = tie((both, keep_z, near_out, turned_out, far_out))
    moved = over_line(both, gap)
    leave_y = add(keep_z[1], came_z[1])
    leave_y, joined = tie((leave_y, joined))
    far_z = over_cross(leave_y)
    input_low = finish_call(info, joined, weight, x, middle_grad, gain)
    input_low, moved, far_z, turned_out = tie((input_low, moved, far_z, turned_out))
    chunk = jnp.concatenate([add(keep_x[0], came_x[0], far_x), add(keep_z[0], came_z[0], far_z)], axis=2)
    chunk_shape = chunk.shape
    by_line = (lines, 3 * share // lines, chunk_shape[2])
    chunk = along_line(chunk.reshape(by_line))
    both = in_order(both, moved, gap)
    near_low = over_core(input_low[1])
    turned_low = over_core(input_low[3])
    far_low = over_cross(input_low[2])
    diagonal_out = over_cross(turned_out)
    while gap > 2:
        gap = gap // 2
        both = in_order(both, over_line(both, gap), gap)
    moved = over_line(both, 1)
    moved, chunk, near_low, turned_low, far_low, diagonal_out = tie(
        (moved, chunk, near_low, turned_low, far_low, diagonal_out)
    )
    both = in_order(both, moved, 1)
    other = over_side(both)
    diagonal_low = over_cross(turned_low)
    chunk = sum_low(chunk)
    chunk, info_in = tie((chunk, info))
    spread = along_line(jnp.broadcast_to(chunk[None], by_line)).reshape(chunk_shape)
    block_out = restore_call(info_in, (out[0], near_out, far_out, diagonal_out), BF).reshape(tokens.shape)
    pieces = (input_low[0], near_low, far_low, diagonal_low)
    input_grad = restore_call(info_in, pieces, F32).reshape(tokens.shape)

    both = both.reshape(2, quarter, -1)
    other = other.reshape(2, quarter, -1)
    lower = jnp.where(side == 0, both, other)
    upper = jnp.where(side == 0, other, both)
    grad_m = jnp.concatenate([lower[0], upper[0], lower[1], upper[1]], axis=0).astype(F32)
    grad_o = grad_m[:, :width]
    grad_i = grad_m[:, width : width + 2 * FF]
    rest = grad_m[:, width + 2 * FF :]
    grad_d = jnp.concatenate(
        [rest[:, :width], jnp.concatenate([rest[:half, width:], rest[half:, width:]], axis=1)], axis=0
    )
    *inward_new, product = inward_call(spread, inward_weight, inward_first, inward_second)
    own_gain = gain_weight.astype(BF).astype(F32)
    gain_grad = jnp.stack(
        [
            jnp.sum(product, axis=1),
            jnp.sum(grad_i * expand_weight.astype(BF).astype(F32), axis=1),
        ]
    ) / own_gain

    results = [block_out, input_grad]
    results += inward_new
    results += adam_update(outward_weight, grad_o, outward_first, outward_second, rates[1], weight_decay)
    results += adam_update(expand_weight, grad_i, expand_first, expand_second, rates[2], weight_decay)
    results += adam_update(shrink_weight, grad_d, shrink_first, shrink_second, rates[3], weight_decay)
    results += adam_update(gain_weight, gain_grad, gain_first, gain_second, rates[4], 0.0)
    return tuple(results)


def solution(mesh):
    split = P(None, "dp", "fsdp", None)
    rows = P("fsdp", None)
    columns = P(None, "fsdp")
    kinds = (rows, rows, rows, rows, columns)
    in_specs = (split, split, P(None, "dp")) + kinds * 3
    out_specs = (split, split) + (rows,) * 12 + (columns,) * 3
    return jax.shard_map(local, mesh=mesh, in_specs=in_specs, out_specs=out_specs, check_vma=False)
```

```python
import functools

import jax
import jax.numpy as jnp
from jax import lax
from jax.experimental import pallas as pl
from jax.experimental.pallas import tpu as pltpu
from jax.sharding import PartitionSpec as P

FF = 1152
HEADS = 12
HDIM = 64
STEP = 10

rope_base = 160000.0
norm_eps = 1e-05
adam_beta = 0.5
adam_eps = 1e-08
weight_decay = 0.01
rates = (0.07, 2.0, 0.07, 0.06, 0.2)
masked_score = -1e30

BF = jnp.bfloat16
F32 = jnp.float32
NN = (((1,), (0,)), ((), ()))
NT = (((1,), (1,)), ((), ()))
TN = (((0,), (0,)), ((), ()))
VMEM_BYTES = 58 << 20
LANES = 128
PAIRS = HEADS * HDIM // LANES


def cost(flops, size):
    return pl.CostEstimate(flops=int(flops), bytes_accessed=int(size), transcendentals=0)


def dot(left, right, dims=NN):
    return lax.dot_general(left, right, dims, preferred_element_type=F32)


def swap_halves(values):
    lane = lax.broadcasted_iota(jnp.int32, (1, LANES), 1)
    former = lax.rem(lane, HDIM) < HDIM // 2
    ahead = pltpu.roll(values, LANES - HDIM // 2, 1)
    behind = pltpu.roll(values, HDIM // 2, 1)
    return jnp.where(former, ahead, behind)


def centre_scale(values):
    center = values - jnp.mean(values, axis=-1, keepdims=True)
    spread = jnp.mean(center * center, axis=-1, keepdims=True)
    inverse = lax.rsqrt(spread + norm_eps)
    return center * inverse, inverse


def norm_back(grad, normed, inverse, gain):
    scaled = grad * gain
    mean_one = jnp.mean(scaled, axis=-1, keepdims=True)
    mean_two = jnp.mean(scaled * normed, axis=-1, keepdims=True)
    return inverse * (scaled - mean_one - normed * mean_two)


def place(scratch, pieces, info, rows):
    half = rows // 2
    for r, piece in enumerate(pieces):
        owner = info[0] ^ r
        for part, ref in enumerate(piece):
            side = part if r < 2 else info[2] ^ part
            at = pl.ds(pl.multiple_of(owner * rows + side * half, 32), half)
            for pair in range(PAIRS):
                for kind in range(3):
                    source = (kind * PAIRS + pair) * LANES
                    target = (pair * 3 + kind) * LANES
                    scratch[at, target : target + LANES] = ref[:half, source : source + LANES]


def pick(index, choices):
    value = choices[-1]
    for k in range(len(choices) - 2, -1, -1):
        value = jnp.where(index == k, choices[k], value)
    return value


def qkv_kernel(
    info, x_ref, cos_ref, sin_ref, w0, w1, w2a, w2b, w3a, w3b, ht_ref, qkv_ref, w_ref, gain_ref, *, share
):
    pieces = ((w0.at[0], w0.at[1]), (w1.at[0], w1.at[1]), (w2a, w2b), (w3a, w3b))

    @pl.when(pl.program_id(0) == 0)
    def _():
        place(w_ref, pieces, info, share)
        half = share // 2
        for row in range(2):
            found = []
            for r, piece in enumerate(pieces):
                one = piece[0][half : half + 1, :share].astype(F32)
                two = piece[1][half : half + 1, :share].astype(F32)
                swap = row if r < 2 else info[2] ^ row
                found.append(jnp.where(swap == 0, one, two))
            ordered = [pick(info[0] ^ owner, found) for owner in range(4)]
            gain_ref[row : row + 1, :] = jnp.concatenate(ordered, axis=1)

    normed, unused = centre_scale(x_ref[...].astype(F32))
    low = (normed * gain_ref[0:1, :]).astype(BF)
    ht_ref[...] = low.T
    cosine = cos_ref[...]
    sine = sin_ref[...]
    for pair in range(PAIRS):
        start = pair * 3 * LANES
        if pair % 2 == 0:
            joined = dot(low, w_ref[:, start : start + 6 * LANES])
        for kind in range(3):
            at = (pair % 2 * 3 + kind) * LANES
            block = joined[:, at : at + LANES]
            if kind < 2:
                block = block * cosine + swap_halves(block) * sine
            block = block.astype(BF)
            if kind == 0:
                block = block * jnp.asarray(HDIM**-0.5, BF)
            qkv_ref[:, start + kind * LANES : start + (kind + 1) * LANES] = block


def qkv_call(info, x, cosine, sine, pieces, tile=256):
    rows, width = x.shape
    wide = pieces[0].shape[2]
    whole = lambda i, s: (0, 0)
    by_row = lambda i, s: (i, 0)
    return pl.pallas_call(
        functools.partial(qkv_kernel, share=width // 4),
        grid_spec=pltpu.PrefetchScalarGridSpec(
            num_scalar_prefetch=1,
            grid=(rows // tile,),
            in_specs=[
                pl.BlockSpec((tile, width), by_row),
                pl.BlockSpec((tile, LANES), by_row),
                pl.BlockSpec((tile, LANES), by_row),
            ]
            + [pl.BlockSpec(piece.shape, lambda i, s, n=piece.ndim: (0,) * n) for piece in pieces],
            out_specs=[
                pl.BlockSpec((width, tile), lambda i, s: (0, i)),
                pl.BlockSpec((tile, wide), by_row),
                pl.BlockSpec((width, wide), whole),
                pl.BlockSpec((2, width), whole),
            ],
        ),
        out_shape=[
            jax.ShapeDtypeStruct((width, rows), BF),
            jax.ShapeDtypeStruct((rows, wide), BF),
            jax.ShapeDtypeStruct((width, wide), BF),
            jax.ShapeDtypeStruct((2, width), F32),
        ],
        compiler_params=pltpu.CompilerParams(vmem_limit_bytes=VMEM_BYTES),
        cost_estimate=cost(2 * rows * width * wide, 36e6),
        name="qkv",
    )(info, x, cosine, sine, *pieces)


def attend_kernel(info, qkv_ref, *rest, tile):
    o_ref, r_ref, p_ref = rest[-3:]
    rows = qkv_ref.shape[0]
    key_at = lax.broadcasted_iota(jnp.int32, (1, rows), 1)
    bias = jnp.where(key_at < info[1], 0.0, masked_score).astype(F32)
    keys = qkv_ref[:, LANES : 2 * LANES]
    values = qkv_ref[:, 2 * LANES :]
    low = lax.broadcasted_iota(jnp.int32, (1, LANES), 1) < HDIM
    one = jnp.ones((), BF)
    zero = jnp.zeros((), BF)
    sides = (jnp.where(low, values, one), jnp.where(low, one, values))
    for step in range(rows // tile):
        at = pl.ds(step * tile, tile)
        queries = qkv_ref[at, :LANES]
        heads = (jnp.where(low, queries, zero), jnp.where(low, zero, queries))
        outs = []
        for head in range(2):
            scores = dot(heads[head], keys, NT) + bias
            peak = jnp.max(scores, axis=-1, keepdims=True)
            terms = jnp.exp(scores - peak).astype(BF)
            p_ref[head, at, :] = terms
            outs.append(dot(terms, sides[head]))
        mixed = jnp.where(low, outs[0], outs[1])
        total = pltpu.roll(jnp.where(low, outs[1], outs[0]), HDIM, 1)
        inverse = 1.0 / total
        o_ref[at, :] = (mixed * inverse).astype(BF)
        r_ref[at, :] = inverse


def attend_call(info, qkv, start, count, buffers, tile=512):
    rows = qkv.shape[0]
    width = qkv.shape[1] // 3
    block = pl.BlockSpec((rows, LANES), lambda p, s: (0, start + p))
    buffers = tuple(buffers)
    return pl.pallas_call(
        functools.partial(attend_kernel, tile=tile),
        grid_spec=pltpu.PrefetchScalarGridSpec(
            num_scalar_prefetch=1,
            grid=(count,),
            in_specs=[pl.BlockSpec((rows, 3 * LANES), lambda p, s: (0, start + p))]
            + [pl.BlockSpec(memory_space=pl.ANY)] * len(buffers),
            out_specs=[
                block,
                block,
                pl.BlockSpec((2, rows, rows), lambda p, s: (start + p, 0, 0)),
            ],
        ),
        out_shape=[
            jax.ShapeDtypeStruct((rows, width), BF),
            jax.ShapeDtypeStruct((rows, width), F32),
            jax.ShapeDtypeStruct((HEADS, rows, rows), BF),
        ],
        input_output_aliases={2 + k: k for k in range(len(buffers))},
        compiler_params=pltpu.CompilerParams(vmem_limit_bytes=VMEM_BYTES),
        cost_estimate=cost(16 * rows * rows * LANES * count, 17e6 * count),
        name="attend",
    )(info, qkv, *buffers)


def feed_kernel(
    info, x_ref, o_ref, r_ref, cot_ref, gain_ref, m0, m1, m2a, m2b, m3a, m3b,
    out0, out1, out2, out3, dmid_ref, do_ref, keep_ref, send_ref,
    wo, wi, wd, acc_o, acc_i, acc_d, *, tile, share,
):
    step = pl.program_id(0)
    me = info[0]
    width = x_ref.shape[1]
    inner = wi.shape[1]
    base = width + inner
    half = share // 2

    @pl.when(step == 0)
    def _():
        pieces = ((m0.at[0], m0.at[1]), (m1.at[0], m1.at[1]), (m2a, m2b), (m3a, m3b))
        for r, piece in enumerate(pieces):
            owner = me ^ r
            for part, ref in enumerate(piece):
                side = part if r < 2 else info[2] ^ part
                at = pl.ds(pl.multiple_of(owner * share + side * half, 32), half)
                wo[at, :] = ref[:, :width]
                wi[at, :] = ref[:, width:base]
                down = owner * (3 * half)
                at = pl.ds(pl.multiple_of(down + side * half, 32), half)
                wd[at, :] = ref[:, base : base + width]
                at = pl.ds(pl.multiple_of(down + 2 * half, 32), half)

                @pl.when(side == 0)
                def _():
                    wd[at, : width // 2] = ref[:, base + width :]

                @pl.when(side == 1)
                def _():
                    wd[at, width // 2 :] = ref[:, base + width :]

        acc_o[...] = jnp.zeros_like(acc_o)
        acc_i[...] = jnp.zeros_like(acc_i)
        acc_d[...] = jnp.zeros_like(acc_d)

    gain = gain_ref[1:2, :]
    mixed = o_ref[...]
    middle = x_ref[...].astype(F32) + dot(mixed, wo[...])
    normed, inverse = centre_scale(middle)
    hidden = (normed * gain).astype(BF)
    gate = dot(hidden, wi[:, :FF])
    upward = dot(hidden, wi[:, FF:])
    cdf = 0.5 * (1.0 + lax.erf(gate * 0.7071067811865476))
    gelu = gate * cdf
    slope = cdf + gate * (jnp.exp(-0.5 * gate * gate) * 0.3989422804014327)
    state = (gelu * upward).astype(BF)
    row_at = step * tile + lax.broadcasted_iota(jnp.int32, (tile, 1), 0)
    live = row_at < info[1]
    result = jnp.where(live, middle + dot(state, wd[...]), 0.0).astype(BF)
    for r, out_ref in enumerate((out0, out1, out2, out3)):

        @pl.when(me ^ step == r)
        def _():
            out_ref[...] = result

    branch = jnp.where(live, cot_ref[...].astype(F32), 0.0)
    branch_low = branch.astype(BF)
    acc_d[...] += dot(state, branch_low, TN)
    state_grad = dot(branch_low, wd[...], NT)
    gate_grad = (state_grad * upward * slope).astype(BF)
    up_grad = (state_grad * gelu).astype(BF)
    acc_i[:, :FF] += dot(hidden, gate_grad, TN)
    acc_i[:, FF:] += dot(hidden, up_grad, TN)
    hidden_grad = dot(gate_grad, wi[:, :FF], NT) + dot(up_grad, wi[:, FF:], NT)
    mixer = (branch + norm_back(hidden_grad, normed, inverse, gain)).astype(BF)
    dmid_ref[...] = mixer
    acc_o[...] += dot(mixed, mixer, TN)
    do_ref[...] = (dot(mixer, wo[...], NT) * r_ref[...]).astype(BF)

    @pl.when(step == pl.num_programs(0) - 1)
    def _():
        quarter = share // 4
        for r in range(4):
            owner = me ^ r
            target = send_ref if r % 2 else keep_ref
            mate = r // 2
            for part in range(2):
                for other in range(2):
                    side = info[2] ^ other
                    group, spot = ((2 * (1 - mate), other), (3 - 2 * other, mate))[part]
                    to = slice(spot * quarter, (spot + 1) * quarter)
                    shift = part * half + side * quarter
                    at = pl.ds(pl.multiple_of(owner * share + shift, 16), quarter)
                    target[group, to, :width] = acc_o[at, :].astype(BF)
                    target[group, to, width:base] = acc_i[at, :].astype(BF)
                    at = pl.ds(pl.multiple_of(owner * (3 * half) + shift, 16), quarter)
                    target[group, to, base : base + width] = acc_d[at, :].astype(BF)
                    at = pl.ds(pl.multiple_of(owner * (3 * half) + share + side * quarter, 16), quarter)
                    fold = slice(part * width // 2, (part + 1) * width // 2)
                    target[group, to, base + width :] = acc_d[at, fold].astype(BF)


def feed_call(info, x, mixed, inverse, cot, gain, pieces):
    rows, width = x.shape
    tile = rows // 4
    share = width // 4
    packed = pieces[0].shape[2]
    whole = lambda i, s: (0, 0)
    cube = lambda i, s: (0, 0, 0)
    by_row = lambda i, s: (i, 0)
    block = pl.BlockSpec((tile, width), by_row)
    return pl.pallas_call(
        functools.partial(feed_kernel, tile=tile, share=share),
        grid_spec=pltpu.PrefetchScalarGridSpec(
            num_scalar_prefetch=1,
            grid=(rows // tile,),
            in_specs=[block, block, block, block, pl.BlockSpec((2, width), whole)]
            + [pl.BlockSpec(piece.shape, lambda i, s, n=piece.ndim: (0,) * n) for piece in pieces],
            out_specs=[pl.BlockSpec((tile, width), whole)] * 4
            + [block, block]
            + [pl.BlockSpec((4, share // 2, packed), cube)] * 2,
            scratch_shapes=[
                pltpu.VMEM((width, width), BF),
                pltpu.VMEM((width, 2 * FF), BF),
                pltpu.VMEM((FF, width), BF),
                pltpu.VMEM((width, width), F32),
                pltpu.VMEM((width, 2 * FF), F32),
                pltpu.VMEM((FF, width), F32),
            ],
        ),
        out_shape=[jax.ShapeDtypeStruct((tile, width), BF)] * 4
        + [jax.ShapeDtypeStruct((rows, width), BF)] * 2
        + [jax.ShapeDtypeStruct((4, share // 2, packed), BF)] * 2,
        compiler_params=pltpu.CompilerParams(vmem_limit_bytes=VMEM_BYTES),
        cost_estimate=cost(6 * rows * width * (width + 3 * FF), 130e6),
        name="feed",
    )(info, x, mixed, inverse, cot, gain, *pieces)


def back_kernel(info, qkv_ref, o_ref, do_ref, p_ref, cos_ref, sin_ref, ht_ref, *rest, tile):
    keep_ref, send_ref, joined_ref = rest[-3:]
    rows = qkv_ref.shape[0]
    low = lax.broadcasted_iota(jnp.int32, (1, LANES), 1) < HDIM
    zero = jnp.zeros((), BF)
    keys = qkv_ref[:, LANES : 2 * LANES]
    values = qkv_ref[:, 2 * LANES :]
    key_heads = (jnp.where(low, keys, zero), jnp.where(low, zero, keys))
    key_grads = [None, None]
    value_grads = [None, None]
    query_grads = []
    for part in range(rows // tile):
        at = pl.ds(part * tile, tile)
        queries = qkv_ref[at, :LANES]
        grads = do_ref[at, :]
        wide = grads.astype(F32)
        inner = wide * o_ref[at, :].astype(F32)
        grad_heads = (jnp.where(low, grads, zero), jnp.where(low, zero, grads))
        queries_t = queries.astype(F32).T.astype(BF)
        grads_t = wide.T.astype(BF)
        query_grad = None
        for head in range(2):
            mine = low if head == 0 else jnp.logical_not(low)
            lanes = slice(head * HDIM, (head + 1) * HDIM)
            row_inner = jnp.sum(jnp.where(mine, inner, 0.0), axis=-1, keepdims=True)
            term_grad = dot(grad_heads[head], values, NT)
            terms = p_ref[head, at, :]
            score_grad = (terms.astype(F32) * (term_grad - row_inner)).astype(BF)
            partial = dot(score_grad, key_heads[head])
            query_grad = partial if query_grad is None else query_grad + partial
            for grad_list, left, right in (
                (key_grads, queries_t, score_grad),
                (value_grads, grads_t, terms),
            ):
                value = dot(left[lanes], right)
                grad_list[head] = value if grad_list[head] is None else grad_list[head] + value
        query_grads.append(query_grad)
    cosine = cos_ref[...]
    sine = sin_ref[...]
    query_grad = jnp.concatenate(query_grads, axis=0) * (HDIM**-0.5)
    key_grad = jnp.concatenate(key_grads, axis=0).T
    value_grad = jnp.concatenate(value_grads, axis=0).T
    joined = jnp.concatenate(
        [
            (query_grad * cosine - swap_halves(query_grad) * sine).astype(BF),
            (key_grad * cosine - swap_halves(key_grad) * sine).astype(BF),
            value_grad.astype(BF),
        ],
        axis=1,
    )
    joined_ref[...] = joined
    weight_grad = dot(ht_ref[...], joined).astype(BF)
    share = weight_grad.shape[0] // 4
    me = info[0]
    for owner in range(4):
        rel = me ^ owner
        value = weight_grad[owner * share : (owner + 1) * share, :]
        for target, odd in ((keep_ref, 0), (send_ref, 1)):

            @pl.when(rel % 2 == odd)
            def _():
                for kind in range(3):
                    target[rel // 2, kind] = value[:, kind * LANES : (kind + 1) * LANES]


def back_call(info, qkv, mixed, grads, terms, cosine, sine, hidden_t, start, count, slot, slots, buffers, tile=512):
    rows, width = mixed.shape
    whole = lambda p, s: (0, 0)
    block = pl.BlockSpec((rows, LANES), lambda p, s: (0, start + p))
    wide = pl.BlockSpec((rows, 3 * LANES), lambda p, s: (0, start + p))
    table = pl.BlockSpec((rows, LANES), whole)
    operands = [qkv, mixed, grads, terms, cosine, sine, hidden_t]
    share = width // 4
    piece = pl.BlockSpec((2, 3, share, LANES), lambda p, s: (0, 0, 0, slot + p))
    chunk = jax.ShapeDtypeStruct((2, 3, share, LANES * slots), BF)
    aliases = {}
    for k, buffer in enumerate(buffers):
        aliases[1 + len(operands)] = 3 - len(buffers) + k
        operands.append(buffer)
    return pl.pallas_call(
        functools.partial(back_kernel, tile=tile),
        grid_spec=pltpu.PrefetchScalarGridSpec(
            num_scalar_prefetch=1,
            grid=(count,),
            in_specs=[
                wide,
                block,
                block,
                pl.BlockSpec((2, rows, rows), lambda p, s: (start + p, 0, 0)),
                table,
                table,
                pl.BlockSpec((width, rows), whole),
            ]
            + [pl.BlockSpec(memory_space=pl.ANY)] * len(buffers),
            out_specs=[piece, piece, wide],
        ),
        out_shape=[chunk, chunk, jax.ShapeDtypeStruct((rows, 3 * width), BF)],
        input_output_aliases=aliases,
        compiler_params=pltpu.CompilerParams(vmem_limit_bytes=VMEM_BYTES),
        cost_estimate=cost(20 * rows * rows * LANES * count, 36e6 * count),
        name="back",
    )(info, *operands)


def finish_kernel(info, joined_ref, w_ref, x_ref, dmid_ref, gain_ref, dx0, dx1, dx2, dx3):
    normed, inverse = centre_scale(x_ref[...].astype(F32))
    hidden_grad = dot(joined_ref[...], w_ref[...], NT)
    back = norm_back(hidden_grad, normed, inverse, gain_ref[0:1, :])
    result = (dmid_ref[...].astype(F32) + back).astype(BF)
    for r, dx_ref in enumerate((dx0, dx1, dx2, dx3)):

        @pl.when(info[0] ^ pl.program_id(0) == r)
        def _():
            dx_ref[...] = result


def finish_call(info, joined, weight, x, dmid, gain):
    rows, width = x.shape
    tile = rows // 4
    wide = joined.shape[1]
    by_row = lambda i, s: (i, 0)
    whole = lambda i, s: (0, 0)
    return pl.pallas_call(
        finish_kernel,
        grid_spec=pltpu.PrefetchScalarGridSpec(
            num_scalar_prefetch=1,
            grid=(4,),
            in_specs=[
                pl.BlockSpec((tile, wide), by_row),
                pl.BlockSpec((width, wide), whole),
                pl.BlockSpec((tile, width), by_row),
                pl.BlockSpec((tile, width), by_row),
                pl.BlockSpec((2, width), whole),
            ],
            out_specs=[pl.BlockSpec((tile, width), whole)] * 4,
        ),
        out_shape=[jax.ShapeDtypeStruct((tile, width), BF)] * 4,
        compiler_params=pltpu.CompilerParams(vmem_limit_bytes=VMEM_BYTES),
        cost_estimate=cost(2 * rows * width * wide, 24e6),
        name="finish",
    )(info, joined, weight, x, dmid, gain)


def restore_kernel(info, p0, p1, p2, p3, out_ref):
    for r, piece in enumerate((p0, p1, p2, p3)):
        out_ref[info[0] ^ r] = piece[...].astype(out_ref.dtype)


def restore_call(info, pieces, kind):
    rows, width = pieces[0].shape
    return pl.pallas_call(
        restore_kernel,
        grid_spec=pltpu.PrefetchScalarGridSpec(
            num_scalar_prefetch=1,
            grid=(1,),
            in_specs=[pl.BlockSpec((rows, width), lambda i, s: (0, 0))] * 4,
            out_specs=pl.BlockSpec((4, rows, width), lambda i, s: (0, 0, 0)),
        ),
        out_shape=jax.ShapeDtypeStruct((4, rows, width), kind),
        compiler_params=pltpu.CompilerParams(vmem_limit_bytes=VMEM_BYTES),
        cost_estimate=cost(0, 12e6),
        name="restore",
    )(info, *pieces)


def adam_update(master, gradient, moment_one, moment_two, step_rate, decay_rate):
    first_new = adam_beta * moment_one + (1.0 - adam_beta) * gradient
    second_new = adam_beta * moment_two + (1.0 - adam_beta) * gradient * gradient
    correction = 1.0 - adam_beta**STEP
    direction = first_new / correction / (jnp.sqrt(second_new / correction) + adam_eps)
    renewed = master - step_rate * (direction + decay_rate * master)
    return (renewed, first_new, second_new)


def inward_kernel(grad_ref, master_ref, one_ref, two_ref, *rest):
    renewed_ref, first_ref, second_ref, product_ref = rest[-4:]
    grad = grad_ref[0].astype(F32)
    master = master_ref[...]
    renewed_ref[...], first_ref[...], second_ref[...] = adam_update(
        master, grad, one_ref[...], two_ref[...], rates[0], weight_decay
    )
    product = grad * master.astype(BF).astype(F32)

    @pl.when(pl.program_id(0) == 0)
    def _():
        product_ref[...] = jnp.zeros_like(product_ref)

    for start in range(0, product.shape[1], LANES):
        product_ref[...] += product[:, start : start + LANES]


def inward_call(grad, master, one, two):
    rows, wide = master.shape
    columns = grad.shape[2]
    block = pl.BlockSpec((rows, columns), lambda k: (0, k))
    array = jax.ShapeDtypeStruct((rows, wide), F32)
    return pl.pallas_call(
        inward_kernel,
        grid=(3,),
        in_specs=[pl.BlockSpec((1, rows, columns), lambda k: (k, 0, 0)), block, block, block],
        out_specs=[block, block, block, pl.BlockSpec((rows, LANES), lambda k: (0, 0))],
        out_shape=[array, array, array, jax.ShapeDtypeStruct((rows, LANES), F32)],
        compiler_params=pltpu.CompilerParams(vmem_limit_bytes=VMEM_BYTES),
        cost_estimate=cost(0, 18e6),
        name="inward",
    )(grad, master, one, two)


def others_kernel(side, grad_ref, *refs, width, inner):
    masters = refs[:9]
    results = refs[-10:-1]
    product_ref = refs[-1]
    step = pl.program_id(0)
    base = width + inner

    def update(kind, grad):
        master, one, two = masters[3 * kind : 3 * kind + 3]
        values = adam_update(master[...], grad, one[...], two[...], rates[kind + 1], weight_decay)
        for ref, value in zip(results[3 * kind : 3 * kind + 3], values):
            ref[...] = value

    @pl.when(step < 2)
    def _():
        grad = grad_ref[step].astype(F32)
        update(0, grad[:, :width])
        update(1, grad[:, width:base])
        update(2, grad[:, base : base + width])
        product = grad[:, width:base] * masters[3][...].astype(BF).astype(F32)
        total = product[:, :LANES]
        for start in range(LANES, inner, LANES):
            total = total + product[:, start : start + LANES]
        product_ref[...] = total

    @pl.when(step == 2)
    def _():
        update(2, jnp.concatenate([grad_ref[k, :, base + width :].astype(F32) for k in range(2)], axis=1))


def others_call(side, grad, arrays, buffers):
    quarter = grad.shape[1]
    width = arrays[0].shape[1]
    inner = arrays[3].shape[1]
    short = lambda j, s: (2 * jnp.minimum(j, 1) + s[0], 0)
    full = lambda j, s: (2 * j + s[0], 0)
    blocks = []
    for array, place in zip(arrays, (short,) * 6 + (full,) * 3):
        blocks.append(pl.BlockSpec((quarter, array.shape[1]), place))
    sums = jax.ShapeDtypeStruct((arrays[0].shape[0], LANES), F32)
    return pl.pallas_call(
        functools.partial(others_kernel, width=width, inner=inner),
        grid_spec=pltpu.PrefetchScalarGridSpec(
            num_scalar_prefetch=1,
            grid=(3,),
            in_specs=[pl.BlockSpec(grad.shape, lambda j, s: (0, 0, 0))]
            + blocks
            + [pl.BlockSpec(memory_space=pl.ANY)] * len(buffers),
            out_specs=blocks + [pl.BlockSpec((quarter, LANES), short)],
        ),
        out_shape=[jax.ShapeDtypeStruct(array.shape, F32) for array in arrays] + [sums],
        input_output_aliases={11 + k: k for k in range(len(buffers))},
        compiler_params=pltpu.CompilerParams(vmem_limit_bytes=VMEM_BYTES),
        cost_estimate=cost(0, 14e6),
        name="others",
    )(side, grad, *arrays, *buffers)


def tables(seq_total):
    lane = jnp.arange(LANES, dtype=jnp.int32)
    exponent = (lane % (HDIM // 2)).astype(F32) * (2.0 / HDIM)
    inverse = jnp.power(jnp.float32(rope_base), -exponent)
    angles = jnp.arange(seq_total, dtype=F32)[:, None] * inverse[None, :]
    sign = jnp.where(lane % HDIM < HDIM // 2, -1.0, 1.0).astype(F32)
    return jnp.cos(angles), jnp.sin(angles) * sign[None, :]


CORE = [(0, 1), (1, 0), (2, 3), (3, 2)]
CROSS = [(0, 2), (1, 3), (2, 0), (3, 1)]
tie = lax.optimization_barrier


def over_core(array):
    return lax.ppermute(array, "fsdp", CORE)


def over_cross(array):
    return lax.ppermute(array, "fsdp", CROSS)


def over_side(array):
    return lax.ppermute(array, "dp", [(k, k ^ 1) for k in range(lax.axis_size("dp"))])


def along_line(array, groups=None):
    return lax.all_to_all(array, "dp", 0, 0, axis_index_groups=groups)


def add_low(left, right):
    return (left.astype(F32) + right.astype(F32)).astype(BF)


def sum_low(array):
    return jnp.sum(array.astype(F32), axis=0).astype(BF)


def pick_half(array, index, axis=0):
    return lax.dynamic_index_in_dim(array, index, axis, keepdims=False)


def local(
    tokens, cotangent, lengths,
    inward_weight, outward_weight, expand_weight, shrink_weight, gain_weight,
    inward_first, outward_first, expand_first, shrink_first, gain_first,
    inward_second, outward_second, expand_second, shrink_second, gain_second,
):
    micro_count, group_size, local_len, width = tokens.shape
    fsdp = lax.axis_size("fsdp")
    lines = lax.axis_size("dp")
    assert fsdp == 4 and micro_count * group_size == fsdp and lines % 2 == 0
    seq_total = local_len * fsdp
    share, wide = inward_weight.shape
    half = share // 2
    me = lax.axis_index("fsdp").astype(jnp.int32)
    side = (lax.axis_index("dp") % 2).astype(jnp.int32)
    info = jnp.stack([me, pick_half(lengths.reshape(fsdp), me), side])
    columns = [[k for k in range(lines) if k % 2 == odd] for odd in range(2)]

    def to_sequence(array):
        array = array.reshape(fsdp, local_len, width)
        return lax.all_to_all(array, "fsdp", 0, 0).reshape(seq_total, width)

    def with_gains(weight, gains):
        gains = jnp.pad(gains.astype(BF)[:, None, :], ((0, 0), (0, 7), (0, wide - share)))
        return jnp.concatenate([weight.astype(BF), gains], axis=1)

    inward_halves = inward_weight.reshape(2, half, wide)
    leaving = with_gains(pick_half(inward_halves, side)[None], pick_half(gain_weight, side)[None])[0]
    far_one = over_cross(leaving)

    (inward_halves, outward, leaving) = tie((inward_halves, outward_weight, leaving))
    own = with_gains(inward_halves, gain_weight)
    near = over_core(own)
    tokens, own = tie((tokens, own))
    x = to_sequence(tokens)
    shrink_low = shrink_weight.astype(BF)
    folded = jnp.concatenate([shrink_low[share:, : width // 2], shrink_low[share:, width // 2 :]], axis=0)
    packed = jnp.concatenate(
        [outward.astype(BF), expand_weight.astype(BF), shrink_low[:share], folded], axis=1
    ).reshape(2, half, -1)
    cosine, sine = tables(seq_total)
    leaving = pick_half(packed, side)
    far_one, cosine, sine, info, packed, leaving = tie((far_one, cosine, sine, info, packed, leaving))
    far_two = over_side(far_one)
    inward_pieces = (own, near, far_one, far_two, over_core(far_one), over_core(far_two))

    leaving, x = tie((leaving, x))
    other_far_one = over_cross(leaving)
    other_near = over_core(packed)

    hidden_t, qkv, weight, gain = qkv_call(info, x, cosine, sine, inward_pieces)
    cotangent, qkv = tie((cotangent, qkv))
    cot = to_sequence(cotangent)
    buffers = attend_call(info, qkv, 0, 2, ())
    other_far_one, buffers = tie((other_far_one, buffers))
    other_far_two = over_side(other_far_one)
    mixed, inverse, terms = attend_call(info, qkv, 2, 4, buffers)
    mixed, other_far_two = tie((mixed, other_far_two))
    other_pieces = (
        packed, other_near, other_far_one, other_far_two, over_core(other_far_one), over_core(other_far_two)
    )
    *out, middle_grad, grads, keep, send = feed_call(info, x, mixed, inverse, cot, gain, other_pieces)

    def back(start, count, slot, slots, buffers):
        return back_call(
            info, qkv, mixed, grads, terms, cosine, sine, hidden_t, start, count, slot, slots, buffers
        )

    quarter = half // 2
    level = lines // 2
    line_at = lax.axis_index("dp") // 2

    def over_line(array, gap):
        return lax.ppermute(array, "dp", [(k, k ^ (2 * gap)) for k in range(lines)])

    def halve(array, gap):
        array = array.reshape((array.shape[0] // 2, 2) + array.shape[1:])
        bit = (line_at // gap) % 2
        came = over_line(pick_half(array, 1 - bit, 1), gap)
        return pick_half(array, bit, 1), came

    def in_order(mine, other, gap):
        bit = (line_at // gap) % 2
        pair = jnp.stack([jnp.where(bit == 0, mine, other), jnp.where(bit == 0, other, mine)], axis=1)
        return pair.reshape((-1,) + mine.shape[1:])

    def add(*parts):
        total = parts[0].astype(F32)
        for part in parts[1:]:
            total = total + part.astype(F32)
        return total.astype(BF)

    came = over_core(send)
    keep_x, send_x, joined = back(0, 2, 0, 2, ())
    leave_y = add(keep[0], came[0])
    leave_x = add(keep[1], came[1])
    leave_y, leave_x, joined = tie((leave_y, leave_x, joined))
    first_y = over_cross(leave_y)
    second_x = over_side(leave_x)
    came_x = over_core(send_x)
    keep_v, send_v, joined = back(2, 3, 0, 3, (joined,))
    leave_x = add(keep[2, quarter:], came[2, quarter:], first_y[quarter:])
    leave_y = add(keep[3, quarter:], came[3, quarter:], second_x[quarter:])
    leave_x, leave_y, came_x, out, joined = tie((leave_x, leave_y, came_x, out, joined))
    first_x = over_side(leave_x)
    second_y = over_cross(leave_y)
    came_v = over_core(send_v)
    near_out = over_core(out[1])
    turned_out = over_core(out[3])
    keep_z, send_z, joined = back(5, 1, 0, 1, (joined,))

    came_z = over_core(send_z)
    first = add(keep[2, :quarter], came[2, :quarter], first_y[:quarter], first_x)
    second = add(keep[3, :quarter], came[3, :quarter], second_x[:quarter], second_y)
    both = jnp.concatenate([first, second], axis=0).reshape(level, half // level, -1)
    both, keep_z, near_out, turned_out, came_v = tie((both, keep_z, near_out, turned_out, came_v))
    far_x = over_cross(add(keep_x[1], came_x[1]))
    far_v = over_cross(add(keep_v[1], came_v[1]))
    gap = 1
    stay, moved = halve(both, gap)
    leave_y = add(keep_z[1], came_z[1])
    far_z = over_cross(leave_y)
    while gap * 2 < level:
        stay, moved, leave_y, out = tie((stay, moved, leave_y, out))
        both = add(stay, moved)
        gap = gap * 2
        stay, moved = halve(both, gap)
    stay, leave_y, out, turned_out = tie((stay, leave_y, out, turned_out))
    far_out = over_cross(out[2])
    diagonal_out = over_cross(turned_out)
    moved, far_x, far_v, far_z = tie((moved, far_x, far_v, far_z))
    chunk = jnp.concatenate(
        [add(keep_x[0], came_x[0], far_x), add(keep_v[0], came_v[0], far_v), add(keep_z[0], came_z[0], far_z)], axis=2
    )
    both = add(stay, moved)
    chunk_shape = chunk.shape
    by_line = (lines, 3 * share // lines, chunk_shape[2])
    chunk, both, joined = tie((chunk, both, joined))
    chunk = along_line(chunk.reshape(by_line))
    moved = over_line(both, gap)
    input_low = finish_call(info, joined, weight, x, middle_grad, gain)
    moved, far_out, diagonal_out, input_low = tie((moved, far_out, diagonal_out, input_low))
    both = in_order(both, moved, gap)
    while gap > 2:
        gap = gap // 2
        both = in_order(both, over_line(both, gap), gap)
    both, info_out = tie((both, info))
    block_out = restore_call(info_out, (out[0], near_out, far_out, diagonal_out), BF).reshape(tokens.shape)
    moved = over_line(both, 1)
    chunk, input_low, block_out = tie((chunk, input_low, block_out))
    chunk = sum_low(chunk)
    near_low = over_core(input_low[1])
    turned_low = over_core(input_low[3])
    far_low = over_cross(input_low[2])
    chunk, info_in = tie((chunk, info))
    spread = along_line(jnp.broadcast_to(chunk[None], by_line)).reshape(chunk_shape)
    moved, turned_low, near_low = tie((moved, turned_low, near_low))
    both = in_order(both, moved, 1)
    other = over_side(both)
    diagonal_low = over_cross(turned_low)
    pieces = (input_low[0], near_low, far_low, diagonal_low)
    input_grad = restore_call(info_in, pieces, F32).reshape(tokens.shape)

    arrays = (
        outward_weight, outward_first, outward_second,
        expand_weight, expand_first, expand_second,
        shrink_weight, shrink_first, shrink_second,
    )
    own_side = side.reshape(1)
    other_side = (1 - side).reshape(1)
    others_new = others_call(own_side, both.reshape(2, quarter, -1), arrays, ())
    *inward_new, product = inward_call(spread, inward_weight, inward_first, inward_second)
    other, product = tie((other, product))
    *others_new, expand_product = others_call(other_side, other.reshape(2, quarter, -1), arrays, others_new)
    own_gain = gain_weight.astype(BF).astype(F32)
    gain_grad = jnp.stack(
        [
            jnp.sum(product, axis=1),
            jnp.sum(expand_product, axis=1),
        ]
    ) / own_gain

    results = [block_out, input_grad]
    results += inward_new
    results += others_new
    results += adam_update(gain_weight, gain_grad, gain_first, gain_second, rates[4], 0.0)
    return tuple(results)


def solution(mesh):
    split = P(None, "dp", "fsdp", None)
    rows = P("fsdp", None)
    columns = P(None, "fsdp")
    kinds = (rows, rows, rows, rows, columns)
    in_specs = (split, split, P(None, "dp")) + kinds * 3
    out_specs = (split, split) + (rows,) * 12 + (columns,) * 3
    return jax.shard_map(local, mesh=mesh, in_specs=in_specs, out_specs=out_specs, check_vma=False)
```

```python
import functools

import jax
import jax.numpy as jnp
from jax import lax
from jax.experimental import pallas as pl
from jax.experimental.pallas import tpu as pltpu
from jax.sharding import PartitionSpec as P

FF = 1152
HEADS = 12
HDIM = 64
STEP = 10

rope_base = 160000.0
norm_eps = 1e-05
adam_beta = 0.5
adam_eps = 1e-08
weight_decay = 0.01
rates = (0.07, 2.0, 0.07, 0.06, 0.2)
masked_score = -1e30
small_score = 50.0

BF = jnp.bfloat16
F32 = jnp.float32
NN = (((1,), (0,)), ((), ()))
NT = (((1,), (1,)), ((), ()))
TN = (((0,), (0,)), ((), ()))
VMEM_BYTES = 58 << 20
LANES = 128
PAIRS = HEADS * HDIM // LANES


def cost(flops, size):
    return pl.CostEstimate(flops=int(flops), bytes_accessed=int(size), transcendentals=0)


def dot(left, right, dims=NN):
    return lax.dot_general(left, right, dims, preferred_element_type=F32)


def swap_halves(values):
    lane = lax.broadcasted_iota(jnp.int32, (1, LANES), 1)
    former = lax.rem(lane, HDIM) < HDIM // 2
    ahead = pltpu.roll(values, LANES - HDIM // 2, 1)
    behind = pltpu.roll(values, HDIM // 2, 1)
    return jnp.where(former, ahead, behind)


def centre_scale(values):
    center = values - jnp.mean(values, axis=-1, keepdims=True)
    spread = jnp.mean(center * center, axis=-1, keepdims=True)
    inverse = lax.rsqrt(spread + norm_eps)
    return center * inverse, inverse


def norm_back(grad, normed, inverse, gain):
    scaled = grad * gain
    mean_one = jnp.mean(scaled, axis=-1, keepdims=True)
    mean_two = jnp.mean(scaled * normed, axis=-1, keepdims=True)
    return inverse * (scaled - mean_one - normed * mean_two)


def quarters(refs):
    own, near = refs[:2]
    return tuple(tuple(ref.at[k] for k in range(4)) for ref in (own, near)) + (refs[2:6], refs[6:10])


def place(scratch, pieces, info, rows):
    quarter = rows // 4
    for r, piece in enumerate(pieces):
        owner = info[0] ^ r
        for k, ref in enumerate(piece):
            side = k if r < 2 else info[3] ^ k
            at = pl.ds(pl.multiple_of(owner * rows + side * quarter, 16), quarter)
            for pair in range(PAIRS):
                for kind in range(3):
                    source = (kind * PAIRS + pair) * LANES
                    target = (pair * 3 + kind) * LANES
                    scratch[at, target : target + LANES] = ref[:quarter, source : source + LANES]


def pick(index, choices):
    value = choices[-1]
    for k in range(len(choices) - 2, -1, -1):
        value = jnp.where(index == k, choices[k], value)
    return value


def qkv_kernel(info, x_ref, cos_ref, sin_ref, *refs, share):
    ht_ref, qkv_ref, w_ref, gain_ref = refs[-4:]

    @pl.when(pl.program_id(0) == 0)
    def _():
        pieces = quarters(refs[:10])
        place(w_ref, pieces, info, share)
        quarter = share // 4
        for row in range(2):
            found = []
            for r, piece in enumerate(pieces):
                rows = [ref[quarter : quarter + 1, :share].astype(F32) for ref in piece]
                found.append(rows[row] if r < 2 else pick(info[3] ^ row, rows))
            ordered = [pick(info[0] ^ owner, found) for owner in range(4)]
            gain_ref[row : row + 1, :] = jnp.concatenate(ordered, axis=1)

    normed, unused = centre_scale(x_ref[...].astype(F32))
    low = (normed * gain_ref[0:1, :]).astype(BF)
    ht_ref[...] = low.T
    cosine = cos_ref[...]
    sine = sin_ref[...]
    for pair in range(PAIRS):
        start = pair * 3 * LANES
        if pair % 2 == 0:
            joined = dot(low, w_ref[:, start : start + 6 * LANES])
        for kind in range(3):
            at = (pair % 2 * 3 + kind) * LANES
            block = joined[:, at : at + LANES]
            if kind < 2:
                block = block * cosine + swap_halves(block) * sine
            block = block.astype(BF)
            if kind == 0:
                block = block * jnp.asarray(HDIM**-0.5, BF)
            qkv_ref[:, start + kind * LANES : start + (kind + 1) * LANES] = block


def qkv_call(info, x, cosine, sine, pieces, tile=256):
    rows, width = x.shape
    wide = pieces[0].shape[2]
    whole = lambda i, s: (0, 0)
    by_row = lambda i, s: (i, 0)
    return pl.pallas_call(
        functools.partial(qkv_kernel, share=width // 4),
        grid_spec=pltpu.PrefetchScalarGridSpec(
            num_scalar_prefetch=1,
            grid=(rows // tile,),
            in_specs=[
                pl.BlockSpec((tile, width), by_row),
                pl.BlockSpec((tile, LANES), by_row),
                pl.BlockSpec((tile, LANES), by_row),
            ]
            + [pl.BlockSpec(piece.shape, lambda i, s, n=piece.ndim: (0,) * n) for piece in pieces],
            out_specs=[
                pl.BlockSpec((width, tile), lambda i, s: (0, i)),
                pl.BlockSpec((tile, wide), by_row),
                pl.BlockSpec((width, wide), whole),
                pl.BlockSpec((2, width), whole),
            ],
        ),
        out_shape=[
            jax.ShapeDtypeStruct((width, rows), BF),
            jax.ShapeDtypeStruct((rows, wide), BF),
            jax.ShapeDtypeStruct((width, wide), BF),
            jax.ShapeDtypeStruct((2, width), F32),
        ],
        compiler_params=pltpu.CompilerParams(vmem_limit_bytes=VMEM_BYTES),
        cost_estimate=cost(2 * rows * width * wide, 36e6),
        name="qkv",
    )(info, x, cosine, sine, *pieces)


def attend_kernel(info, qkv_ref, *rest, tile):
    o_ref, r_ref, p_ref = rest[-3:]
    rows = qkv_ref.shape[0]
    key_at = lax.broadcasted_iota(jnp.int32, (1, rows), 1)
    bias = jnp.where(key_at < info[1], 0.0, masked_score).astype(F32)
    keys = qkv_ref[:, LANES : 2 * LANES]
    values = qkv_ref[:, 2 * LANES :]
    low = lax.broadcasted_iota(jnp.int32, (1, LANES), 1) < HDIM
    one = jnp.ones((), BF)
    zero = jnp.zeros((), BF)
    sides = (jnp.where(low, values, one), jnp.where(low, one, values))
    def heads_of(at):
        queries = qkv_ref[at, :LANES]
        return jnp.where(low, queries, zero), jnp.where(low, zero, queries)

    def finish(at, outs):
        mixed = jnp.where(low, outs[0], outs[1])
        total = pltpu.roll(jnp.where(low, outs[1], outs[0]), HDIM, 1)
        inverse = 1.0 / total
        o_ref[at, :] = (mixed * inverse).astype(BF)
        r_ref[at, :] = inverse

    mine = lax.broadcasted_iota(jnp.int32, (LANES, LANES), 0) // HDIM
    same = mine == lax.broadcasted_iota(jnp.int32, (LANES, LANES), 1) // HDIM
    same = same.astype(BF)

    def longest(values):
        return jnp.max(dot(values * values, same), axis=0, keepdims=True)

    bound = jnp.max(longest(qkv_ref[:, :LANES]) * longest(keys))

    @pl.when(bound < small_score * small_score)
    def _():
        for step in range(rows // tile):
            at = pl.ds(step * tile, tile)
            outs = []
            for head, queries in enumerate(heads_of(at)):
                terms = jnp.exp(dot(queries, keys, NT) + bias).astype(BF)
                p_ref[head, at, :] = terms
                outs.append(dot(terms, sides[head]))
            finish(at, outs)

    @pl.when(jnp.logical_not(bound < small_score * small_score))
    def _():
        some = 128

        def body(step, unused):
            at = pl.ds(pl.multiple_of(step * some, some), some)
            outs = []
            for head, queries in enumerate(heads_of(at)):
                scores = dot(queries, keys, NT) + bias
                peak = jnp.max(scores, axis=-1, keepdims=True)
                terms = jnp.exp(scores - peak).astype(BF)
                p_ref[head, at, :] = terms
                outs.append(dot(terms, sides[head]))
            finish(at, outs)
            return unused

        lax.fori_loop(0, rows // some, body, 0)


def attend_call(info, qkv, start, count, buffers, tile=512):
    rows = qkv.shape[0]
    width = qkv.shape[1] // 3
    block = pl.BlockSpec((rows, LANES), lambda p, s: (0, start + p))
    buffers = tuple(buffers)
    return pl.pallas_call(
        functools.partial(attend_kernel, tile=tile),
        grid_spec=pltpu.PrefetchScalarGridSpec(
            num_scalar_prefetch=1,
            grid=(count,),
            in_specs=[pl.BlockSpec((rows, 3 * LANES), lambda p, s: (0, start + p))]
            + [pl.BlockSpec(memory_space=pl.ANY)] * len(buffers),
            out_specs=[
                block,
                block,
                pl.BlockSpec((2, rows, rows), lambda p, s: (start + p, 0, 0)),
            ],
        ),
        out_shape=[
            jax.ShapeDtypeStruct((rows, width), BF),
            jax.ShapeDtypeStruct((rows, width), F32),
            jax.ShapeDtypeStruct((HEADS, rows, rows), BF),
        ],
        input_output_aliases={2 + k: k for k in range(len(buffers))},
        compiler_params=pltpu.CompilerParams(vmem_limit_bytes=VMEM_BYTES),
        cost_estimate=cost(16 * rows * rows * LANES * count, 17e6 * count),
        name="attend",
    )(info, qkv, *buffers)


def feed_kernel(
    info, x_ref, o_ref, r_ref, cot_ref, gain_ref, m0, m1, m2, m3, m4, m5, m6, m7, m8, m9,
    out0, out1, out2, out3, dmid_ref, do_ref, keep_ref, send_ref,
    wo, wi, wd, acc_o, acc_i, acc_d, *, tile, share,
):
    step = pl.program_id(0)
    me = info[0]
    width = x_ref.shape[1]
    inner = wi.shape[1]
    base = width + inner
    half = share // 2

    @pl.when(step == 0)
    def _():
        fourth = share // 4
        for r, piece in enumerate(quarters((m0, m1, m2, m3, m4, m5, m6, m7, m8, m9))):
            owner = me ^ r
            for k, ref in enumerate(piece):
                side = k if r < 2 else info[3] ^ k
                at = pl.ds(pl.multiple_of(owner * share + side * fourth, 16), fourth)
                wo[at, :] = ref[:, :width]
                wi[at, :] = ref[:, width:base]
                down = owner * (3 * half)
                at = pl.ds(pl.multiple_of(down + side * fourth, 16), fourth)
                wd[at, :] = ref[:, base : base + width]
                at = pl.ds(pl.multiple_of(down + share + side % 2 * fourth, 16), fourth)
                fold = pl.ds(pl.multiple_of(side // 2 * (width // 2), LANES), width // 2)
                wd[at, fold] = ref[:, base + width :]

        acc_o[...] = jnp.zeros_like(acc_o)
        acc_i[...] = jnp.zeros_like(acc_i)
        acc_d[...] = jnp.zeros_like(acc_d)

    gain = gain_ref[1:2, :]
    mixed = o_ref[...]
    middle = x_ref[...].astype(F32) + dot(mixed, wo[...])
    normed, inverse = centre_scale(middle)
    hidden = (normed * gain).astype(BF)
    gate = dot(hidden, wi[:, :FF])
    upward = dot(hidden, wi[:, FF:])
    cdf = 0.5 * (1.0 + lax.erf(gate * 0.7071067811865476))
    gelu = gate * cdf
    slope = cdf + gate * (jnp.exp(-0.5 * gate * gate) * 0.3989422804014327)
    state = (gelu * upward).astype(BF)
    row_at = step * tile + lax.broadcasted_iota(jnp.int32, (tile, 1), 0)
    live = row_at < info[1]
    result = jnp.where(live, middle + dot(state, wd[...]), 0.0).astype(BF)
    for r, out_ref in enumerate((out0, out1, out2, out3)):

        @pl.when(me ^ step == r)
        def _():
            out_ref[...] = result

    branch = jnp.where(live, cot_ref[...].astype(F32), 0.0)
    branch_low = branch.astype(BF)
    acc_d[...] += dot(state, branch_low, TN)
    state_grad = dot(branch_low, wd[...], NT)
    gate_grad = (state_grad * upward * slope).astype(BF)
    up_grad = (state_grad * gelu).astype(BF)
    acc_i[:, :FF] += dot(hidden, gate_grad, TN)
    acc_i[:, FF:] += dot(hidden, up_grad, TN)
    hidden_grad = dot(gate_grad, wi[:, :FF], NT) + dot(up_grad, wi[:, FF:], NT)
    mixer = (branch + norm_back(hidden_grad, normed, inverse, gain)).astype(BF)
    dmid_ref[...] = mixer
    acc_o[...] += dot(mixed, mixer, TN)
    do_ref[...] = (dot(mixer, wo[...], NT) * r_ref[...]).astype(BF)

    @pl.when(step == pl.num_programs(0) - 1)
    def _():
        quarter = share // 4
        for r in range(4):
            owner = me ^ r
            target = send_ref if r % 2 else keep_ref
            mate = r // 2
            for part in range(2):
                for other in range(2):
                    side = info[2] ^ other
                    group, spot = ((2 * (1 - mate), other), (3 - 2 * other, mate))[part]
                    to = slice(spot * quarter, (spot + 1) * quarter)
                    shift = part * half + side * quarter
                    at = pl.ds(pl.multiple_of(owner * share + shift, 16), quarter)
                    target[group, to, :width] = acc_o[at, :].astype(BF)
                    target[group, to, width:base] = acc_i[at, :].astype(BF)
                    at = pl.ds(pl.multiple_of(owner * (3 * half) + shift, 16), quarter)
                    target[group, to, base : base + width] = acc_d[at, :].astype(BF)
                    at = pl.ds(pl.multiple_of(owner * (3 * half) + share + side * quarter, 16), quarter)
                    fold = slice(part * width // 2, (part + 1) * width // 2)
                    target[group, to, base + width :] = acc_d[at, fold].astype(BF)


def feed_call(info, x, mixed, inverse, cot, gain, pieces):
    rows, width = x.shape
    tile = rows // 4
    share = width // 4
    packed = pieces[0].shape[2]
    whole = lambda i, s: (0, 0)
    cube = lambda i, s: (0, 0, 0)
    by_row = lambda i, s: (i, 0)
    block = pl.BlockSpec((tile, width), by_row)
    return pl.pallas_call(
        functools.partial(feed_kernel, tile=tile, share=share),
        grid_spec=pltpu.PrefetchScalarGridSpec(
            num_scalar_prefetch=1,
            grid=(rows // tile,),
            in_specs=[block, block, block, block, pl.BlockSpec((2, width), whole)]
            + [pl.BlockSpec(piece.shape, lambda i, s, n=piece.ndim: (0,) * n) for piece in pieces],
            out_specs=[pl.BlockSpec((tile, width), whole)] * 4
            + [block, block]
            + [pl.BlockSpec((4, share // 2, packed), cube)] * 2,
            scratch_shapes=[
                pltpu.VMEM((width, width), BF),
                pltpu.VMEM((width, 2 * FF), BF),
                pltpu.VMEM((FF, width), BF),
                pltpu.VMEM((width, width), F32),
                pltpu.VMEM((width, 2 * FF), F32),
                pltpu.VMEM((FF, width), F32),
            ],
        ),
        out_shape=[jax.ShapeDtypeStruct((tile, width), BF)] * 4
        + [jax.ShapeDtypeStruct((rows, width), BF)] * 2
        + [jax.ShapeDtypeStruct((4, share // 2, packed), BF)] * 2,
        compiler_params=pltpu.CompilerParams(vmem_limit_bytes=VMEM_BYTES),
        cost_estimate=cost(6 * rows * width * (width + 3 * FF), 130e6),
        name="feed",
    )(info, x, mixed, inverse, cot, gain, *pieces)


def back_kernel(info, qkv_ref, o_ref, do_ref, p_ref, cos_ref, sin_ref, ht_ref, *rest, tile):
    keep_ref, send_ref, joined_ref = rest[-3:]
    rows = qkv_ref.shape[0]
    low = lax.broadcasted_iota(jnp.int32, (1, LANES), 1) < HDIM
    zero = jnp.zeros((), BF)
    keys = qkv_ref[:, LANES : 2 * LANES]
    values = qkv_ref[:, 2 * LANES :]
    key_heads = (jnp.where(low, keys, zero), jnp.where(low, zero, keys))
    key_grads = [None, None]
    value_grads = [None, None]
    query_grads = []
    for part in range(rows // tile):
        at = pl.ds(part * tile, tile)
        queries = qkv_ref[at, :LANES]
        grads = do_ref[at, :]
        wide = grads.astype(F32)
        inner = wide * o_ref[at, :].astype(F32)
        grad_heads = (jnp.where(low, grads, zero), jnp.where(low, zero, grads))
        queries_t = queries.astype(F32).T.astype(BF)
        grads_t = wide.T.astype(BF)
        query_grad = None
        for head in range(2):
            mine = low if head == 0 else jnp.logical_not(low)
            lanes = slice(head * HDIM, (head + 1) * HDIM)
            row_inner = jnp.sum(jnp.where(mine, inner, 0.0), axis=-1, keepdims=True)
            term_grad = dot(grad_heads[head], values, NT)
            terms = p_ref[head, at, :]
            score_grad = (terms.astype(F32) * (term_grad - row_inner)).astype(BF)
            partial = dot(score_grad, key_heads[head])
            query_grad = partial if query_grad is None else query_grad + partial
            for grad_list, left, right in (
                (key_grads, queries_t, score_grad),
                (value_grads, grads_t, terms),
            ):
                value = dot(left[lanes], right)
                grad_list[head] = value if grad_list[head] is None else grad_list[head] + value
        query_grads.append(query_grad)
    cosine = cos_ref[...]
    sine = sin_ref[...]
    query_grad = jnp.concatenate(query_grads, axis=0) * (HDIM**-0.5)
    key_grad = jnp.concatenate(key_grads, axis=0).T
    value_grad = jnp.concatenate(value_grads, axis=0).T
    joined = jnp.concatenate(
        [
            (query_grad * cosine - swap_halves(query_grad) * sine).astype(BF),
            (key_grad * cosine - swap_halves(key_grad) * sine).astype(BF),
            value_grad.astype(BF),
        ],
        axis=1,
    )
    joined_ref[...] = joined
    weight_grad = dot(ht_ref[...], joined).astype(BF)
    share = weight_grad.shape[0] // 4
    me = info[0]
    for owner in range(4):
        rel = me ^ owner
        value = weight_grad[owner * share : (owner + 1) * share, :]
        for target, odd in ((keep_ref, 0), (send_ref, 1)):

            @pl.when(rel % 2 == odd)
            def _():
                for kind in range(3):
                    target[rel // 2, kind] = value[:, kind * LANES : (kind + 1) * LANES]


def back_call(info, qkv, mixed, grads, terms, cosine, sine, hidden_t, start, count, slot, slots, buffers, tile=512):
    rows, width = mixed.shape
    whole = lambda p, s: (0, 0)
    block = pl.BlockSpec((rows, LANES), lambda p, s: (0, start + p))
    wide = pl.BlockSpec((rows, 3 * LANES), lambda p, s: (0, start + p))
    table = pl.BlockSpec((rows, LANES), whole)
    operands = [qkv, mixed, grads, terms, cosine, sine, hidden_t]
    share = width // 4
    piece = pl.BlockSpec((2, 3, share, LANES), lambda p, s: (0, 0, 0, slot + p))
    chunk = jax.ShapeDtypeStruct((2, 3, share, LANES * slots), BF)
    aliases = {}
    for k, buffer in enumerate(buffers):
        aliases[1 + len(operands)] = 3 - len(buffers) + k
        operands.append(buffer)
    return pl.pallas_call(
        functools.partial(back_kernel, tile=tile),
        grid_spec=pltpu.PrefetchScalarGridSpec(
            num_scalar_prefetch=1,
            grid=(count,),
            in_specs=[
                wide,
                block,
                block,
                pl.BlockSpec((2, rows, rows), lambda p, s: (start + p, 0, 0)),
                table,
                table,
                pl.BlockSpec((width, rows), whole),
            ]
            + [pl.BlockSpec(memory_space=pl.ANY)] * len(buffers),
            out_specs=[piece, piece, wide],
        ),
        out_shape=[chunk, chunk, jax.ShapeDtypeStruct((rows, 3 * width), BF)],
        input_output_aliases=aliases,
        compiler_params=pltpu.CompilerParams(vmem_limit_bytes=VMEM_BYTES),
        cost_estimate=cost(20 * rows * rows * LANES * count, 36e6 * count),
        name="back",
    )(info, *operands)


def finish_kernel(info, joined_ref, w_ref, x_ref, dmid_ref, gain_ref, dx0, dx1, dx2, dx3):
    normed, inverse = centre_scale(x_ref[...].astype(F32))
    hidden_grad = dot(joined_ref[...], w_ref[...], NT)
    back = norm_back(hidden_grad, normed, inverse, gain_ref[0:1, :])
    result = (dmid_ref[...].astype(F32) + back).astype(BF)
    for r, dx_ref in enumerate((dx0, dx1, dx2, dx3)):

        @pl.when(info[0] ^ pl.program_id(0) == r)
        def _():
            dx_ref[...] = result


def finish_call(info, joined, weight, x, dmid, gain):
    rows, width = x.shape
    tile = rows // 4
    wide = joined.shape[1]
    by_row = lambda i, s: (i, 0)
    whole = lambda i, s: (0, 0)
    return pl.pallas_call(
        finish_kernel,
        grid_spec=pltpu.PrefetchScalarGridSpec(
            num_scalar_prefetch=1,
            grid=(4,),
            in_specs=[
                pl.BlockSpec((tile, wide), by_row),
                pl.BlockSpec((width, wide), whole),
                pl.BlockSpec((tile, width), by_row),
                pl.BlockSpec((tile, width), by_row),
                pl.BlockSpec((2, width), whole),
            ],
            out_specs=[pl.BlockSpec((tile, width), whole)] * 4,
        ),
        out_shape=[jax.ShapeDtypeStruct((tile, width), BF)] * 4,
        compiler_params=pltpu.CompilerParams(vmem_limit_bytes=VMEM_BYTES),
        cost_estimate=cost(0, 4e6),
        name="finish",
    )(info, joined, weight, x, dmid, gain)


def restore_kernel(info, p0, p1, p2, p3, out_ref):
    for r, piece in enumerate((p0, p1, p2, p3)):
        out_ref[info[0] ^ r] = piece[...].astype(out_ref.dtype)


def restore_call(info, pieces, kind):
    rows, width = pieces[0].shape
    return pl.pallas_call(
        restore_kernel,
        grid_spec=pltpu.PrefetchScalarGridSpec(
            num_scalar_prefetch=1,
            grid=(1,),
            in_specs=[pl.BlockSpec((rows, width), lambda i, s: (0, 0))] * 4,
            out_specs=pl.BlockSpec((4, rows, width), lambda i, s: (0, 0, 0)),
        ),
        out_shape=jax.ShapeDtypeStruct((4, rows, width), kind),
        compiler_params=pltpu.CompilerParams(vmem_limit_bytes=VMEM_BYTES),
        cost_estimate=cost(0, 12e6),
        name="restore",
    )(info, *pieces)


def adam_update(master, gradient, moment_one, moment_two, step_rate, decay_rate):
    first_new = adam_beta * moment_one + (1.0 - adam_beta) * gradient
    second_new = adam_beta * moment_two + (1.0 - adam_beta) * gradient * gradient
    correction = 1.0 - adam_beta**STEP
    direction = first_new / correction / (jnp.sqrt(second_new / correction) + adam_eps)
    renewed = master - step_rate * (direction + decay_rate * master)
    return (renewed, first_new, second_new)


def inward_kernel(grad_ref, master_ref, one_ref, two_ref, *rest):
    renewed_ref, first_ref, second_ref, product_ref = rest[-4:]
    grad = grad_ref[0].astype(F32)
    master = master_ref[...]
    renewed_ref[...], first_ref[...], second_ref[...] = adam_update(
        master, grad, one_ref[...], two_ref[...], rates[0], weight_decay
    )
    product = grad * master.astype(BF).astype(F32)

    @pl.when(pl.program_id(0) == 0)
    def _():
        product_ref[...] = jnp.zeros_like(product_ref)

    for start in range(0, product.shape[1], LANES):
        product_ref[...] += product[:, start : start + LANES]


def inward_call(grad, master, one, two):
    rows, wide = master.shape
    columns = grad.shape[2]
    block = pl.BlockSpec((rows, columns), lambda k: (0, k))
    array = jax.ShapeDtypeStruct((rows, wide), F32)
    return pl.pallas_call(
        inward_kernel,
        grid=(3,),
        in_specs=[pl.BlockSpec((1, rows, columns), lambda k: (k, 0, 0)), block, block, block],
        out_specs=[block, block, block, pl.BlockSpec((rows, LANES), lambda k: (0, 0))],
        out_shape=[array, array, array, jax.ShapeDtypeStruct((rows, LANES), F32)],
        compiler_params=pltpu.CompilerParams(vmem_limit_bytes=VMEM_BYTES),
        cost_estimate=cost(0, 18e6),
        name="inward",
    )(grad, master, one, two)


def others_kernel(side, grad_ref, *refs, width, inner):
    masters = refs[:9]
    results = refs[-10:-1]
    product_ref = refs[-1]
    step = pl.program_id(0)
    base = width + inner

    def update(kind, grad):
        master, one, two = masters[3 * kind : 3 * kind + 3]
        values = adam_update(master[...], grad, one[...], two[...], rates[kind + 1], weight_decay)
        for ref, value in zip(results[3 * kind : 3 * kind + 3], values):
            ref[...] = value

    @pl.when(step < 2)
    def _():
        grad = grad_ref[step].astype(F32)
        update(0, grad[:, :width])
        update(1, grad[:, width:base])
        update(2, grad[:, base : base + width])
        product = grad[:, width:base] * masters[3][...].astype(BF).astype(F32)
        total = product[:, :LANES]
        for start in range(LANES, inner, LANES):
            total = total + product[:, start : start + LANES]
        product_ref[...] = total

    @pl.when(step == 2)
    def _():
        update(2, jnp.concatenate([grad_ref[k, :, base + width :].astype(F32) for k in range(2)], axis=1))


def others_call(side, grad, arrays, buffers):
    quarter = grad.shape[1]
    width = arrays[0].shape[1]
    inner = arrays[3].shape[1]
    short = lambda j, s: (2 * jnp.minimum(j, 1) + s[0], 0)
    full = lambda j, s: (2 * j + s[0], 0)
    blocks = []
    for array, place in zip(arrays, (short,) * 6 + (full,) * 3):
        blocks.append(pl.BlockSpec((quarter, array.shape[1]), place))
    sums = jax.ShapeDtypeStruct((arrays[0].shape[0], LANES), F32)
    return pl.pallas_call(
        functools.partial(others_kernel, width=width, inner=inner),
        grid_spec=pltpu.PrefetchScalarGridSpec(
            num_scalar_prefetch=1,
            grid=(3,),
            in_specs=[pl.BlockSpec(grad.shape, lambda j, s: (0, 0, 0))]
            + blocks
            + [pl.BlockSpec(memory_space=pl.ANY)] * len(buffers),
            out_specs=blocks + [pl.BlockSpec((quarter, LANES), short)],
        ),
        out_shape=[jax.ShapeDtypeStruct(array.shape, F32) for array in arrays] + [sums],
        input_output_aliases={11 + k: k for k in range(len(buffers))},
        compiler_params=pltpu.CompilerParams(vmem_limit_bytes=VMEM_BYTES),
        cost_estimate=cost(0, 14e6),
        name="others",
    )(side, grad, *arrays, *buffers)


def tables(seq_total):
    lane = jnp.arange(LANES, dtype=jnp.int32)
    exponent = (lane % (HDIM // 2)).astype(F32) * (2.0 / HDIM)
    inverse = jnp.power(jnp.float32(rope_base), -exponent)
    angles = jnp.arange(seq_total, dtype=F32)[:, None] * inverse[None, :]
    sign = jnp.where(lane % HDIM < HDIM // 2, -1.0, 1.0).astype(F32)
    return jnp.cos(angles), jnp.sin(angles) * sign[None, :]


CORE = [(0, 1), (1, 0), (2, 3), (3, 2)]
CROSS = [(0, 2), (1, 3), (2, 0), (3, 1)]
tie = lax.optimization_barrier


def over_core(array):
    return lax.ppermute(array, "fsdp", CORE)


def over_cross(array):
    return lax.ppermute(array, "fsdp", CROSS)


def over_side(array):
    return lax.ppermute(array, "dp", [(k, k ^ 1) for k in range(lax.axis_size("dp"))])


def along_line(array, groups=None):
    return lax.all_to_all(array, "dp", 0, 0, axis_index_groups=groups)


def add_low(left, right):
    return (left.astype(F32) + right.astype(F32)).astype(BF)


def sum_low(array):
    return jnp.sum(array.astype(F32), axis=0).astype(BF)


def pick_half(array, index, axis=0):
    return lax.dynamic_index_in_dim(array, index, axis, keepdims=False)


def local(
    tokens, cotangent, lengths,
    inward_weight, outward_weight, expand_weight, shrink_weight, gain_weight,
    inward_first, outward_first, expand_first, shrink_first, gain_first,
    inward_second, outward_second, expand_second, shrink_second, gain_second,
):
    micro_count, group_size, local_len, width = tokens.shape
    fsdp = lax.axis_size("fsdp")
    lines = lax.axis_size("dp")
    assert fsdp == 4 and micro_count * group_size == fsdp and lines % 4 == 0
    seq_total = local_len * fsdp
    share, wide = inward_weight.shape
    half = share // 2
    me = lax.axis_index("fsdp").astype(jnp.int32)
    side = (lax.axis_index("dp") % 2).astype(jnp.int32)
    fourth = (lax.axis_index("dp") % 4).astype(jnp.int32)
    info = jnp.stack([me, pick_half(lengths.reshape(fsdp), me), side, fourth])
    columns = [[k for k in range(lines) if k % 2 == odd] for odd in range(2)]

    def to_sequence(array):
        array = array.reshape(fsdp, local_len, width)
        return lax.all_to_all(array, "fsdp", 0, 0).reshape(seq_total, width)

    def around(array):
        return [array] + [lax.ppermute(array, "dp", [(d, d ^ k) for d in range(lines)]) for k in range(1, 4)]

    def with_gains(weight, gains):
        gains = jnp.pad(gains.astype(BF)[:, None, :], ((0, 0), (0, 7), (0, wide - share)))
        return jnp.concatenate([weight.astype(BF), gains], axis=1)

    inward_parts = inward_weight.reshape(4, half // 2, wide)
    gain_parts = jnp.pad(gain_weight, ((0, 2), (0, 0)))
    leaving = with_gains(pick_half(inward_parts, fourth)[None], pick_half(gain_parts, fourth)[None])[0]
    far = over_cross(leaving)

    (inward_parts, outward, leaving) = tie((inward_parts, outward_weight, leaving))
    own = with_gains(inward_parts, gain_parts)
    near = over_core(own)
    tokens, own = tie((tokens, own))
    x = to_sequence(tokens)
    shrink_low = shrink_weight.astype(BF)
    folded = jnp.concatenate([shrink_low[share:, : width // 2], shrink_low[share:, width // 2 :]], axis=0)
    packed = jnp.concatenate(
        [outward.astype(BF), expand_weight.astype(BF), shrink_low[:share], folded], axis=1
    ).reshape(4, half // 2, -1)
    cosine, sine = tables(seq_total)
    leaving = pick_half(packed, fourth)
    far = around(far)
    far, cosine, sine, info, packed, leaving = tie((far, cosine, sine, info, packed, leaving))
    inward_pieces = (own, near, *far, *[over_core(piece) for piece in far])

    leaving, x = tie((leaving, x))
    other_far = over_cross(leaving)
    other_near = over_core(packed)

    hidden_t, qkv, weight, gain = qkv_call(info, x, cosine, sine, inward_pieces)
    cotangent, other_far, qkv = tie((cotangent, other_far, qkv))
    other_far = around(other_far)
    cot = to_sequence(cotangent)
    mixed, inverse, terms = attend_call(info, qkv, 0, PAIRS, ())
    mixed, other_far = tie((mixed, other_far))
    other_pieces = (packed, other_near, *other_far, *[over_core(piece) for piece in other_far])
    *out, middle_grad, grads, keep, send = feed_call(info, x, mixed, inverse, cot, gain, other_pieces)

    def back(start, count, slot, slots, buffers):
        return back_call(
            info, qkv, mixed, grads, terms, cosine, sine, hidden_t, start, count, slot, slots, buffers
        )

    quarter = half // 2
    level = lines // 2
    line_at = lax.axis_index("dp") // 2

    def over_line(array, gap):
        return lax.ppermute(array, "dp", [(k, k ^ (2 * gap)) for k in range(lines)])

    def halve(array, gap):
        array = array.reshape((array.shape[0] // 2, 2) + array.shape[1:])
        bit = (line_at // gap) % 2
        came = over_line(pick_half(array, 1 - bit, 1), gap)
        return pick_half(array, bit, 1), came

    def in_order(mine, other, gap):
        bit = (line_at // gap) % 2
        pair = jnp.stack([jnp.where(bit == 0, mine, other), jnp.where(bit == 0, other, mine)], axis=1)
        return pair.reshape((-1,) + mine.shape[1:])

    def add(*parts):
        total = parts[0].astype(F32)
        for part in parts[1:]:
            total = total + part.astype(F32)
        return total.astype(BF)

    came = over_core(send)
    keep_x, send_x, joined = back(0, 2, 0, 2, ())
    leave_y = add(keep[0], came[0])
    leave_x = add(keep[1], came[1])
    leave_y, leave_x, joined = tie((leave_y, leave_x, joined))
    first_y = over_cross(leave_y)
    second_x = over_side(leave_x)
    came_x = over_core(send_x)
    keep_v, send_v, joined = back(2, 3, 0, 3, (joined,))
    leave_x = add(keep[2, quarter:], came[2, quarter:], first_y[quarter:])
    leave_y = add(keep[3, quarter:], came[3, quarter:], second_x[quarter:])
    leave_x, leave_y, came_x, out, joined = tie((leave_x, leave_y, came_x, out, joined))
    first_x = over_side(leave_x)
    second_y = over_cross(leave_y)
    came_v = over_core(send_v)
    near_out = over_core(out[1])
    turned_out = over_core(out[3])
    keep_z, send_z, joined = back(5, 1, 0, 1, (joined,))

    came_z = over_core(send_z)
    first = add(keep[2, :quarter], came[2, :quarter], first_y[:quarter], first_x)
    second = add(keep[3, :quarter], came[3, :quarter], second_x[:quarter], second_y)
    both = jnp.concatenate([first, second], axis=0).reshape(level, half // level, -1)
    both, keep_z, near_out, turned_out, came_v = tie((both, keep_z, near_out, turned_out, came_v))
    far_x = over_cross(add(keep_x[1], came_x[1]))
    far_v = over_cross(add(keep_v[1], came_v[1]))
    gap = 1
    stay, moved = halve(both, gap)
    leave_y = add(keep_z[1], came_z[1])
    far_z = over_cross(leave_y)
    while gap * 2 < level:
        stay, moved, leave_y, out = tie((stay, moved, leave_y, out))
        both = add(stay, moved)
        gap = gap * 2
        stay, moved = halve(both, gap)
    stay, leave_y, out, turned_out = tie((stay, leave_y, out, turned_out))
    far_out = over_cross(out[2])
    diagonal_out = over_cross(turned_out)
    moved, far_x, far_v, far_z = tie((moved, far_x, far_v, far_z))
    chunk = jnp.concatenate(
        [add(keep_x[0], came_x[0], far_x), add(keep_v[0], came_v[0], far_v), add(keep_z[0], came_z[0], far_z)], axis=2
    )
    both = add(stay, moved)
    chunk_shape = chunk.shape
    by_line = (lines, 3 * share // lines, chunk_shape[2])
    chunk, both, joined = tie((chunk, both, joined))
    chunk = along_line(chunk.reshape(by_line))
    moved = over_line(both, gap)
    input_low = finish_call(info, joined, weight, x, middle_grad, gain)
    moved, far_out, diagonal_out, input_low = tie((moved, far_out, diagonal_out, input_low))
    both = in_order(both, moved, gap)
    while gap > 2:
        gap = gap // 2
        both = in_order(both, over_line(both, gap), gap)
    both, info_out = tie((both, info))
    block_out = restore_call(info_out, (out[0], near_out, far_out, diagonal_out), BF).reshape(tokens.shape)
    moved = over_line(both, 1)
    chunk, input_low, block_out = tie((chunk, input_low, block_out))
    chunk = sum_low(chunk)
    near_low = over_core(input_low[1])
    turned_low = over_core(input_low[3])
    far_low = over_cross(input_low[2])
    chunk, info_in = tie((chunk, info))
    spread = along_line(jnp.broadcast_to(chunk[None], by_line)).reshape(chunk_shape)
    moved, turned_low, near_low = tie((moved, turned_low, near_low))
    both = in_order(both, moved, 1)
    other = over_side(both)
    diagonal_low = over_cross(turned_low)
    pieces = (input_low[0], near_low, far_low, diagonal_low)
    input_grad = restore_call(info_in, pieces, F32).reshape(tokens.shape)

    arrays = (
        outward_weight, outward_first, outward_second,
        expand_weight, expand_first, expand_second,
        shrink_weight, shrink_first, shrink_second,
    )
    own_side = side.reshape(1)
    other_side = (1 - side).reshape(1)
    others_new = others_call(own_side, both.reshape(2, quarter, -1), arrays, ())
    *inward_new, product = inward_call(spread, inward_weight, inward_first, inward_second)
    other, product = tie((other, product))
    *others_new, expand_product = others_call(other_side, other.reshape(2, quarter, -1), arrays, others_new)
    own_gain = gain_weight.astype(BF).astype(F32)
    gain_grad = jnp.stack(
        [
            jnp.sum(product, axis=1),
            jnp.sum(expand_product, axis=1),
        ]
    ) / own_gain

    results = [block_out, input_grad]
    results += inward_new
    results += others_new
    results += adam_update(gain_weight, gain_grad, gain_first, gain_second, rates[4], 0.0)
    return tuple(results)


def solution(mesh):
    split = P(None, "dp", "fsdp", None)
    rows = P("fsdp", None)
    columns = P(None, "fsdp")
    kinds = (rows, rows, rows, rows, columns)
    in_specs = (split, split, P(None, "dp")) + kinds * 3
    out_specs = (split, split) + (rows,) * 12 + (columns,) * 3
    return jax.shard_map(local, mesh=mesh, in_specs=in_specs, out_specs=out_specs, check_vma=False)
```

```python
import functools

import jax
import jax.numpy as jnp
from jax import lax
from jax.experimental import pallas as pl
from jax.experimental.pallas import tpu as pltpu
from jax.sharding import PartitionSpec as P

FF = 1152
HEADS = 12
HDIM = 64
STEP = 10

rope_base = 160000.0
norm_eps = 1e-05
adam_beta = 0.5
adam_eps = 1e-08
weight_decay = 0.01
rates = (0.07, 2.0, 0.07, 0.06, 0.2)
masked_score = -1e30
small_score = 50.0

BF = jnp.bfloat16
F32 = jnp.float32
NN = (((1,), (0,)), ((), ()))
NT = (((1,), (1,)), ((), ()))
TN = (((0,), (0,)), ((), ()))
VMEM_BYTES = 58 << 20
LANES = 128
PAIRS = HEADS * HDIM // LANES


def cost(flops, size):
    return pl.CostEstimate(flops=int(flops), bytes_accessed=int(size), transcendentals=0)


def dot(left, right, dims=NN):
    return lax.dot_general(left, right, dims, preferred_element_type=F32)


def swap_halves(values):
    lane = lax.broadcasted_iota(jnp.int32, (1, LANES), 1)
    former = lax.rem(lane, HDIM) < HDIM // 2
    ahead = pltpu.roll(values, LANES - HDIM // 2, 1)
    behind = pltpu.roll(values, HDIM // 2, 1)
    return jnp.where(former, ahead, behind)


def centre_scale(values):
    center = values - jnp.mean(values, axis=-1, keepdims=True)
    spread = jnp.mean(center * center, axis=-1, keepdims=True)
    inverse = lax.rsqrt(spread + norm_eps)
    return center * inverse, inverse


def norm_back(grad, normed, inverse, gain):
    scaled = grad * gain
    mean_one = jnp.mean(scaled, axis=-1, keepdims=True)
    mean_two = jnp.mean(scaled * normed, axis=-1, keepdims=True)
    return inverse * (scaled - mean_one - normed * mean_two)


def quarters(refs):
    own, near = refs[:2]
    return tuple(tuple(ref.at[k] for k in range(4)) for ref in (own, near)) + (refs[2:6], refs[6:10])


def place(scratch, pieces, info, rows):
    quarter = rows // 4
    for r, piece in enumerate(pieces):
        owner = info[0] ^ r
        for k, ref in enumerate(piece):
            side = k if r < 2 else info[3] ^ k
            at = pl.ds(pl.multiple_of(owner * rows + side * quarter, 16), quarter)
            for pair in range(PAIRS):
                for kind in range(3):
                    source = (kind * PAIRS + pair) * LANES
                    target = (pair * 3 + kind) * LANES
                    scratch[at, target : target + LANES] = ref[:quarter, source : source + LANES]


def pick(index, choices):
    value = choices[-1]
    for k in range(len(choices) - 2, -1, -1):
        value = jnp.where(index == k, choices[k], value)
    return value


def qkv_kernel(info, x_ref, cos_ref, sin_ref, *refs, share):
    ht_ref, qkv_ref, w_ref, gain_ref = refs[-4:]

    @pl.when(pl.program_id(0) == 0)
    def _():
        pieces = quarters(refs[:10])
        place(w_ref, pieces, info, share)
        quarter = share // 4
        for row in range(2):
            found = []
            for r, piece in enumerate(pieces):
                rows = [ref[quarter : quarter + 1, :share].astype(F32) for ref in piece]
                found.append(rows[row] if r < 2 else pick(info[3] ^ row, rows))
            ordered = [pick(info[0] ^ owner, found) for owner in range(4)]
            gain_ref[row : row + 1, :] = jnp.concatenate(ordered, axis=1)

    normed, unused = centre_scale(x_ref[...].astype(F32))
    low = (normed * gain_ref[0:1, :]).astype(BF)
    ht_ref[...] = low.T
    cosine = cos_ref[...]
    sine = sin_ref[...]
    for pair in range(PAIRS):
        start = pair * 3 * LANES
        if pair % 2 == 0:
            joined = dot(low, w_ref[:, start : start + 6 * LANES])
        for kind in range(3):
            at = (pair % 2 * 3 + kind) * LANES
            block = joined[:, at : at + LANES]
            if kind < 2:
                block = block * cosine + swap_halves(block) * sine
            block = block.astype(BF)
            if kind == 0:
                block = block * jnp.asarray(HDIM**-0.5, BF)
            qkv_ref[:, start + kind * LANES : start + (kind + 1) * LANES] = block


def qkv_call(info, x, cosine, sine, pieces, tile=256):
    rows, width = x.shape
    wide = pieces[0].shape[2]
    whole = lambda i, s: (0, 0)
    by_row = lambda i, s: (i, 0)
    return pl.pallas_call(
        functools.partial(qkv_kernel, share=width // 4),
        grid_spec=pltpu.PrefetchScalarGridSpec(
            num_scalar_prefetch=1,
            grid=(rows // tile,),
            in_specs=[
                pl.BlockSpec((tile, width), by_row),
                pl.BlockSpec((tile, LANES), by_row),
                pl.BlockSpec((tile, LANES), by_row),
            ]
            + [pl.BlockSpec(piece.shape, lambda i, s, n=piece.ndim: (0,) * n) for piece in pieces],
            out_specs=[
                pl.BlockSpec((width, tile), lambda i, s: (0, i)),
                pl.BlockSpec((tile, wide), by_row),
                pl.BlockSpec((width, wide), whole),
                pl.BlockSpec((2, width), whole),
            ],
        ),
        out_shape=[
            jax.ShapeDtypeStruct((width, rows), BF),
            jax.ShapeDtypeStruct((rows, wide), BF),
            jax.ShapeDtypeStruct((width, wide), BF),
            jax.ShapeDtypeStruct((2, width), F32),
        ],
        compiler_params=pltpu.CompilerParams(vmem_limit_bytes=VMEM_BYTES),
        cost_estimate=cost(2 * rows * width * wide, 36e6),
        name="qkv",
    )(info, x, cosine, sine, *pieces)


def attend_kernel(info, qkv_ref, *rest, tile):
    o_ref, r_ref, p_ref = rest[-3:]
    rows = qkv_ref.shape[0]
    key_at = lax.broadcasted_iota(jnp.int32, (1, rows), 1)
    bias = jnp.where(key_at < info[1], 0.0, masked_score).astype(F32)
    keys = qkv_ref[:, LANES : 2 * LANES]
    values = qkv_ref[:, 2 * LANES :]
    low = lax.broadcasted_iota(jnp.int32, (1, LANES), 1) < HDIM
    one = jnp.ones((), BF)
    zero = jnp.zeros((), BF)
    sides = (jnp.where(low, values, one), jnp.where(low, one, values))
    def heads_of(at):
        queries = qkv_ref[at, :LANES]
        return jnp.where(low, queries, zero), jnp.where(low, zero, queries)

    def finish(at, outs):
        mixed = jnp.where(low, outs[0], outs[1])
        total = pltpu.roll(jnp.where(low, outs[1], outs[0]), HDIM, 1)
        inverse = 1.0 / total
        o_ref[at, :] = (mixed * inverse).astype(BF)
        r_ref[at, :] = inverse

    mine = lax.broadcasted_iota(jnp.int32, (LANES, LANES), 0) // HDIM
    same = mine == lax.broadcasted_iota(jnp.int32, (LANES, LANES), 1) // HDIM
    same = same.astype(BF)

    def longest(values):
        return jnp.max(dot(values * values, same), axis=0, keepdims=True)

    bound = jnp.max(longest(qkv_ref[:, :LANES]) * longest(keys))

    @pl.when(bound < small_score * small_score)
    def _():
        for step in range(rows // tile):
            at = pl.ds(step * tile, tile)
            outs = []
            for head, queries in enumerate(heads_of(at)):
                terms = jnp.exp(dot(queries, keys, NT) + bias).astype(BF)
                p_ref[head, at, :] = terms
                outs.append(dot(terms, sides[head]))
            finish(at, outs)

    @pl.when(jnp.logical_not(bound < small_score * small_score))
    def _():
        some = 128

        def body(step, unused):
            at = pl.ds(pl.multiple_of(step * some, some), some)
            outs = []
            for head, queries in enumerate(heads_of(at)):
                scores = dot(queries, keys, NT) + bias
                peak = jnp.max(scores, axis=-1, keepdims=True)
                terms = jnp.exp(scores - peak).astype(BF)
                p_ref[head, at, :] = terms
                outs.append(dot(terms, sides[head]))
            finish(at, outs)
            return unused

        lax.fori_loop(0, rows // some, body, 0)


def attend_call(info, qkv, start, count, buffers, tile=512):
    rows = qkv.shape[0]
    width = qkv.shape[1] // 3
    block = pl.BlockSpec((rows, LANES), lambda p, s: (0, start + p))
    buffers = tuple(buffers)
    return pl.pallas_call(
        functools.partial(attend_kernel, tile=tile),
        grid_spec=pltpu.PrefetchScalarGridSpec(
            num_scalar_prefetch=1,
            grid=(count,),
            in_specs=[pl.BlockSpec((rows, 3 * LANES), lambda p, s: (0, start + p))]
            + [pl.BlockSpec(memory_space=pl.ANY)] * len(buffers),
            out_specs=[
                block,
                block,
                pl.BlockSpec((2, rows, rows), lambda p, s: (start + p, 0, 0)),
            ],
        ),
        out_shape=[
            jax.ShapeDtypeStruct((rows, width), BF),
            jax.ShapeDtypeStruct((rows, width), F32),
            jax.ShapeDtypeStruct((HEADS, rows, rows), BF),
        ],
        input_output_aliases={2 + k: k for k in range(len(buffers))},
        compiler_params=pltpu.CompilerParams(vmem_limit_bytes=VMEM_BYTES),
        cost_estimate=cost(16 * rows * rows * LANES * count, 17e6 * count),
        name="attend",
    )(info, qkv, *buffers)


def feed_kernel(
    info, x_ref, o_ref, r_ref, cot_ref, gain_ref, m0, m1, m2, m3, m4, m5, m6, m7, m8, m9,
    out0, out1, out2, out3, dmid_ref, do_ref, keep_ref, send_ref,
    wo, wi, wd, acc_o, acc_i, acc_d, *, tile, share,
):
    step = pl.program_id(0)
    me = info[0]
    width = x_ref.shape[1]
    inner = wi.shape[1]
    base = width + inner
    half = share // 2

    @pl.when(step == 0)
    def _():
        fourth = share // 4
        for r, piece in enumerate(quarters((m0, m1, m2, m3, m4, m5, m6, m7, m8, m9))):
            owner = me ^ r
            for k, ref in enumerate(piece):
                side = k if r < 2 else info[3] ^ k
                at = pl.ds(pl.multiple_of(owner * share + side * fourth, 16), fourth)
                wo[at, :] = ref[:, :width]
                wi[at, :] = ref[:, width:base]
                down = owner * (3 * half)
                at = pl.ds(pl.multiple_of(down + side * fourth, 16), fourth)
                wd[at, :] = ref[:, base : base + width]
                at = pl.ds(pl.multiple_of(down + share + side % 2 * fourth, 16), fourth)
                fold = pl.ds(pl.multiple_of(side // 2 * (width // 2), LANES), width // 2)
                wd[at, fold] = ref[:, base + width :]

        acc_o[...] = jnp.zeros_like(acc_o)
        acc_i[...] = jnp.zeros_like(acc_i)
        acc_d[...] = jnp.zeros_like(acc_d)

    gain = gain_ref[1:2, :]
    mixed = o_ref[...]
    middle = x_ref[...].astype(F32) + dot(mixed, wo[...])
    normed, inverse = centre_scale(middle)
    hidden = (normed * gain).astype(BF)
    gate = dot(hidden, wi[:, :FF])
    upward = dot(hidden, wi[:, FF:])
    cdf = 0.5 * (1.0 + lax.erf(gate * 0.7071067811865476))
    gelu = gate * cdf
    slope = cdf + gate * (jnp.exp(-0.5 * gate * gate) * 0.3989422804014327)
    state = (gelu * upward).astype(BF)
    row_at = step * tile + lax.broadcasted_iota(jnp.int32, (tile, 1), 0)
    live = row_at < info[1]
    result = jnp.where(live, middle + dot(state, wd[...]), 0.0).astype(BF)
    for r, out_ref in enumerate((out0, out1, out2, out3)):

        @pl.when(me ^ step == r)
        def _():
            out_ref[...] = result

    branch = jnp.where(live, cot_ref[...].astype(F32), 0.0)
    branch_low = branch.astype(BF)
    acc_d[...] += dot(state, branch_low, TN)
    state_grad = dot(branch_low, wd[...], NT)
    gate_grad = (state_grad * upward * slope).astype(BF)
    up_grad = (state_grad * gelu).astype(BF)
    acc_i[:, :FF] += dot(hidden, gate_grad, TN)
    acc_i[:, FF:] += dot(hidden, up_grad, TN)
    hidden_grad = dot(gate_grad, wi[:, :FF], NT) + dot(up_grad, wi[:, FF:], NT)
    mixer = (branch + norm_back(hidden_grad, normed, inverse, gain)).astype(BF)
    dmid_ref[...] = mixer
    acc_o[...] += dot(mixed, mixer, TN)
    do_ref[...] = (dot(mixer, wo[...], NT) * r_ref[...]).astype(BF)

    @pl.when(step == pl.num_programs(0) - 1)
    def _():
        quarter = share // 4
        for r in range(4):
            owner = me ^ r
            target = send_ref if r % 2 else keep_ref
            mate = r // 2
            for part in range(2):
                for other in range(2):
                    side = info[2] ^ other
                    group, spot = ((2 * (1 - mate), other), (3 - 2 * other, mate))[part]
                    to = slice(spot * quarter, (spot + 1) * quarter)
                    shift = part * half + side * quarter
                    at = pl.ds(pl.multiple_of(owner * share + shift, 16), quarter)
                    target[group, to, :width] = acc_o[at, :].astype(BF)
                    target[group, to, width:base] = acc_i[at, :].astype(BF)
                    at = pl.ds(pl.multiple_of(owner * (3 * half) + shift, 16), quarter)
                    target[group, to, base : base + width] = acc_d[at, :].astype(BF)
                    at = pl.ds(pl.multiple_of(owner * (3 * half) + share + side * quarter, 16), quarter)
                    fold = slice(part * width // 2, (part + 1) * width // 2)
                    target[group, to, base + width :] = acc_d[at, fold].astype(BF)


def feed_call(info, x, mixed, inverse, cot, gain, pieces):
    rows, width = x.shape
    tile = rows // 4
    share = width // 4
    packed = pieces[0].shape[2]
    whole = lambda i, s: (0, 0)
    cube = lambda i, s: (0, 0, 0)
    by_row = lambda i, s: (i, 0)
    block = pl.BlockSpec((tile, width), by_row)
    return pl.pallas_call(
        functools.partial(feed_kernel, tile=tile, share=share),
        grid_spec=pltpu.PrefetchScalarGridSpec(
            num_scalar_prefetch=1,
            grid=(rows // tile,),
            in_specs=[block, block, block, block, pl.BlockSpec((2, width), whole)]
            + [pl.BlockSpec(piece.shape, lambda i, s, n=piece.ndim: (0,) * n) for piece in pieces],
            out_specs=[pl.BlockSpec((tile, width), whole)] * 4
            + [block, block]
            + [pl.BlockSpec((4, share // 2, packed), cube)] * 2,
            scratch_shapes=[
                pltpu.VMEM((width, width), BF),
                pltpu.VMEM((width, 2 * FF), BF),
                pltpu.VMEM((FF, width), BF),
                pltpu.VMEM((width, width), F32),
                pltpu.VMEM((width, 2 * FF), F32),
                pltpu.VMEM((FF, width), F32),
            ],
        ),
        out_shape=[jax.ShapeDtypeStruct((tile, width), BF)] * 4
        + [jax.ShapeDtypeStruct((rows, width), BF)] * 2
        + [jax.ShapeDtypeStruct((4, share // 2, packed), BF)] * 2,
        compiler_params=pltpu.CompilerParams(vmem_limit_bytes=VMEM_BYTES),
        cost_estimate=cost(6 * rows * width * (width + 3 * FF), 130e6),
        name="feed",
    )(info, x, mixed, inverse, cot, gain, *pieces)


def back_kernel(info, qkv_ref, o_ref, do_ref, p_ref, cos_ref, sin_ref, ht_ref, *rest, tile):
    keep_ref, send_ref, joined_ref = rest[-3:]
    rows = qkv_ref.shape[0]
    low = lax.broadcasted_iota(jnp.int32, (1, LANES), 1) < HDIM
    zero = jnp.zeros((), BF)
    keys = qkv_ref[:, LANES : 2 * LANES]
    values = qkv_ref[:, 2 * LANES :]
    key_heads = (jnp.where(low, keys, zero), jnp.where(low, zero, keys))
    key_grads = [None, None]
    value_grads = [None, None]
    query_grads = []
    for part in range(rows // tile):
        at = pl.ds(part * tile, tile)
        queries = qkv_ref[at, :LANES]
        grads = do_ref[at, :]
        wide = grads.astype(F32)
        inner = wide * o_ref[at, :].astype(F32)
        grad_heads = (jnp.where(low, grads, zero), jnp.where(low, zero, grads))
        queries_t = queries.astype(F32).T.astype(BF)
        grads_t = wide.T.astype(BF)
        query_grad = None
        for head in range(2):
            mine = low if head == 0 else jnp.logical_not(low)
            lanes = slice(head * HDIM, (head + 1) * HDIM)
            row_inner = jnp.sum(jnp.where(mine, inner, 0.0), axis=-1, keepdims=True)
            term_grad = dot(grad_heads[head], values, NT)
            terms = p_ref[head, at, :]
            score_grad = (terms.astype(F32) * (term_grad - row_inner)).astype(BF)
            partial = dot(score_grad, key_heads[head])
            query_grad = partial if query_grad is None else query_grad + partial
            for grad_list, left, right in (
                (key_grads, queries_t, score_grad),
                (value_grads, grads_t, terms),
            ):
                value = dot(left[lanes], right)
                grad_list[head] = value if grad_list[head] is None else grad_list[head] + value
        query_grads.append(query_grad)
    cosine = cos_ref[...]
    sine = sin_ref[...]
    query_grad = jnp.concatenate(query_grads, axis=0) * (HDIM**-0.5)
    key_grad = jnp.concatenate(key_grads, axis=0).T
    value_grad = jnp.concatenate(value_grads, axis=0).T
    joined = jnp.concatenate(
        [
            (query_grad * cosine - swap_halves(query_grad) * sine).astype(BF),
            (key_grad * cosine - swap_halves(key_grad) * sine).astype(BF),
            value_grad.astype(BF),
        ],
        axis=1,
    )
    joined_ref[...] = joined
    weight_grad = dot(ht_ref[...], joined).astype(BF)
    share = weight_grad.shape[0] // 4
    me = info[0]
    for owner in range(4):
        rel = me ^ owner
        value = weight_grad[owner * share : (owner + 1) * share, :]
        for target, odd in ((keep_ref, 0), (send_ref, 1)):

            @pl.when(rel % 2 == odd)
            def _():
                for kind in range(3):
                    target[rel // 2, kind] = value[:, kind * LANES : (kind + 1) * LANES]


def back_call(info, qkv, mixed, grads, terms, cosine, sine, hidden_t, start, count, slot, slots, buffers, tile=512):
    rows, width = mixed.shape
    whole = lambda p, s: (0, 0)
    block = pl.BlockSpec((rows, LANES), lambda p, s: (0, start + p))
    wide = pl.BlockSpec((rows, 3 * LANES), lambda p, s: (0, start + p))
    table = pl.BlockSpec((rows, LANES), whole)
    operands = [qkv, mixed, grads, terms, cosine, sine, hidden_t]
    share = width // 4
    piece = pl.BlockSpec((2, 3, share, LANES), lambda p, s: (0, 0, 0, slot + p))
    chunk = jax.ShapeDtypeStruct((2, 3, share, LANES * slots), BF)
    aliases = {}
    for k, buffer in enumerate(buffers):
        aliases[1 + len(operands)] = 3 - len(buffers) + k
        operands.append(buffer)
    return pl.pallas_call(
        functools.partial(back_kernel, tile=tile),
        grid_spec=pltpu.PrefetchScalarGridSpec(
            num_scalar_prefetch=1,
            grid=(count,),
            in_specs=[
                wide,
                block,
                block,
                pl.BlockSpec((2, rows, rows), lambda p, s: (start + p, 0, 0)),
                table,
                table,
                pl.BlockSpec((width, rows), whole),
            ]
            + [pl.BlockSpec(memory_space=pl.ANY)] * len(buffers),
            out_specs=[piece, piece, wide],
        ),
        out_shape=[chunk, chunk, jax.ShapeDtypeStruct((rows, 3 * width), BF)],
        input_output_aliases=aliases,
        compiler_params=pltpu.CompilerParams(vmem_limit_bytes=VMEM_BYTES),
        cost_estimate=cost(20 * rows * rows * LANES * count, 36e6 * count),
        name="back",
    )(info, *operands)


def finish_kernel(info, joined_ref, w_ref, x_ref, dmid_ref, gain_ref, dx0, dx1, dx2, dx3):
    normed, inverse = centre_scale(x_ref[...].astype(F32))
    hidden_grad = dot(joined_ref[...], w_ref[...], NT)
    back = norm_back(hidden_grad, normed, inverse, gain_ref[0:1, :])
    result = (dmid_ref[...].astype(F32) + back).astype(BF)
    for r, dx_ref in enumerate((dx0, dx1, dx2, dx3)):

        @pl.when(info[0] ^ pl.program_id(0) == r)
        def _():
            dx_ref[...] = result


def finish_call(info, joined, weight, x, dmid, gain):
    rows, width = x.shape
    tile = rows // 4
    wide = joined.shape[1]
    by_row = lambda i, s: (i, 0)
    whole = lambda i, s: (0, 0)
    return pl.pallas_call(
        finish_kernel,
        grid_spec=pltpu.PrefetchScalarGridSpec(
            num_scalar_prefetch=1,
            grid=(4,),
            in_specs=[
                pl.BlockSpec((tile, wide), by_row),
                pl.BlockSpec((width, wide), whole),
                pl.BlockSpec((tile, width), by_row),
                pl.BlockSpec((tile, width), by_row),
                pl.BlockSpec((2, width), whole),
            ],
            out_specs=[pl.BlockSpec((tile, width), whole)] * 4,
        ),
        out_shape=[jax.ShapeDtypeStruct((tile, width), BF)] * 4,
        compiler_params=pltpu.CompilerParams(vmem_limit_bytes=VMEM_BYTES),
        cost_estimate=cost(0, 4e6),
        name="finish",
    )(info, joined, weight, x, dmid, gain)


def restore_kernel(info, p0, p1, p2, p3, out_ref):
    for r, piece in enumerate((p0, p1, p2, p3)):
        out_ref[info[0] ^ r] = piece[...].astype(out_ref.dtype)


def restore_call(info, pieces, kind):
    rows, width = pieces[0].shape
    return pl.pallas_call(
        restore_kernel,
        grid_spec=pltpu.PrefetchScalarGridSpec(
            num_scalar_prefetch=1,
            grid=(1,),
            in_specs=[pl.BlockSpec((rows, width), lambda i, s: (0, 0))] * 4,
            out_specs=pl.BlockSpec((4, rows, width), lambda i, s: (0, 0, 0)),
        ),
        out_shape=jax.ShapeDtypeStruct((4, rows, width), kind),
        compiler_params=pltpu.CompilerParams(vmem_limit_bytes=VMEM_BYTES),
        cost_estimate=cost(0, 12e6),
        name="restore",
    )(info, *pieces)


def adam_update(master, gradient, moment_one, moment_two, step_rate, decay_rate):
    first_new = adam_beta * moment_one + (1.0 - adam_beta) * gradient
    second_new = adam_beta * moment_two + (1.0 - adam_beta) * gradient * gradient
    correction = 1.0 - adam_beta**STEP
    direction = first_new / correction / (jnp.sqrt(second_new / correction) + adam_eps)
    renewed = master - step_rate * (direction + decay_rate * master)
    return (renewed, first_new, second_new)


def inward_kernel(grad_ref, master_ref, one_ref, two_ref, *rest):
    renewed_ref, first_ref, second_ref, product_ref = rest[-4:]
    grad = grad_ref[0].astype(F32)
    master = master_ref[...]
    renewed_ref[...], first_ref[...], second_ref[...] = adam_update(
        master, grad, one_ref[...], two_ref[...], rates[0], weight_decay
    )
    product = grad * master.astype(BF).astype(F32)

    @pl.when(pl.program_id(0) == 0)
    def _():
        product_ref[...] = jnp.zeros_like(product_ref)

    for start in range(0, product.shape[1], LANES):
        product_ref[...] += product[:, start : start + LANES]


def inward_call(grad, master, one, two):
    rows, wide = master.shape
    columns = grad.shape[2]
    block = pl.BlockSpec((rows, columns), lambda k: (0, k))
    array = jax.ShapeDtypeStruct((rows, wide), F32)
    return pl.pallas_call(
        inward_kernel,
        grid=(3,),
        in_specs=[pl.BlockSpec((1, rows, columns), lambda k: (k, 0, 0)), block, block, block],
        out_specs=[block, block, block, pl.BlockSpec((rows, LANES), lambda k: (0, 0))],
        out_shape=[array, array, array, jax.ShapeDtypeStruct((rows, LANES), F32)],
        compiler_params=pltpu.CompilerParams(vmem_limit_bytes=VMEM_BYTES),
        cost_estimate=cost(0, 18e6),
        name="inward",
    )(grad, master, one, two)


def others_kernel(side, grad_ref, *refs, width, inner):
    masters = refs[:9]
    results = refs[-10:-1]
    product_ref = refs[-1]
    step = pl.program_id(0)
    base = width + inner

    def update(kind, grad):
        master, one, two = masters[3 * kind : 3 * kind + 3]
        values = adam_update(master[...], grad, one[...], two[...], rates[kind + 1], weight_decay)
        for ref, value in zip(results[3 * kind : 3 * kind + 3], values):
            ref[...] = value

    @pl.when(step < 2)
    def _():
        grad = grad_ref[step].astype(F32)
        update(0, grad[:, :width])
        update(1, grad[:, width:base])
        update(2, grad[:, base : base + width])
        product = grad[:, width:base] * masters[3][...].astype(BF).astype(F32)
        total = product[:, :LANES]
        for start in range(LANES, inner, LANES):
            total = total + product[:, start : start + LANES]
        product_ref[...] = total

    @pl.when(step == 2)
    def _():
        update(2, jnp.concatenate([grad_ref[k, :, base + width :].astype(F32) for k in range(2)], axis=1))


def others_call(side, grad, arrays, buffers):
    quarter = grad.shape[1]
    width = arrays[0].shape[1]
    inner = arrays[3].shape[1]
    short = lambda j, s: (2 * jnp.minimum(j, 1) + s[0], 0)
    full = lambda j, s: (2 * j + s[0], 0)
    blocks = []
    for array, place in zip(arrays, (short,) * 6 + (full,) * 3):
        blocks.append(pl.BlockSpec((quarter, array.shape[1]), place))
    sums = jax.ShapeDtypeStruct((arrays[0].shape[0], LANES), F32)
    return pl.pallas_call(
        functools.partial(others_kernel, width=width, inner=inner),
        grid_spec=pltpu.PrefetchScalarGridSpec(
            num_scalar_prefetch=1,
            grid=(3,),
            in_specs=[pl.BlockSpec(grad.shape, lambda j, s: (0, 0, 0))]
            + blocks
            + [pl.BlockSpec(memory_space=pl.ANY)] * len(buffers),
            out_specs=blocks + [pl.BlockSpec((quarter, LANES), short)],
        ),
        out_shape=[jax.ShapeDtypeStruct(array.shape, F32) for array in arrays] + [sums],
        input_output_aliases={11 + k: k for k in range(len(buffers))},
        compiler_params=pltpu.CompilerParams(vmem_limit_bytes=VMEM_BYTES),
        cost_estimate=cost(0, 14e6),
        name="others",
    )(side, grad, *arrays, *buffers)


def tables(seq_total):
    lane = jnp.arange(LANES, dtype=jnp.int32)
    exponent = (lane % (HDIM // 2)).astype(F32) * (2.0 / HDIM)
    inverse = jnp.power(jnp.float32(rope_base), -exponent)
    angles = jnp.arange(seq_total, dtype=F32)[:, None] * inverse[None, :]
    sign = jnp.where(lane % HDIM < HDIM // 2, -1.0, 1.0).astype(F32)
    return jnp.cos(angles), jnp.sin(angles) * sign[None, :]


CORE = [(0, 1), (1, 0), (2, 3), (3, 2)]
CROSS = [(0, 2), (1, 3), (2, 0), (3, 1)]
tie = lax.optimization_barrier


def over_core(array):
    return lax.ppermute(array, "fsdp", CORE)


def over_cross(array):
    return lax.ppermute(array, "fsdp", CROSS)


def over_side(array):
    return lax.ppermute(array, "dp", [(k, k ^ 1) for k in range(lax.axis_size("dp"))])


def along_line(array, groups=None):
    return lax.all_to_all(array, "dp", 0, 0, axis_index_groups=groups)


def add_low(left, right):
    return (left.astype(F32) + right.astype(F32)).astype(BF)


def sum_low(array):
    return jnp.sum(array.astype(F32), axis=0).astype(BF)


def pick_half(array, index, axis=0):
    return lax.dynamic_index_in_dim(array, index, axis, keepdims=False)


def local(
    tokens, cotangent, lengths,
    inward_weight, outward_weight, expand_weight, shrink_weight, gain_weight,
    inward_first, outward_first, expand_first, shrink_first, gain_first,
    inward_second, outward_second, expand_second, shrink_second, gain_second,
):
    micro_count, group_size, local_len, width = tokens.shape
    fsdp = lax.axis_size("fsdp")
    lines = lax.axis_size("dp")
    assert fsdp == 4 and micro_count * group_size == fsdp and lines % 4 == 0
    seq_total = local_len * fsdp
    share, wide = inward_weight.shape
    half = share // 2
    me = lax.axis_index("fsdp").astype(jnp.int32)
    side = (lax.axis_index("dp") % 2).astype(jnp.int32)
    fourth = (lax.axis_index("dp") % 4).astype(jnp.int32)
    info = jnp.stack([me, pick_half(lengths.reshape(fsdp), me), side, fourth])
    columns = [[k for k in range(lines) if k % 2 == odd] for odd in range(2)]

    def to_sequence(array):
        array = array.reshape(fsdp, local_len, width)
        return lax.all_to_all(array, "fsdp", 0, 0).reshape(seq_total, width)

    def around(array):
        return [array] + [lax.ppermute(array, "dp", [(d, d ^ k) for d in range(lines)]) for k in range(1, 4)]

    def with_gains(weight, gains):
        gains = jnp.pad(gains.astype(BF)[:, None, :], ((0, 0), (0, 7), (0, wide - share)))
        return jnp.concatenate([weight.astype(BF), gains], axis=1)

    inward_parts = inward_weight.reshape(4, half // 2, wide)
    gain_parts = jnp.pad(gain_weight, ((0, 2), (0, 0)))
    leaving = with_gains(pick_half(inward_parts, fourth)[None], pick_half(gain_parts, fourth)[None])[0]
    far = over_cross(leaving)

    (inward_parts, outward, leaving) = tie((inward_parts, outward_weight, leaving))
    own = with_gains(inward_parts, gain_parts)
    near = over_core(own)
    tokens, own = tie((tokens, own))
    x = to_sequence(tokens)
    shrink_low = shrink_weight.astype(BF)
    folded = jnp.concatenate([shrink_low[share:, : width // 2], shrink_low[share:, width // 2 :]], axis=0)
    packed = jnp.concatenate(
        [outward.astype(BF), expand_weight.astype(BF), shrink_low[:share], folded], axis=1
    ).reshape(4, half // 2, -1)
    cosine, sine = tables(seq_total)
    leaving = pick_half(packed, fourth)
    far = around(far)
    far, cosine, sine, info, packed, leaving = tie((far, cosine, sine, info, packed, leaving))
    inward_pieces = (own, near, *far, *[over_core(piece) for piece in far])

    leaving, x = tie((leaving, x))
    other_far = over_cross(leaving)
    other_near = over_core(packed)

    hidden_t, qkv, weight, gain = qkv_call(info, x, cosine, sine, inward_pieces)
    cotangent, other_far, qkv = tie((cotangent, other_far, qkv))
    other_far = around(other_far)
    cot = to_sequence(cotangent)
    mixed, inverse, terms = attend_call(info, qkv, 0, PAIRS, ())
    mixed, other_far = tie((mixed, other_far))
    other_pieces = (packed, other_near, *other_far, *[over_core(piece) for piece in other_far])
    *out, middle_grad, grads, keep, send = feed_call(info, x, mixed, inverse, cot, gain, other_pieces)

    def back(start, count, slot, slots, buffers):
        return back_call(
            info, qkv, mixed, grads, terms, cosine, sine, hidden_t, start, count, slot, slots, buffers
        )

    quarter = half // 2
    level = lines // 2
    line_at = lax.axis_index("dp") // 2

    def over_line(array, gap):
        return lax.ppermute(array, "dp", [(k, k ^ (2 * gap)) for k in range(lines)])

    def halve(array, gap):
        array = array.reshape((array.shape[0] // 2, 2) + array.shape[1:])
        bit = (line_at // gap) % 2
        came = over_line(pick_half(array, 1 - bit, 1), gap)
        return pick_half(array, bit, 1), came

    def in_order(mine, other, gap):
        bit = (line_at // gap) % 2
        pair = jnp.stack([jnp.where(bit == 0, mine, other), jnp.where(bit == 0, other, mine)], axis=1)
        return pair.reshape((-1,) + mine.shape[1:])

    def add(*parts):
        total = parts[0].astype(F32)
        for part in parts[1:]:
            total = total + part.astype(F32)
        return total.astype(BF)

    came = over_core(send)
    keep_x, send_x, joined = back(0, 2, 0, 2, ())
    leave_y = add(keep[0], came[0])
    leave_x = add(keep[1], came[1])
    leave_y, leave_x, joined = tie((leave_y, leave_x, joined))
    first_y = over_cross(leave_y)
    second_x = over_side(leave_x)
    came_x = over_core(send_x)
    keep_v, send_v, joined = back(2, 3, 0, 3, (joined,))
    leave_x = add(keep[2, quarter:], came[2, quarter:], first_y[quarter:])
    leave_y = add(keep[3, quarter:], came[3, quarter:], second_x[quarter:])
    leave_x, leave_y, came_x, out, joined = tie((leave_x, leave_y, came_x, out, joined))
    first_x = over_side(leave_x)
    second_y = over_cross(leave_y)
    came_v = over_core(send_v)
    near_out = over_core(out[1])
    turned_out = over_core(out[3])
    keep_z, send_z, joined = back(5, 1, 0, 1, (joined,))

    came_z = over_core(send_z)
    first = add(keep[2, :quarter], came[2, :quarter], first_y[:quarter], first_x)
    second = add(keep[3, :quarter], came[3, :quarter], second_x[:quarter], second_y)
    both = jnp.concatenate([first, second], axis=0).reshape(level, half // level, -1)
    both, keep_z, near_out, turned_out, came_v = tie((both, keep_z, near_out, turned_out, came_v))
    far_x = over_cross(add(keep_x[1], came_x[1]))
    far_v = over_cross(add(keep_v[1], came_v[1]))
    gap = 1
    stay, moved = halve(both, gap)
    leave_y = add(keep_z[1], came_z[1])
    far_z = over_cross(leave_y)
    while gap * 2 < level:
        stay, moved, leave_y, out = tie((stay, moved, leave_y, out))
        both = add(stay, moved)
        gap = gap * 2
        stay, moved = halve(both, gap)
    stay, leave_y, out, turned_out = tie((stay, leave_y, out, turned_out))
    far_out = over_cross(out[2])
    diagonal_out = over_cross(turned_out)
    moved, far_x, far_v, far_z = tie((moved, far_x, far_v, far_z))
    chunk = jnp.concatenate(
        [add(keep_x[0], came_x[0], far_x), add(keep_v[0], came_v[0], far_v), add(keep_z[0], came_z[0], far_z)], axis=2
    )
    both = add(stay, moved)
    chunk_shape = chunk.shape
    by_line = (lines, 3 * share // lines, chunk_shape[2])
    chunk, both, joined = tie((chunk, both, joined))
    chunk = along_line(chunk.reshape(by_line))
    moved = over_line(both, gap)
    input_low = finish_call(info, joined, weight, x, middle_grad, gain)
    moved, far_out, diagonal_out, input_low = tie((moved, far_out, diagonal_out, input_low))
    both = in_order(both, moved, gap)
    while gap > 2:
        gap = gap // 2
        both = in_order(both, over_line(both, gap), gap)
    both, info_out = tie((both, info))
    block_out = restore_call(info_out, (out[0], near_out, far_out, diagonal_out), BF).reshape(tokens.shape)
    moved = over_line(both, 1)
    far_low = over_cross(input_low[2])
    chunk, far_low, input_low, block_out = tie((chunk, far_low, input_low, block_out))
    chunk = sum_low(chunk)
    near_low = over_core(input_low[1])
    turned_low = over_core(input_low[3])
    chunk, info_in = tie((chunk, info))
    spread = along_line(jnp.broadcast_to(chunk[None], by_line)).reshape(chunk_shape)
    moved, turned_low, near_low = tie((moved, turned_low, near_low))
    both = in_order(both, moved, 1)
    other = over_side(both)
    diagonal_low = over_cross(turned_low)
    pieces = (input_low[0], near_low, far_low, diagonal_low)
    input_grad = restore_call(info_in, pieces, F32).reshape(tokens.shape)

    arrays = (
        outward_weight, outward_first, outward_second,
        expand_weight, expand_first, expand_second,
        shrink_weight, shrink_first, shrink_second,
    )
    own_side = side.reshape(1)
    other_side = (1 - side).reshape(1)
    others_new = others_call(own_side, both.reshape(2, quarter, -1), arrays, ())
    *inward_new, product = inward_call(spread, inward_weight, inward_first, inward_second)
    other, product = tie((other, product))
    *others_new, expand_product = others_call(other_side, other.reshape(2, quarter, -1), arrays, others_new)
    own_gain = gain_weight.astype(BF).astype(F32)
    gain_grad = jnp.stack(
        [
            jnp.sum(product, axis=1),
            jnp.sum(expand_product, axis=1),
        ]
    ) / own_gain

    results = [block_out, input_grad]
    results += inward_new
    results += others_new
    results += adam_update(gain_weight, gain_grad, gain_first, gain_second, rates[4], 0.0)
    return tuple(results)


def solution(mesh):
    split = P(None, "dp", "fsdp", None)
    rows = P("fsdp", None)
    columns = P(None, "fsdp")
    kinds = (rows, rows, rows, rows, columns)
    in_specs = (split, split, P(None, "dp")) + kinds * 3
    out_specs = (split, split) + (rows,) * 12 + (columns,) * 3
    return jax.shard_map(local, mesh=mesh, in_specs=in_specs, out_specs=out_specs, check_vma=False)
```

```python
import functools

import jax
import jax.numpy as jnp
from jax import lax
from jax.experimental import pallas as pl
from jax.experimental.pallas import tpu as pltpu
from jax.sharding import PartitionSpec as P

FF = 1152
HEADS = 12
HDIM = 64
STEP = 10

rope_base = 160000.0
norm_eps = 1e-05
adam_beta = 0.5
adam_eps = 1e-08
weight_decay = 0.01
rates = (0.07, 2.0, 0.07, 0.06, 0.2)
masked_score = -1e30
small_score = 50.0

BF = jnp.bfloat16
F32 = jnp.float32
NN = (((1,), (0,)), ((), ()))
NT = (((1,), (1,)), ((), ()))
TN = (((0,), (0,)), ((), ()))
VMEM_BYTES = 58 << 20
LANES = 128
PAIRS = HEADS * HDIM // LANES


def cost(flops, size):
    return pl.CostEstimate(flops=int(flops), bytes_accessed=int(size), transcendentals=0)


def dot(left, right, dims=NN):
    return lax.dot_general(left, right, dims, preferred_element_type=F32)


def swap_halves(values):
    lane = lax.broadcasted_iota(jnp.int32, (1, LANES), 1)
    former = lax.rem(lane, HDIM) < HDIM // 2
    ahead = pltpu.roll(values, LANES - HDIM // 2, 1)
    behind = pltpu.roll(values, HDIM // 2, 1)
    return jnp.where(former, ahead, behind)


def centre_scale(values):
    center = values - jnp.mean(values, axis=-1, keepdims=True)
    spread = jnp.mean(center * center, axis=-1, keepdims=True)
    inverse = lax.rsqrt(spread + norm_eps)
    return center * inverse, inverse


def norm_back(grad, normed, inverse, gain):
    scaled = grad * gain
    mean_one = jnp.mean(scaled, axis=-1, keepdims=True)
    mean_two = jnp.mean(scaled * normed, axis=-1, keepdims=True)
    return inverse * (scaled - mean_one - normed * mean_two)


def quarters(refs):
    own, near = refs[:2]
    return tuple(tuple(ref.at[k] for k in range(4)) for ref in (own, near)) + (refs[2:6], refs[6:10])


def place(scratch, pieces, info, rows):
    quarter = rows // 4
    for r, piece in enumerate(pieces):
        owner = info[0] ^ r
        for k, ref in enumerate(piece):
            side = k if r < 2 else info[3] ^ k
            at = pl.ds(pl.multiple_of(owner * rows + side * quarter, 16), quarter)
            for pair in range(PAIRS):
                for kind in range(3):
                    source = (kind * PAIRS + pair) * LANES
                    target = (pair * 3 + kind) * LANES
                    scratch[at, target : target + LANES] = ref[:quarter, source : source + LANES]


def pick(index, choices):
    value = choices[-1]
    for k in range(len(choices) - 2, -1, -1):
        value = jnp.where(index == k, choices[k], value)
    return value


def qkv_kernel(info, x_ref, cos_ref, sin_ref, *refs, share):
    ht_ref, qkv_ref, w_ref, gain_ref = refs[-4:]

    @pl.when(pl.program_id(0) == 0)
    def _():
        pieces = quarters(refs[:10])
        place(w_ref, pieces, info, share)
        quarter = share // 4
        for row in range(2):
            found = []
            for r, piece in enumerate(pieces):
                rows = [ref[quarter : quarter + 1, :share].astype(F32) for ref in piece]
                found.append(rows[row] if r < 2 else pick(info[3] ^ row, rows))
            ordered = [pick(info[0] ^ owner, found) for owner in range(4)]
            gain_ref[row : row + 1, :] = jnp.concatenate(ordered, axis=1)

    normed, unused = centre_scale(x_ref[...].astype(F32))
    low = (normed * gain_ref[0:1, :]).astype(BF)
    ht_ref[...] = low.T
    cosine = cos_ref[...]
    sine = sin_ref[...]
    for pair in range(PAIRS):
        start = pair * 3 * LANES
        if pair % 2 == 0:
            joined = dot(low, w_ref[:, start : start + 6 * LANES])
        for kind in range(3):
            at = (pair % 2 * 3 + kind) * LANES
            block = joined[:, at : at + LANES]
            if kind < 2:
                block = block * cosine + swap_halves(block) * sine
            block = block.astype(BF)
            if kind == 0:
                block = block * jnp.asarray(HDIM**-0.5, BF)
            qkv_ref[:, start + kind * LANES : start + (kind + 1) * LANES] = block


def qkv_call(info, x, cosine, sine, pieces, tile=256):
    rows, width = x.shape
    wide = pieces[0].shape[2]
    whole = lambda i, s: (0, 0)
    by_row = lambda i, s: (i, 0)
    return pl.pallas_call(
        functools.partial(qkv_kernel, share=width // 4),
        grid_spec=pltpu.PrefetchScalarGridSpec(
            num_scalar_prefetch=1,
            grid=(rows // tile,),
            in_specs=[
                pl.BlockSpec((tile, width), by_row),
                pl.BlockSpec((tile, LANES), by_row),
                pl.BlockSpec((tile, LANES), by_row),
            ]
            + [pl.BlockSpec(piece.shape, lambda i, s, n=piece.ndim: (0,) * n) for piece in pieces],
            out_specs=[
                pl.BlockSpec((width, tile), lambda i, s: (0, i)),
                pl.BlockSpec((tile, wide), by_row),
                pl.BlockSpec((width, wide), whole),
                pl.BlockSpec((2, width), whole),
            ],
        ),
        out_shape=[
            jax.ShapeDtypeStruct((width, rows), BF),
            jax.ShapeDtypeStruct((rows, wide), BF),
            jax.ShapeDtypeStruct((width, wide), BF),
            jax.ShapeDtypeStruct((2, width), F32),
        ],
        compiler_params=pltpu.CompilerParams(vmem_limit_bytes=VMEM_BYTES),
        cost_estimate=cost(2 * rows * width * wide, 36e6),
        name="qkv",
    )(info, x, cosine, sine, *pieces)


def attend_kernel(info, qkv_ref, *rest, tile):
    o_ref, r_ref, p_ref = rest[-3:]
    rows = qkv_ref.shape[0]
    key_at = lax.broadcasted_iota(jnp.int32, (1, rows), 1)
    bias = jnp.where(key_at < info[1], 0.0, masked_score).astype(F32)
    keys = qkv_ref[:, LANES : 2 * LANES]
    values = qkv_ref[:, 2 * LANES :]
    low = lax.broadcasted_iota(jnp.int32, (1, LANES), 1) < HDIM
    one = jnp.ones((), BF)
    zero = jnp.zeros((), BF)
    sides = (jnp.where(low, values, one), jnp.where(low, one, values))
    def heads_of(at):
        queries = qkv_ref[at, :LANES]
        return jnp.where(low, queries, zero), jnp.where(low, zero, queries)

    def finish(at, outs):
        mixed = jnp.where(low, outs[0], outs[1])
        total = pltpu.roll(jnp.where(low, outs[1], outs[0]), HDIM, 1)
        inverse = 1.0 / total
        o_ref[at, :] = (mixed * inverse).astype(BF)
        r_ref[at, :] = inverse

    mine = lax.broadcasted_iota(jnp.int32, (LANES, LANES), 0) // HDIM
    same = mine == lax.broadcasted_iota(jnp.int32, (LANES, LANES), 1) // HDIM
    same = same.astype(BF)

    def longest(values):
        return jnp.max(dot(values * values, same), axis=0, keepdims=True)

    bound = jnp.max(longest(qkv_ref[:, :LANES]) * longest(keys))

    @pl.when(bound < small_score * small_score)
    def _():
        for step in range(rows // tile):
            at = pl.ds(step * tile, tile)
            outs = []
            for head, queries in enumerate(heads_of(at)):
                terms = jnp.exp(dot(queries, keys, NT) + bias).astype(BF)
                p_ref[head, at, :] = terms
                outs.append(dot(terms, sides[head]))
            finish(at, outs)

    @pl.when(jnp.logical_not(bound < small_score * small_score))
    def _():
        some = 128

        def body(step, unused):
            at = pl.ds(pl.multiple_of(step * some, some), some)
            outs = []
            for head, queries in enumerate(heads_of(at)):
                scores = dot(queries, keys, NT) + bias
                peak = jnp.max(scores, axis=-1, keepdims=True)
                terms = jnp.exp(scores - peak).astype(BF)
                p_ref[head, at, :] = terms
                outs.append(dot(terms, sides[head]))
            finish(at, outs)
            return unused

        lax.fori_loop(0, rows // some, body, 0)


def attend_call(info, qkv, start, count, buffers, tile=512):
    rows = qkv.shape[0]
    width = qkv.shape[1] // 3
    block = pl.BlockSpec((rows, LANES), lambda p, s: (0, start + p))
    buffers = tuple(buffers)
    return pl.pallas_call(
        functools.partial(attend_kernel, tile=tile),
        grid_spec=pltpu.PrefetchScalarGridSpec(
            num_scalar_prefetch=1,
            grid=(count,),
            in_specs=[pl.BlockSpec((rows, 3 * LANES), lambda p, s: (0, start + p))]
            + [pl.BlockSpec(memory_space=pl.ANY)] * len(buffers),
            out_specs=[
                block,
                block,
                pl.BlockSpec((2, rows, rows), lambda p, s: (start + p, 0, 0)),
            ],
        ),
        out_shape=[
            jax.ShapeDtypeStruct((rows, width), BF),
            jax.ShapeDtypeStruct((rows, width), F32),
            jax.ShapeDtypeStruct((HEADS, rows, rows), BF),
        ],
        input_output_aliases={2 + k: k for k in range(len(buffers))},
        compiler_params=pltpu.CompilerParams(vmem_limit_bytes=VMEM_BYTES),
        cost_estimate=cost(16 * rows * rows * LANES * count, 17e6 * count),
        name="attend",
    )(info, qkv, *buffers)


def feed_kernel(
    info, x_ref, o_ref, r_ref, cot_ref, gain_ref, m0, m1, m2, m3, m4, m5, m6, m7, m8, m9,
    out0, out1, out2, out3, dmid_ref, do_ref, keep_ref, send_ref,
    wo, wi, wd, acc_o, acc_i, acc_d, *, tile, share,
):
    step = pl.program_id(0)
    me = info[0]
    width = x_ref.shape[1]
    inner = wi.shape[1]
    base = width + inner
    half = share // 2

    @pl.when(step == 0)
    def _():
        fourth = share // 4
        for r, piece in enumerate(quarters((m0, m1, m2, m3, m4, m5, m6, m7, m8, m9))):
            owner = me ^ r
            for k, ref in enumerate(piece):
                side = k if r < 2 else info[3] ^ k
                at = pl.ds(pl.multiple_of(owner * share + side * fourth, 16), fourth)
                wo[at, :] = ref[:, :width]
                wi[at, :] = ref[:, width:base]
                down = owner * (3 * half)
                at = pl.ds(pl.multiple_of(down + side * fourth, 16), fourth)
                wd[at, :] = ref[:, base : base + width]
                at = pl.ds(pl.multiple_of(down + share + side % 2 * fourth, 16), fourth)
                fold = pl.ds(pl.multiple_of(side // 2 * (width // 2), LANES), width // 2)
                wd[at, fold] = ref[:, base + width :]

        acc_o[...] = jnp.zeros_like(acc_o)
        acc_i[...] = jnp.zeros_like(acc_i)
        acc_d[...] = jnp.zeros_like(acc_d)

    gain = gain_ref[1:2, :]
    mixed = o_ref[...]
    middle = x_ref[...].astype(F32) + dot(mixed, wo[...])
    normed, inverse = centre_scale(middle)
    hidden = (normed * gain).astype(BF)
    gate = dot(hidden, wi[:, :FF])
    upward = dot(hidden, wi[:, FF:])
    cdf = 0.5 * (1.0 + lax.erf(gate * 0.7071067811865476))
    gelu = gate * cdf
    slope = cdf + gate * (jnp.exp(-0.5 * gate * gate) * 0.3989422804014327)
    state = (gelu * upward).astype(BF)
    row_at = step * tile + lax.broadcasted_iota(jnp.int32, (tile, 1), 0)
    live = row_at < info[1]
    result = jnp.where(live, middle + dot(state, wd[...]), 0.0).astype(BF)
    for r, out_ref in enumerate((out0, out1, out2, out3)):

        @pl.when(me ^ step == r)
        def _():
            out_ref[...] = result

    branch = jnp.where(live, cot_ref[...].astype(F32), 0.0)
    branch_low = branch.astype(BF)
    acc_d[...] += dot(state, branch_low, TN)
    state_grad = dot(branch_low, wd[...], NT)
    gate_grad = (state_grad * upward * slope).astype(BF)
    up_grad = (state_grad * gelu).astype(BF)
    acc_i[:, :FF] += dot(hidden, gate_grad, TN)
    acc_i[:, FF:] += dot(hidden, up_grad, TN)
    hidden_grad = dot(gate_grad, wi[:, :FF], NT) + dot(up_grad, wi[:, FF:], NT)
    mixer = (branch + norm_back(hidden_grad, normed, inverse, gain)).astype(BF)
    dmid_ref[...] = mixer
    acc_o[...] += dot(mixed, mixer, TN)
    do_ref[...] = (dot(mixer, wo[...], NT) * r_ref[...]).astype(BF)

    @pl.when(step == pl.num_programs(0) - 1)
    def _():
        quarter = share // 4
        for r in range(4):
            owner = me ^ r
            target = send_ref if r % 2 else keep_ref
            mate = r // 2
            for part in range(2):
                for other in range(2):
                    side = info[2] ^ other
                    group, spot = ((2 * (1 - mate), other), (3 - 2 * other, mate))[part]
                    to = slice(spot * quarter, (spot + 1) * quarter)
                    shift = part * half + side * quarter
                    at = pl.ds(pl.multiple_of(owner * share + shift, 16), quarter)
                    target[group, to, :width] = acc_o[at, :].astype(BF)
                    target[group, to, width:base] = acc_i[at, :].astype(BF)
                    at = pl.ds(pl.multiple_of(owner * (3 * half) + shift, 16), quarter)
                    target[group, to, base : base + width] = acc_d[at, :].astype(BF)
                    at = pl.ds(pl.multiple_of(owner * (3 * half) + share + side * quarter, 16), quarter)
                    fold = slice(part * width // 2, (part + 1) * width // 2)
                    target[group, to, base + width :] = acc_d[at, fold].astype(BF)


def feed_call(info, x, mixed, inverse, cot, gain, pieces):
    rows, width = x.shape
    tile = rows // 4
    share = width // 4
    packed = pieces[0].shape[2]
    whole = lambda i, s: (0, 0)
    cube = lambda i, s: (0, 0, 0)
    by_row = lambda i, s: (i, 0)
    block = pl.BlockSpec((tile, width), by_row)
    return pl.pallas_call(
        functools.partial(feed_kernel, tile=tile, share=share),
        grid_spec=pltpu.PrefetchScalarGridSpec(
            num_scalar_prefetch=1,
            grid=(rows // tile,),
            in_specs=[block, block, block, block, pl.BlockSpec((2, width), whole)]
            + [pl.BlockSpec(piece.shape, lambda i, s, n=piece.ndim: (0,) * n) for piece in pieces],
            out_specs=[pl.BlockSpec((tile, width), whole)] * 4
            + [block, block]
            + [pl.BlockSpec((4, share // 2, packed), cube)] * 2,
            scratch_shapes=[
                pltpu.VMEM((width, width), BF),
                pltpu.VMEM((width, 2 * FF), BF),
                pltpu.VMEM((FF, width), BF),
                pltpu.VMEM((width, width), F32),
                pltpu.VMEM((width, 2 * FF), F32),
                pltpu.VMEM((FF, width), F32),
            ],
        ),
        out_shape=[jax.ShapeDtypeStruct((tile, width), BF)] * 4
        + [jax.ShapeDtypeStruct((rows, width), BF)] * 2
        + [jax.ShapeDtypeStruct((4, share // 2, packed), BF)] * 2,
        compiler_params=pltpu.CompilerParams(vmem_limit_bytes=VMEM_BYTES),
        cost_estimate=cost(6 * rows * width * (width + 3 * FF), 130e6),
        name="feed",
    )(info, x, mixed, inverse, cot, gain, *pieces)


def back_kernel(info, qkv_ref, o_ref, do_ref, p_ref, cos_ref, sin_ref, ht_ref, *rest, tile):
    keep_ref, send_ref, joined_ref = rest[-3:]
    rows = qkv_ref.shape[0]
    low = lax.broadcasted_iota(jnp.int32, (1, LANES), 1) < HDIM
    zero = jnp.zeros((), BF)
    keys = qkv_ref[:, LANES : 2 * LANES]
    values = qkv_ref[:, 2 * LANES :]
    key_heads = (jnp.where(low, keys, zero), jnp.where(low, zero, keys))
    key_grads = [None, None]
    value_grads = [None, None]
    query_grads = []
    for part in range(rows // tile):
        at = pl.ds(part * tile, tile)
        queries = qkv_ref[at, :LANES]
        grads = do_ref[at, :]
        wide = grads.astype(F32)
        inner = wide * o_ref[at, :].astype(F32)
        grad_heads = (jnp.where(low, grads, zero), jnp.where(low, zero, grads))
        queries_t = queries.astype(F32).T.astype(BF)
        grads_t = wide.T.astype(BF)
        query_grad = None
        for head in range(2):
            mine = low if head == 0 else jnp.logical_not(low)
            lanes = slice(head * HDIM, (head + 1) * HDIM)
            row_inner = jnp.sum(jnp.where(mine, inner, 0.0), axis=-1, keepdims=True)
            term_grad = dot(grad_heads[head], values, NT)
            terms = p_ref[head, at, :]
            score_grad = (terms.astype(F32) * (term_grad - row_inner)).astype(BF)
            partial = dot(score_grad, key_heads[head])
            query_grad = partial if query_grad is None else query_grad + partial
            for grad_list, left, right in (
                (key_grads, queries_t, score_grad),
                (value_grads, grads_t, terms),
            ):
                value = dot(left[lanes], right)
                grad_list[head] = value if grad_list[head] is None else grad_list[head] + value
        query_grads.append(query_grad)
    cosine = cos_ref[...]
    sine = sin_ref[...]
    query_grad = jnp.concatenate(query_grads, axis=0) * (HDIM**-0.5)
    key_grad = jnp.concatenate(key_grads, axis=0).T
    value_grad = jnp.concatenate(value_grads, axis=0).T
    joined = jnp.concatenate(
        [
            (query_grad * cosine - swap_halves(query_grad) * sine).astype(BF),
            (key_grad * cosine - swap_halves(key_grad) * sine).astype(BF),
            value_grad.astype(BF),
        ],
        axis=1,
    )
    joined_ref[...] = joined
    weight_grad = dot(ht_ref[...], joined).astype(BF)
    share = weight_grad.shape[0] // 4
    me = info[0]
    for owner in range(4):
        rel = me ^ owner
        value = weight_grad[owner * share : (owner + 1) * share, :]
        for target, odd in ((keep_ref, 0), (send_ref, 1)):

            @pl.when(rel % 2 == odd)
            def _():
                for kind in range(3):
                    target[rel // 2, kind] = value[:, kind * LANES : (kind + 1) * LANES]


def back_call(info, qkv, mixed, grads, terms, cosine, sine, hidden_t, start, count, slot, slots, buffers, tile=512):
    rows, width = mixed.shape
    whole = lambda p, s: (0, 0)
    block = pl.BlockSpec((rows, LANES), lambda p, s: (0, start + p))
    wide = pl.BlockSpec((rows, 3 * LANES), lambda p, s: (0, start + p))
    table = pl.BlockSpec((rows, LANES), whole)
    operands = [qkv, mixed, grads, terms, cosine, sine, hidden_t]
    share = width // 4
    piece = pl.BlockSpec((2, 3, share, LANES), lambda p, s: (0, 0, 0, slot + p))
    chunk = jax.ShapeDtypeStruct((2, 3, share, LANES * slots), BF)
    aliases = {}
    for k, buffer in enumerate(buffers):
        aliases[1 + len(operands)] = 3 - len(buffers) + k
        operands.append(buffer)
    return pl.pallas_call(
        functools.partial(back_kernel, tile=tile),
        grid_spec=pltpu.PrefetchScalarGridSpec(
            num_scalar_prefetch=1,
            grid=(count,),
            in_specs=[
                wide,
                block,
                block,
                pl.BlockSpec((2, rows, rows), lambda p, s: (start + p, 0, 0)),
                table,
                table,
                pl.BlockSpec((width, rows), whole),
            ]
            + [pl.BlockSpec(memory_space=pl.ANY)] * len(buffers),
            out_specs=[piece, piece, wide],
        ),
        out_shape=[chunk, chunk, jax.ShapeDtypeStruct((rows, 3 * width), BF)],
        input_output_aliases=aliases,
        compiler_params=pltpu.CompilerParams(vmem_limit_bytes=VMEM_BYTES),
        cost_estimate=cost(20 * rows * rows * LANES * count, 36e6 * count),
        name="back",
    )(info, *operands)


def finish_kernel(info, joined_ref, w_ref, x_ref, dmid_ref, gain_ref, dx0, dx1, dx2, dx3):
    normed, inverse = centre_scale(x_ref[...].astype(F32))
    hidden_grad = dot(joined_ref[...], w_ref[...], NT)
    back = norm_back(hidden_grad, normed, inverse, gain_ref[0:1, :])
    result = (dmid_ref[...].astype(F32) + back).astype(BF)
    for r, dx_ref in enumerate((dx0, dx1, dx2, dx3)):

        @pl.when(info[0] ^ pl.program_id(0) == r)
        def _():
            dx_ref[...] = result


def finish_call(info, joined, weight, x, dmid, gain):
    rows, width = x.shape
    tile = rows // 4
    wide = joined.shape[1]
    by_row = lambda i, s: (i, 0)
    whole = lambda i, s: (0, 0)
    return pl.pallas_call(
        finish_kernel,
        grid_spec=pltpu.PrefetchScalarGridSpec(
            num_scalar_prefetch=1,
            grid=(4,),
            in_specs=[
                pl.BlockSpec((tile, wide), by_row),
                pl.BlockSpec((width, wide), whole),
                pl.BlockSpec((tile, width), by_row),
                pl.BlockSpec((tile, width), by_row),
                pl.BlockSpec((2, width), whole),
            ],
            out_specs=[pl.BlockSpec((tile, width), whole)] * 4,
        ),
        out_shape=[jax.ShapeDtypeStruct((tile, width), BF)] * 4,
        compiler_params=pltpu.CompilerParams(vmem_limit_bytes=VMEM_BYTES),
        cost_estimate=cost(0, 4e6),
        name="finish",
    )(info, joined, weight, x, dmid, gain)


def restore_kernel(info, p0, p1, p2, p3, out_ref):
    for r, piece in enumerate((p0, p1, p2, p3)):
        out_ref[info[0] ^ r] = piece[...].astype(out_ref.dtype)


def restore_call(info, pieces, kind):
    rows, width = pieces[0].shape
    return pl.pallas_call(
        restore_kernel,
        grid_spec=pltpu.PrefetchScalarGridSpec(
            num_scalar_prefetch=1,
            grid=(1,),
            in_specs=[pl.BlockSpec((rows, width), lambda i, s: (0, 0))] * 4,
            out_specs=pl.BlockSpec((4, rows, width), lambda i, s: (0, 0, 0)),
        ),
        out_shape=jax.ShapeDtypeStruct((4, rows, width), kind),
        compiler_params=pltpu.CompilerParams(vmem_limit_bytes=VMEM_BYTES),
        cost_estimate=cost(0, 12e6),
        name="restore",
    )(info, *pieces)


def adam_update(master, gradient, moment_one, moment_two, step_rate, decay_rate):
    first_new = adam_beta * moment_one + (1.0 - adam_beta) * gradient
    second_new = adam_beta * moment_two + (1.0 - adam_beta) * gradient * gradient
    correction = 1.0 - adam_beta**STEP
    direction = first_new / correction / (jnp.sqrt(second_new / correction) + adam_eps)
    renewed = master - step_rate * (direction + decay_rate * master)
    return (renewed, first_new, second_new)


def inward_kernel(grad_ref, master_ref, one_ref, two_ref, *rest):
    renewed_ref, first_ref, second_ref, product_ref = rest[-4:]
    grad = grad_ref[0].astype(F32)
    master = master_ref[...]
    renewed_ref[...], first_ref[...], second_ref[...] = adam_update(
        master, grad, one_ref[...], two_ref[...], rates[0], weight_decay
    )
    product = grad * master.astype(BF).astype(F32)

    @pl.when(pl.program_id(0) == 0)
    def _():
        product_ref[...] = jnp.zeros_like(product_ref)

    for start in range(0, product.shape[1], LANES):
        product_ref[...] += product[:, start : start + LANES]


def inward_call(grad, master, one, two):
    rows, wide = master.shape
    columns = grad.shape[2]
    block = pl.BlockSpec((rows, columns), lambda k: (0, k))
    array = jax.ShapeDtypeStruct((rows, wide), F32)
    return pl.pallas_call(
        inward_kernel,
        grid=(3,),
        in_specs=[pl.BlockSpec((1, rows, columns), lambda k: (k, 0, 0)), block, block, block],
        out_specs=[block, block, block, pl.BlockSpec((rows, LANES), lambda k: (0, 0))],
        out_shape=[array, array, array, jax.ShapeDtypeStruct((rows, LANES), F32)],
        compiler_params=pltpu.CompilerParams(vmem_limit_bytes=VMEM_BYTES),
        cost_estimate=cost(0, 18e6),
        name="inward",
    )(grad, master, one, two)


def others_kernel(side, grad_ref, *refs, width, inner):
    masters = refs[:9]
    results = refs[-10:-1]
    product_ref = refs[-1]
    step = pl.program_id(0)
    base = width + inner

    def update(kind, grad):
        master, one, two = masters[3 * kind : 3 * kind + 3]
        values = adam_update(master[...], grad, one[...], two[...], rates[kind + 1], weight_decay)
        for ref, value in zip(results[3 * kind : 3 * kind + 3], values):
            ref[...] = value

    @pl.when(step < 2)
    def _():
        grad = grad_ref[step].astype(F32)
        update(0, grad[:, :width])
        update(1, grad[:, width:base])
        update(2, grad[:, base : base + width])
        product = grad[:, width:base] * masters[3][...].astype(BF).astype(F32)
        total = product[:, :LANES]
        for start in range(LANES, inner, LANES):
            total = total + product[:, start : start + LANES]
        product_ref[...] = total

    @pl.when(step == 2)
    def _():
        update(2, jnp.concatenate([grad_ref[k, :, base + width :].astype(F32) for k in range(2)], axis=1))


def others_call(side, grad, arrays, buffers):
    quarter = grad.shape[1]
    width = arrays[0].shape[1]
    inner = arrays[3].shape[1]
    short = lambda j, s: (2 * jnp.minimum(j, 1) + s[0], 0)
    full = lambda j, s: (2 * j + s[0], 0)
    blocks = []
    for array, place in zip(arrays, (short,) * 6 + (full,) * 3):
        blocks.append(pl.BlockSpec((quarter, array.shape[1]), place))
    sums = jax.ShapeDtypeStruct((arrays[0].shape[0], LANES), F32)
    return pl.pallas_call(
        functools.partial(others_kernel, width=width, inner=inner),
        grid_spec=pltpu.PrefetchScalarGridSpec(
            num_scalar_prefetch=1,
            grid=(3,),
            in_specs=[pl.BlockSpec(grad.shape, lambda j, s: (0, 0, 0))]
            + blocks
            + [pl.BlockSpec(memory_space=pl.ANY)] * len(buffers),
            out_specs=blocks + [pl.BlockSpec((quarter, LANES), short)],
        ),
        out_shape=[jax.ShapeDtypeStruct(array.shape, F32) for array in arrays] + [sums],
        input_output_aliases={11 + k: k for k in range(len(buffers))},
        compiler_params=pltpu.CompilerParams(vmem_limit_bytes=VMEM_BYTES),
        cost_estimate=cost(0, 14e6),
        name="others",
    )(side, grad, *arrays, *buffers)


def tables(seq_total):
    lane = jnp.arange(LANES, dtype=jnp.int32)
    exponent = (lane % (HDIM // 2)).astype(F32) * (2.0 / HDIM)
    inverse = jnp.power(jnp.float32(rope_base), -exponent)
    angles = jnp.arange(seq_total, dtype=F32)[:, None] * inverse[None, :]
    sign = jnp.where(lane % HDIM < HDIM // 2, -1.0, 1.0).astype(F32)
    return jnp.cos(angles), jnp.sin(angles) * sign[None, :]


CORE = [(0, 1), (1, 0), (2, 3), (3, 2)]
CROSS = [(0, 2), (1, 3), (2, 0), (3, 1)]
tie = lax.optimization_barrier


def over_core(array):
    return lax.ppermute(array, "fsdp", CORE)


def over_cross(array):
    return lax.ppermute(array, "fsdp", CROSS)


def over_side(array):
    return lax.ppermute(array, "dp", [(k, k ^ 1) for k in range(lax.axis_size("dp"))])


def along_line(array, groups=None):
    return lax.all_to_all(array, "dp", 0, 0, axis_index_groups=groups)


def add_low(left, right):
    return (left.astype(F32) + right.astype(F32)).astype(BF)


def sum_low(array):
    return jnp.sum(array.astype(F32), axis=0).astype(BF)


def pick_half(array, index, axis=0):
    return lax.dynamic_index_in_dim(array, index, axis, keepdims=False)


def local(
    tokens, cotangent, lengths,
    inward_weight, outward_weight, expand_weight, shrink_weight, gain_weight,
    inward_first, outward_first, expand_first, shrink_first, gain_first,
    inward_second, outward_second, expand_second, shrink_second, gain_second,
):
    micro_count, group_size, local_len, width = tokens.shape
    fsdp = lax.axis_size("fsdp")
    lines = lax.axis_size("dp")
    assert fsdp == 4 and micro_count * group_size == fsdp and lines % 4 == 0
    seq_total = local_len * fsdp
    share, wide = inward_weight.shape
    half = share // 2
    me = lax.axis_index("fsdp").astype(jnp.int32)
    side = (lax.axis_index("dp") % 2).astype(jnp.int32)
    fourth = (lax.axis_index("dp") % 4).astype(jnp.int32)
    info = jnp.stack([me, pick_half(lengths.reshape(fsdp), me), side, fourth])
    columns = [[k for k in range(lines) if k % 2 == odd] for odd in range(2)]

    def to_sequence(array):
        array = array.reshape(fsdp, local_len, width)
        return lax.all_to_all(array, "fsdp", 0, 0).reshape(seq_total, width)

    def around(array):
        return [array] + [lax.ppermute(array, "dp", [(d, d ^ k) for d in range(lines)]) for k in range(1, 4)]

    def with_gains(weight, gains):
        gains = jnp.pad(gains.astype(BF)[:, None, :], ((0, 0), (0, 7), (0, wide - share)))
        return jnp.concatenate([weight.astype(BF), gains], axis=1)

    inward_parts = inward_weight.reshape(4, half // 2, wide)
    gain_parts = jnp.pad(gain_weight, ((0, 2), (0, 0)))
    leaving = with_gains(pick_half(inward_parts, fourth)[None], pick_half(gain_parts, fourth)[None])[0]
    far = over_cross(leaving)

    inward_parts, outward, leaving, tokens = tie((inward_parts, outward_weight, leaving, tokens))
    own = with_gains(inward_parts, gain_parts)
    near = over_core(own)
    x = to_sequence(tokens)
    shrink_low = shrink_weight.astype(BF)
    folded = jnp.concatenate([shrink_low[share:, : width // 2], shrink_low[share:, width // 2 :]], axis=0)
    packed = jnp.concatenate(
        [outward.astype(BF), expand_weight.astype(BF), shrink_low[:share], folded], axis=1
    ).reshape(4, half // 2, -1)
    cosine, sine = tables(seq_total)
    leaving = pick_half(packed, fourth)
    far = around(far)
    far, cosine, sine, info, packed, leaving = tie((far, cosine, sine, info, packed, leaving))
    inward_pieces = (own, near, *far, *[over_core(piece) for piece in far])

    leaving, x = tie((leaving, x))
    other_far = over_cross(leaving)
    other_near = over_core(packed)

    hidden_t, qkv, weight, gain = qkv_call(info, x, cosine, sine, inward_pieces)
    cotangent, other_far, qkv = tie((cotangent, other_far, qkv))
    other_far = around(other_far)
    cot = to_sequence(cotangent)
    mixed, inverse, terms = attend_call(info, qkv, 0, PAIRS, ())
    mixed, other_far = tie((mixed, other_far))
    other_pieces = (packed, other_near, *other_far, *[over_core(piece) for piece in other_far])
    *out, middle_grad, grads, keep, send = feed_call(info, x, mixed, inverse, cot, gain, other_pieces)

    def back(start, count, slot, slots, buffers):
        return back_call(
            info, qkv, mixed, grads, terms, cosine, sine, hidden_t, start, count, slot, slots, buffers
        )

    quarter = half // 2
    level = lines // 2
    line_at = lax.axis_index("dp") // 2

    def over_line(array, gap):
        return lax.ppermute(array, "dp", [(k, k ^ (2 * gap)) for k in range(lines)])

    def halve(array, gap):
        array = array.reshape((array.shape[0] // 2, 2) + array.shape[1:])
        bit = (line_at // gap) % 2
        came = over_line(pick_half(array, 1 - bit, 1), gap)
        return pick_half(array, bit, 1), came

    def in_order(mine, other, gap):
        bit = (line_at // gap) % 2
        pair = jnp.stack([jnp.where(bit == 0, mine, other), jnp.where(bit == 0, other, mine)], axis=1)
        return pair.reshape((-1,) + mine.shape[1:])

    def add(*parts):
        total = parts[0].astype(F32)
        for part in parts[1:]:
            total = total + part.astype(F32)
        return total.astype(BF)

    came = over_core(send)
    keep_x, send_x, joined = back(0, 2, 0, 2, ())
    leave_y = add(keep[0], came[0])
    leave_x = add(keep[1], came[1])
    leave_y, leave_x, joined = tie((leave_y, leave_x, joined))
    first_y = over_cross(leave_y)
    second_x = over_side(leave_x)
    came_x = over_core(send_x)
    keep_v, send_v, joined = back(2, 3, 0, 3, (joined,))
    leave_x = add(keep[2, quarter:], came[2, quarter:], first_y[quarter:])
    leave_y = add(keep[3, quarter:], came[3, quarter:], second_x[quarter:])
    leave_x, leave_y, came_x, out, joined = tie((leave_x, leave_y, came_x, out, joined))
    first_x = over_side(leave_x)
    second_y = over_cross(leave_y)
    came_v = over_core(send_v)
    near_out = over_core(out[1])
    turned_out = over_core(out[3])
    keep_z, send_z, joined = back(5, 1, 0, 1, (joined,))

    came_z = over_core(send_z)
    first = add(keep[2, :quarter], came[2, :quarter], first_y[:quarter], first_x)
    second = add(keep[3, :quarter], came[3, :quarter], second_x[:quarter], second_y)
    both = jnp.concatenate([first, second], axis=0).reshape(level, half // level, -1)
    both, keep_z, near_out, turned_out, came_v = tie((both, keep_z, near_out, turned_out, came_v))
    far_x = over_cross(add(keep_x[1], came_x[1]))
    far_v = over_cross(add(keep_v[1], came_v[1]))
    gap = 1
    stay, moved = halve(both, gap)
    leave_y = add(keep_z[1], came_z[1])
    far_z = over_cross(leave_y)
    while gap * 2 < level:
        stay, moved, leave_y, out = tie((stay, moved, leave_y, out))
        both = add(stay, moved)
        gap = gap * 2
        stay, moved = halve(both, gap)
    stay, leave_y, out, turned_out = tie((stay, leave_y, out, turned_out))
    far_out = over_cross(out[2])
    diagonal_out = over_cross(turned_out)
    moved, far_x, far_v, far_z = tie((moved, far_x, far_v, far_z))
    chunk = jnp.concatenate(
        [add(keep_x[0], came_x[0], far_x), add(keep_v[0], came_v[0], far_v), add(keep_z[0], came_z[0], far_z)], axis=2
    )
    both = add(stay, moved)
    chunk_shape = chunk.shape
    by_line = (lines, 3 * share // lines, chunk_shape[2])
    chunk, both, joined = tie((chunk, both, joined))
    chunk = along_line(chunk.reshape(by_line))
    moved = over_line(both, gap)
    input_low = finish_call(info, joined, weight, x, middle_grad, gain)
    moved, far_out, diagonal_out, input_low = tie((moved, far_out, diagonal_out, input_low))
    both = in_order(both, moved, gap)
    while gap > 2:
        gap = gap // 2
        both = in_order(both, over_line(both, gap), gap)
    both, info_out = tie((both, info))
    block_out = restore_call(info_out, (out[0], near_out, far_out, diagonal_out), BF).reshape(tokens.shape)
    moved = over_line(both, 1)
    far_low = over_cross(input_low[2])
    chunk, far_low, input_low, block_out = tie((chunk, far_low, input_low, block_out))
    chunk = sum_low(chunk)
    near_low = over_core(input_low[1])
    turned_low = over_core(input_low[3])
    chunk, info_in = tie((chunk, info))
    spread = along_line(jnp.broadcast_to(chunk[None], by_line)).reshape(chunk_shape)
    moved, turned_low, near_low = tie((moved, turned_low, near_low))
    both = in_order(both, moved, 1)
    other = over_side(both)
    diagonal_low = over_cross(turned_low)
    pieces = (input_low[0], near_low, far_low, diagonal_low)
    input_grad = restore_call(info_in, pieces, F32).reshape(tokens.shape)

    arrays = (
        outward_weight, outward_first, outward_second,
        expand_weight, expand_first, expand_second,
        shrink_weight, shrink_first, shrink_second,
    )
    own_side = side.reshape(1)
    other_side = (1 - side).reshape(1)
    others_new = others_call(own_side, both.reshape(2, quarter, -1), arrays, ())
    *inward_new, product = inward_call(spread, inward_weight, inward_first, inward_second)
    other, product = tie((other, product))
    *others_new, expand_product = others_call(other_side, other.reshape(2, quarter, -1), arrays, others_new)
    own_gain = gain_weight.astype(BF).astype(F32)
    gain_grad = jnp.stack(
        [
            jnp.sum(product, axis=1),
            jnp.sum(expand_product, axis=1),
        ]
    ) / own_gain

    results = [block_out, input_grad]
    results += inward_new
    results += others_new
    results += adam_update(gain_weight, gain_grad, gain_first, gain_second, rates[4], 0.0)
    return tuple(results)


def solution(mesh):
    split = P(None, "dp", "fsdp", None)
    rows = P("fsdp", None)
    columns = P(None, "fsdp")
    kinds = (rows, rows, rows, rows, columns)
    in_specs = (split, split, P(None, "dp")) + kinds * 3
    out_specs = (split, split) + (rows,) * 12 + (columns,) * 3
    return jax.shard_map(local, mesh=mesh, in_specs=in_specs, out_specs=out_specs, check_vma=False)
```
